32 devices in a mesh: ctx: 4 (over y, core), fsdp: 8 (over z, x).
Axes of the slice: x: 2, y: 2, z: 4, core: 2. Of those that a mesh axis runs over, the one named last changes fastest.
Arguments:
- layer_in: bfloat16 [8, 512, 1600], P('fsdp', 'ctx'), may hold values from -6 to 6
- out_grad: bfloat16 [8, 512, 1600], P('fsdp', 'ctx'), may hold values from -6 to 6
- doc_lengths: int32 [8, 8], P('fsdp'), may hold values from 1 to 256, 512 in all within a row
- block_deal: int32 [4, 2], replicated, may hold values from 0 to 7, as said below
- norm_gains: bfloat16 [4, 1600], P(None, 'fsdp'), may hold values from 0.5 to 1.5
- query_weight: bfloat16 [1600, 1600], P('fsdp'), may hold values from -0.15625 to 0.15625
- keyval_weight: bfloat16 [1600, 640], P('fsdp'), may hold values from -0.15625 to 0.15625
- attn_proj: bfloat16 [1600, 1600], P('fsdp'), may hold values from -0.15625 to 0.15625
- mamba_in: bfloat16 [1600, 6400], P('fsdp'), may hold values from -0.15625 to 0.15625
- conv_taps: bfloat16 [4, 3200], P(None, 'fsdp'), may hold values from -3 to 3
- conv_bias: bfloat16 [3200], P('fsdp'), may hold values from -1.5 to 1.5
- step_bias: bfloat16 [3200], P('fsdp'), may hold values from -5 to -2
- skip_gain: bfloat16 [3200], P('fsdp'), may hold values from 0.5 to 1.5
- decay_log: bfloat16 [16, 3200], P(None, 'fsdp'), may hold values from -7 to 1
- select_proj: bfloat16 [3200, 132], P('fsdp'), may hold values from -0.109375 to 0.109375
- step_proj: bfloat16 [100, 3200], P(None, 'fsdp'), may hold values from -0.625 to 0.625
- mamba_proj: bfloat16 [3200, 1600], P('fsdp'), may hold values from -0.109375 to 0.109375
- gate_weight: bfloat16 [1600, 5504], P('fsdp'), may hold values from -0.15625 to 0.15625
- up_weight: bfloat16 [1600, 5504], P('fsdp'), may hold values from -0.15625 to 0.15625
- down_weight: bfloat16 [5504, 1600], P('fsdp'), may hold values from -0.078125 to 0.078125
Outputs:
- result: bfloat16 [8, 512, 1600], P('fsdp', 'ctx')
- stream_grad: float32 [8, 512, 1600], P('fsdp', 'ctx')
- gains_grad: float32 [4, 1600], P(None, 'fsdp')
- query_grad: float32 [1600, 1600], P('fsdp')
- keyval_grad: float32 [1600, 640], P('fsdp')
- attn_proj_grad: float32 [1600, 1600], P('fsdp')
- mamba_in_grad: float32 [1600, 6400], P('fsdp')
- conv_taps_grad: float32 [4, 3200], P(None, 'fsdp')
- conv_bias_grad: float32 [3200], P('fsdp')
- step_bias_grad: float32 [3200], P('fsdp')
- skip_gain_grad: float32 [3200], P('fsdp')
- decay_log_grad: float32 [16, 3200], P(None, 'fsdp')
- select_proj_grad: float32 [3200, 132], P('fsdp')
- step_proj_grad: float32 [100, 3200], P(None, 'fsdp')
- mamba_proj_grad: float32 [3200, 1600], P('fsdp')
- gate_grad: float32 [1600, 5504], P('fsdp')
- up_grad: float32 [1600, 5504], P('fsdp')
- down_grad: float32 [5504, 1600], P('fsdp')
The draws below stay inside these ranges and needn't reach their ends.
Inputs may be any that keep to these rules, and one draw needn't show every extreme that they name: `block_deal`: row c names a block b and its mirror 8 - 1 - b; every block of 0 to 7 stands in exactly one row. `doc_lengths`: each stream's 8 lengths sum to 512, and the longest has exactly 256 tokens.
All inputs are finite; a program needn't handle non-finite values.
Results may differ from the reference program's by a relative error of at most 0.022.
Values may be sent and summed in bfloat16 or wider, within the bound.
A program may use at most 384 MiB of HBM per device.

```python
import math
import jax
import jax.numpy as jnp
import numpy as np
from jax import lax

D = 1600
H = 25
KV = 5
HD = 64
INNER = 3200
NS = 16
RANK = 100
FF = 5504
CONV = 4
DOCS = 8
TOK_DEV = 128
STREAMS = 8
SEQ = 512
DOC_MOST = 256
N_CTX = 4


def draw_block_deal(key, part):
    chosen = jax.random.permutation(key, N_CTX).astype(jnp.int32)
    return jnp.stack([chosen, 2 * N_CTX - 1 - chosen], axis=1).astype(jnp.int32)


def level_of(own_key, extent, cuts, low, high):
    def one(position, blocks):
        draws = jax.random.uniform(jax.random.fold_in(jax.random.fold_in(own_key, 6), position), (blocks,), jnp.float32, low / len(cuts), high / len(cuts))
        return jnp.repeat(jnp.exp(draws), extent[position] // blocks).reshape((-1,) + (1,) * (len(extent) - position - 1))

    level = one(*cuts[0])
    for cut in cuts[1:]:
        level = level * one(*cut)
    return level


def split_up(number_of, total, reach, lean):
    loads = [(1 << 20) // math.isqrt(standing ** lean) + 1 for standing in range(2, number_of + 1)]
    spare, holding = total - reach - (number_of - 1), [1] * (number_of - 1)
    while spare > 0:
        free = [i for i in range(number_of - 1) if holding[i] < reach]
        mass, budget = sum([loads[i] for i in free]), spare
        for i in free:
            more = min(reach - holding[i], max(1, budget * loads[i] // mass), spare)
            holding[i] = holding[i] + more
            spare = spare - more
    return np.array([reach] + holding)


def uneven_parts(rng, count, total, bound, slope):
    if count == 2:
        one = jax.random.randint(rng, (), max(1, total - bound), min(bound, total - 1) + 1)
        return jnp.stack([one, total - one])
    sizes = jnp.asarray(split_up(count, total, bound, slope), jnp.int32)
    twos = (count - 1) // 2
    donor, taker = sizes[1:1 + 2 * twos:2], sizes[2:2 + 2 * twos:2]
    slack = jnp.minimum(donor - 1, bound - taker)
    passed = jax.random.randint(jax.random.fold_in(rng, 1), (twos,), 0, 1 << 20) % (slack + 1)
    sizes = sizes.at[1:1 + 2 * twos:2].set(donor - passed).at[2:2 + 2 * twos:2].set(taker + passed)
    return sizes[jax.random.permutation(jax.random.fold_in(rng, 2), count)]


def gaussian(key, extent, deviation, most, pieces=(), held_as=jnp.bfloat16):
    array = jax.random.normal(key, extent, jnp.float32) * deviation
    if len(pieces) > 0:
        array = level_of(key, extent, pieces, -0.22, 0.18) * array
    return jnp.clip(array, min=-most, max=most).astype(held_as)


def setup_inputs(seed: int = 0) -> dict:
    seeds = jax.random.split(jax.random.key(seed), 21)
    layer_in = gaussian(seeds[0], (STREAMS, SEQ, D), 1.0, 6.0, ((0, 8), (1, 4)))
    out_grad = gaussian(seeds[1], (STREAMS, SEQ, D), 1.0, 6.0, ((0, 8), (1, 4)))
    doc_lengths = jax.vmap(lambda own: uneven_parts(own, DOCS, SEQ, DOC_MOST, 2))(jax.random.split(seeds[2], STREAMS)).reshape((STREAMS, DOCS)).astype(jnp.int32)
    block_deal = draw_block_deal(jax.random.fold_in(seeds[20], 71), 0)
    norm_gains = jnp.clip(1.0 + 0.1 * jax.random.normal(seeds[4], (4, D), jnp.float32), 0.5, 1.5).astype(jnp.bfloat16)
    query_weight = gaussian(seeds[5], (D, H * HD), D ** -0.5, 0.15625, ((0, 8),))
    keyval_weight = gaussian(seeds[6], (D, 2 * KV * HD), D ** -0.5, 0.15625, ((0, 8),))
    attn_proj = gaussian(seeds[7], (H * HD, D), (H * HD) ** -0.5, 0.15625, ((0, 8),))
    mamba_in = gaussian(seeds[8], (D, 2 * INNER), D ** -0.5, 0.15625, ((0, 8),))
    conv_taps = gaussian(seeds[9], (CONV, INNER), CONV ** -0.5, 3.0, ((1, 8),))
    conv_bias = gaussian(seeds[10], (INNER,), 0.3, 1.5, ((0, 8),))
    step_bias = jnp.clip(-5.0 + 3.0 * jax.random.uniform(seeds[11], (INNER,), jnp.float32) ** level_of(seeds[11], (INNER,), ((0, 8),), -0.2, 0.2), -5.0, -2.0).astype(jnp.bfloat16)
    skip_gain = jnp.clip(0.5 + 1.0 * jax.random.uniform(seeds[12], (INNER,), jnp.float32) ** level_of(seeds[12], (INNER,), ((0, 8),), -0.2, 0.2), 0.5, 1.5).astype(jnp.bfloat16)
    decay_log = jnp.clip(-7.0 + 8.0 * jax.random.uniform(seeds[13], (NS, INNER), jnp.float32) ** level_of(seeds[13], (NS, INNER), ((1, 8),), -0.2, 0.2), -7.0, 1.0).astype(jnp.bfloat16)
    select_proj = gaussian(seeds[14], (INNER, RANK + 2 * NS), INNER ** -0.5, 0.109375, ((0, 8),))
    step_proj = gaussian(seeds[15], (RANK, INNER), RANK ** -0.5, 0.625, ((1, 8),))
    mamba_proj = gaussian(seeds[16], (INNER, D), INNER ** -0.5, 0.109375, ((0, 8),))
    gate_weight = gaussian(seeds[17], (D, FF), D ** -0.5, 0.15625, ((0, 8),))
    up_weight = gaussian(seeds[18], (D, FF), D ** -0.5, 0.15625, ((0, 8),))
    down_weight = gaussian(seeds[19], (FF, D), FF ** -0.5, 0.078125, ((0, 8),))
    return dict(layer_in=layer_in, out_grad=out_grad, doc_lengths=doc_lengths, block_deal=block_deal, norm_gains=norm_gains, query_weight=query_weight, keyval_weight=keyval_weight, attn_proj=attn_proj, mamba_in=mamba_in, conv_taps=conv_taps, conv_bias=conv_bias, step_bias=step_bias, skip_gain=skip_gain, decay_log=decay_log, select_proj=select_proj, step_proj=step_proj, mamba_proj=mamba_proj, gate_weight=gate_weight, up_weight=up_weight, down_weight=down_weight)


EPS = 1e-06
score_scale = 0.125

@jax.custom_vjp
def low(v):
    return lax.optimization_barrier(v.astype(jnp.bfloat16)).astype(jnp.float32)

@jax.custom_vjp
def low_back(v):
    return v

def low_keep(v):
    return (low(v), None)

def low_pass(kept, grad):
    return (grad,)

def back_keep(v):
    return (v, None)

def back_low(kept, grad):
    return (low(grad),)
low.defvjp(low_keep, low_pass)
low_back.defvjp(back_keep, back_low)

def rms_norm(values, gain):
    return values * lax.rsqrt(lax.optimization_barrier(jnp.mean(values * values, axis=-1, keepdims=True)) + EPS) * gain

def matmul(left, right):
    return jnp.dot(left, right, precision=lax.Precision.HIGHEST, preferred_element_type=jnp.float32)

def attention(queries, keyvals, allowed):
    length = queries.shape[0]
    group = H // KV
    query_groups = queries.reshape(length, KV, group, HD).transpose(1, 0, 2, 3)
    key_groups = keyvals[:, :KV * HD].reshape(length, KV, HD).transpose(1, 0, 2)
    value_groups = keyvals[:, KV * HD:].reshape(length, KV, HD).transpose(1, 0, 2)

    def one_group(parts):
        query_part, key_part, value_part = parts
        scores = jnp.einsum('lgd,sd->gls', query_part, key_part, precision=lax.Precision.HIGHEST) * score_scale
        scores = low_back(jnp.where(allowed[None], scores, -1e+30))
        largest = lax.optimization_barrier(jnp.max(scores, axis=-1, keepdims=True))
        expo = jnp.exp(scores - largest)
        probs = low(expo / lax.optimization_barrier(jnp.sum(expo, axis=-1, keepdims=True)))
        return jnp.einsum('gls,sd->lgd', probs, value_part, precision=lax.Precision.HIGHEST)
    outputs = lax.map(jax.checkpoint(one_group), (query_groups, key_groups, value_groups))
    return outputs.transpose(1, 0, 2, 3).reshape(length, H * HD)

def mamba(normed_low, mamba_in, conv_taps, conv_bias, step_bias, skip_gain, decay_log, select_proj, step_proj):
    length = normed_low.shape[0]
    entry = matmul(normed_low, mamba_in)
    mixer_in = low_back(low(entry[:, :INNER]))
    gate_side = low_back(entry[:, INNER:])
    padded = jnp.concatenate([jnp.zeros((CONV - 1, INNER), jnp.float32), mixer_in], axis=0)
    conv_out = conv_bias + sum((conv_taps[offset] * padded[offset:offset + length] for offset in range(CONV)))
    signal = low(jax.nn.silu(conv_out))
    selected = low_back(matmul(signal, select_proj))
    step_low = low(selected[:, :RANK])
    writes = selected[:, RANK:RANK + NS]
    reads = selected[:, RANK + NS:]
    step_pre = low_back(matmul(step_low, step_proj) + step_bias)
    step_sizes = jax.nn.softplus(step_pre)
    rate = -jnp.exp(decay_log)

    def advance(state, items):
        step_t, signal_t, write_t, read_t = items
        state = jnp.exp(step_t[None, :] * rate) * state + write_t[:, None] * (step_t * signal_t)[None, :]
        return (state, lax.optimization_barrier(jnp.sum(state * read_t[:, None], axis=0)))
    _, outputs = lax.scan(jax.checkpoint(advance), jnp.zeros((NS, INNER), jnp.float32), (step_sizes, signal, writes, reads))
    scanned = outputs + skip_gain * signal
    return low(scanned * jax.nn.silu(gate_side))

def layer(stream, allowed, params):
    norm_gains, query_weight, keyval_weight, attn_proj, mamba_in, conv_taps, conv_bias, step_bias, skip_gain, decay_log, select_proj, step_proj, mamba_proj, gate_weight, up_weight, down_weight = params
    normed_low = low(rms_norm(stream, norm_gains[0]))
    queries = low_back(low(matmul(normed_low, query_weight)))
    keyvals = low_back(low(matmul(normed_low, keyval_weight)))
    attn_rows = low_back(low(attention(queries, keyvals, allowed)))
    attn_out = low_back(matmul(attn_rows, attn_proj))
    mamba_rows = mamba(normed_low, mamba_in, conv_taps, conv_bias, step_bias, skip_gain, decay_log, select_proj, step_proj)
    mamba_out = low_back(matmul(mamba_rows, mamba_proj))
    middle = stream + 0.5 * (rms_norm(attn_out, norm_gains[1]) + rms_norm(mamba_out, norm_gains[2]))
    ffn_low = low(rms_norm(middle, norm_gains[3]))
    gate_pre = low_back(matmul(ffn_low, gate_weight))
    up_pre = low_back(matmul(ffn_low, up_weight))
    hidden = low(jax.nn.silu(gate_pre) * up_pre)
    return middle + matmul(hidden, down_weight)

def reference(layer_in, out_grad, doc_lengths, block_deal, norm_gains, query_weight, keyval_weight, attn_proj, mamba_in, conv_taps, conv_bias, step_bias, skip_gain, decay_log, select_proj, step_proj, mamba_proj, gate_weight, up_weight, down_weight):
    params = tuple((item.astype(jnp.float32) for item in (norm_gains, query_weight, keyval_weight, attn_proj, mamba_in, conv_taps, conv_bias, step_bias, skip_gain, decay_log, select_proj, step_proj, mamba_proj, gate_weight, up_weight, down_weight)))
    half_rows = TOK_DEV // 2
    offsets = jnp.arange(half_rows, dtype=jnp.int32)
    stored_place = (block_deal.reshape(-1).astype(jnp.int32)[:, None] * half_rows + offsets[None, :]).reshape(-1).astype(jnp.int32)
    true_order = jnp.argsort(stored_place).astype(jnp.int32)
    places = jnp.arange(SEQ, dtype=jnp.int32)

    def one_stream(totals, inputs):
        rows_in, rows_grad, lengths = inputs
        lengths = lengths.astype(jnp.int32)
        starts = (jnp.cumsum(lengths) - lengths).astype(jnp.int32)
        segment = (lax.optimization_barrier(jnp.sum((places[:, None] >= starts[None, :]).astype(jnp.int32), axis=1)) - 1).astype(jnp.int32)
        allowed = (places[None, :] <= places[:, None]) & (segment[None, :] == segment[:, None])
        stream = rows_in.astype(jnp.float32)[true_order]
        output, pull_back = jax.vjp(lambda value, *weights: layer(value, allowed, weights), stream, *params)
        grads = pull_back(rows_grad.astype(jnp.float32)[true_order])
        totals = tuple((total + grad for total, grad in zip(totals, grads[1:])))
        return (totals, (output[stored_place].astype(jnp.bfloat16), grads[0][stored_place]))
    zero_totals = tuple((jnp.zeros(item.shape, jnp.float32) for item in params))
    totals, (results, stream_grads) = lax.scan(one_stream, zero_totals, (layer_in, out_grad, doc_lengths))
    return (results, stream_grads, totals[0], totals[1], totals[2], totals[3], totals[4], totals[5], totals[6], totals[7], totals[8], totals[9], totals[10], totals[11], totals[12], totals[13], totals[14], totals[15])
```

```python
import functools
import math

import jax
import jax.numpy as jnp
from jax import lax
from jax.experimental import pallas as pl
from jax.experimental.pallas import tpu as pltpu
from jax.sharding import PartitionSpec as P

H = 25
KV = 5
HD = 64
INNER = 3200
NS = 16
RANK = 100
CONV = 4

EPS = 1e-06
score_scale = 0.125
MESH = pl.DeviceIdType.MESH
ANY = pl.BlockSpec(memory_space=pl.ANY)
VM = pl.BlockSpec(memory_space=pltpu.VMEM)
DMA = pltpu.SemaphoreType.DMA
f32 = jnp.float32
bf16 = jnp.bfloat16


def params(cid, vmem=None):
    return pltpu.CompilerParams(collective_id=cid, has_side_effects=True, vmem_limit_bytes=vmem)


def rcopy(src, dst, ssem, rsem, dev):
    return pltpu.make_async_remote_copy(
        src_ref=src, dst_ref=dst, send_sem=ssem, recv_sem=rsem, device_id=dev, device_id_type=MESH
    )


def greet_line(a, b, lanes):
    bar = pltpu.get_barrier_semaphore()

    @pl.when(a > 0)
    def _():
        pl.semaphore_signal(bar, inc=1, device_id={"fsdp": 2 * (a - 1) + b}, device_id_type=MESH)

    @pl.when(a < lanes - 1)
    def _():
        pl.semaphore_signal(bar, inc=1, device_id={"fsdp": 2 * (a + 1) + b}, device_id_type=MESH)

    pl.semaphore_signal(bar, inc=1, device_id={"fsdp": 2 * a + 1 - b}, device_id_type=MESH)
    peers = 1 + (a > 0).astype(jnp.int32) + (a < lanes - 1).astype(jnp.int32)
    pl.semaphore_wait(bar, peers)


def greet_all(axis, size):
    me = lax.axis_index(axis)
    bar = pltpu.get_barrier_semaphore()
    for d in range(1, size):
        pl.semaphore_signal(
            bar, inc=1, device_id={axis: lax.rem(me + d, size)}, device_id_type=MESH
        )
    pl.semaphore_wait(bar, size - 1)


def gather_rows(x, size, cid):
    rows, cols = x.shape
    lanes = size // 2
    steps = lanes - 1

    def kernel(x_ref, o_ref, lsem, up_s, up_r, dn_s, dn_r, px_s, px_r):
        f = lax.axis_index("fsdp")
        a, b = f // 2, lax.rem(f, 2)
        greet_line(a, b, lanes)
        mine = o_ref.at[pl.ds(pl.multiple_of(f * rows, rows), rows)]
        local = pltpu.make_async_copy(x_ref, mine, lsem)
        local.start()

        def piece(origin):
            at = pl.multiple_of((2 * origin + b) * rows, rows)
            return o_ref.at[pl.ds(at, rows)]

        def up(s):
            src = x_ref if s == 0 else piece(a - s)
            return rcopy(src, piece(a - s), up_s.at[s], up_r.at[s], {"fsdp": 2 * (a + 1) + b})

        def down(s):
            src = x_ref if s == 0 else piece(a + s)
            return rcopy(src, piece(a + s), dn_s.at[s], dn_r.at[s], {"fsdp": 2 * (a - 1) + b})

        def across(origin, own=False):
            src = x_ref if own else piece(origin)
            return rcopy(
                src, piece(origin), px_s.at[origin], px_r.at[origin], {"fsdp": 2 * a + 1 - b}
            )

        def partner(origin):
            at = pl.multiple_of((2 * origin + 1 - b) * rows, rows)
            ref = o_ref.at[pl.ds(at, rows)]
            return rcopy(ref, ref, px_s.at[origin], px_r.at[origin], {"fsdp": 2 * a + 1 - b})

        @pl.when(a < lanes - 1)
        def _():
            up(0).start()

        @pl.when(a > 0)
        def _():
            down(0).start()

        across(a, True).start()
        for s in range(steps):
            @pl.when(a - 1 - s >= 0)
            def _():
                o = piece(a - 1 - s)
                rcopy(o, o, up_s.at[s], up_r.at[s], {"fsdp": 2 * (a - 1) + b}).wait_recv()

                @pl.when(a < lanes - 1)
                def _():
                    up(s + 1).start()

                across(a - 1 - s).start()

            @pl.when(a + 1 + s <= lanes - 1)
            def _():
                o = piece(a + 1 + s)
                rcopy(o, o, dn_s.at[s], dn_r.at[s], {"fsdp": 2 * (a + 1) + b}).wait_recv()

                @pl.when(a > 0)
                def _():
                    down(s + 1).start()

                across(a + 1 + s).start()

        local.wait()
        for s in range(steps):
            @pl.when((a - s >= 0) & (a < lanes - 1))
            def _():
                up(s).wait_send()

            @pl.when((a + s <= lanes - 1) & (a > 0))
            def _():
                down(s).wait_send()

        for origin in range(lanes):
            across(origin).wait_send()
            partner(origin).wait_recv()

    return pl.pallas_call(
        kernel,
        out_shape=jax.ShapeDtypeStruct((size * rows, cols), x.dtype),
        in_specs=[ANY],
        out_specs=ANY,
        scratch_shapes=[DMA]
        + [DMA((lanes,))] * 6,
        compiler_params=params(cid),
        name="gather_rows",
    )(x)


def scatter_rows(p, size, cid):
    rows, cols = p.shape[0] // size, p.shape[1]
    lanes = size // 2
    part = 32 if rows % 32 == 0 else rows

    def kernel(p_ref, o_ref, xbuf, upb, dnb, up_s, up_r, dn_s, dn_r, px_s, px_r):
        f = lax.axis_index("fsdp")
        a, b = f // 2, lax.rem(f, 2)
        greet_line(a, b, lanes)

        def across(dest):
            src = p_ref.at[pl.ds(pl.multiple_of((2 * dest + 1 - b) * rows, rows), rows)]
            return rcopy(
                src, xbuf.at[dest], px_s.at[dest], px_r.at[dest], {"fsdp": 2 * a + 1 - b}
            )

        def up(dest):
            return rcopy(
                xbuf.at[dest], upb.at[dest], up_s.at[dest], up_r.at[dest], {"fsdp": 2 * (a + 1) + b}
            )

        def down(dest):
            return rcopy(
                xbuf.at[dest], dnb.at[dest], dn_s.at[dest], dn_r.at[dest], {"fsdp": 2 * (a - 1) + b}
            )

        def add_in(dest, extra):
            base = pl.multiple_of((2 * dest + b) * rows, rows)

            def body(i, carry):
                at = pl.multiple_of(i * part, part)
                total = xbuf[dest, pl.ds(at, part), :].astype(f32)
                total += p_ref[pl.ds(base + at, part), :].astype(f32)
                if extra is not None:
                    total += extra[dest, pl.ds(at, part), :].astype(f32)
                xbuf[dest, pl.ds(at, part), :] = total.astype(bf16)
                return carry

            lax.fori_loop(0, rows // part, body, 0)

        for d in range(lanes - 1, -1, -1):
            @pl.when(a + d <= lanes - 1)
            def _():
                across(a + d).start()

            if d > 0:
                @pl.when(a - d >= 0)
                def _():
                    across(a - d).start()

        for d in range(lanes - 1, 0, -1):
            @pl.when(a + d <= lanes - 1)
            def _():
                across(a + d).wait_recv()

                @pl.when(a > 0)
                def _():
                    up(a + d).wait_recv()
                    add_in(a + d, upb)

                @pl.when(a == 0)
                def _():
                    add_in(a + d, None)

                up(a + d).start()

            @pl.when(a - d >= 0)
            def _():
                across(a - d).wait_recv()

                @pl.when(a < lanes - 1)
                def _():
                    down(a - d).wait_recv()
                    add_in(a - d, dnb)

                @pl.when(a == lanes - 1)
                def _():
                    add_in(a - d, None)

                down(a - d).start()

        across(a).wait_recv()

        @pl.when(a > 0)
        def _():
            up(a).wait_recv()

        @pl.when(a < lanes - 1)
        def _():
            down(a).wait_recv()

        base = pl.multiple_of((2 * a + b) * rows, rows)
        below, above = (a > 0).astype(f32), (a < lanes - 1).astype(f32)

        def last(i, carry):
            at = pl.multiple_of(i * part, part)
            total = xbuf[a, pl.ds(at, part), :].astype(f32)
            total += p_ref[pl.ds(base + at, part), :].astype(f32)
            o_ref[pl.ds(at, part), :] = total
            return carry

        lax.fori_loop(0, rows // part, last, 0)

        def more(buf):
            def body(i, carry):
                at = pl.multiple_of(i * part, part)
                o_ref[pl.ds(at, part), :] += buf[a, pl.ds(at, part), :].astype(f32)
                return carry

            lax.fori_loop(0, rows // part, body, 0)

        @pl.when(a > 0)
        def _():
            more(upb)

        @pl.when(a < lanes - 1)
        def _():
            more(dnb)

        for dest in range(lanes):
            across(dest).wait_send()

        for d in range(lanes - 1, 0, -1):
            @pl.when(a + d <= lanes - 1)
            def _():
                up(a + d).wait_send()

            @pl.when(a - d >= 0)
            def _():
                down(a - d).wait_send()

    return pl.pallas_call(
        kernel,
        out_shape=jax.ShapeDtypeStruct((rows, cols), f32),
        in_specs=[VM],
        out_specs=VM,
        scratch_shapes=[pltpu.VMEM((lanes, rows, cols), bf16)] * 3 + [DMA((lanes,))] * 6,
        compiler_params=params(cid, 60 << 20),
        name="scatter_rows",
    )(p)


def exchange(x, size, cid, axis="fsdp"):
    def kernel(x_ref, o_ref, lsem, ssem, rsem):
        me = lax.axis_index(axis)
        greet_all(axis, size)
        local = pltpu.make_async_copy(x_ref.at[me], o_ref.at[me], lsem)
        local.start()
        copies = []
        for d in range(1, size):
            to = lax.rem(me + d, size)
            copies.append(
                rcopy(x_ref.at[to], o_ref.at[me], ssem.at[d], rsem.at[d], {axis: to})
            )
            copies[-1].start()
        local.wait()
        for copy in copies:
            copy.wait()

    return pl.pallas_call(
        kernel,
        out_shape=jax.ShapeDtypeStruct(x.shape, x.dtype),
        in_specs=[ANY],
        out_specs=ANY,
        scratch_shapes=[DMA, DMA((size,)), DMA((size,))],
        compiler_params=params(cid),
        name="exchange",
    )(x)


def sum_rows(p, size, cid):
    rows, cols = p.shape[0] // size, p.shape[1]

    def kernel(p_ref, o_ref, buf, ssem, rsem, gs, gr):
        me = lax.axis_index("fsdp")
        greet_all("fsdp", size)

        def at(i):
            return pl.ds(pl.multiple_of(i * rows, rows), rows)

        first = []
        for d in range(1, size):
            to = lax.rem(me + d, size)
            first.append(
                rcopy(p_ref.at[at(to)], buf.at[d], ssem.at[d], rsem.at[d], {"fsdp": to})
            )
            first[-1].start()
        total = p_ref[at(me), :].astype(f32)
        for d in range(1, size):
            first[d - 1].wait_recv()
            total += buf[d].astype(f32)
        o_ref[at(me), :] = total.astype(bf16)
        second = []
        for d in range(1, size):
            to = lax.rem(me + d, size)
            second.append(
                rcopy(o_ref.at[at(me)], o_ref.at[at(me)], gs.at[d], gr.at[d], {"fsdp": to})
            )
            second[-1].start()
        for d in range(1, size):
            first[d - 1].wait_send()
            second[d - 1].wait()

    return pl.pallas_call(
        kernel,
        out_shape=jax.ShapeDtypeStruct(p.shape, bf16),
        in_specs=[VM],
        out_specs=VM,
        scratch_shapes=[pltpu.VMEM((size, rows, cols), bf16)] + [DMA((size,))] * 4,
        compiler_params=params(cid, 32 << 20),
        name="sum_rows",
    )(p)


def gather_ctx(x, size, cid):
    half = size // 2

    def kernel(x_ref, o_ref, lsem, ssem, rsem):
        c = lax.axis_index("ctx")
        greet_all("ctx", size)
        local = pltpu.make_async_copy(x_ref, o_ref.at[c], lsem)
        local.start()
        copies = []
        for d in range(1, size):
            copies.append(
                rcopy(x_ref, o_ref.at[c], ssem.at[d], rsem.at[d], {"ctx": lax.rem(c + d, size)})
            )
            copies[-1].start()
        local.wait()
        for copy in copies:
            copy.wait()

    return pl.pallas_call(
        kernel,
        out_shape=jax.ShapeDtypeStruct((size,) + x.shape, x.dtype),
        in_specs=[ANY],
        out_specs=ANY,
        scratch_shapes=[DMA, DMA((size,)), DMA((size,))],
        compiler_params=params(cid),
        name="gather_ctx",
    )(x)

def norm_forward(values, gain):
    inverse = lax.rsqrt(jnp.mean(values * values, axis=-1, keepdims=True) + EPS)
    return (values * inverse * gain, inverse)


def norm_backward(grad, values, inverse, gain):
    normed = values * inverse
    gain_grad = jnp.sum(grad * normed, axis=0)
    scaled = grad * gain
    return (
        inverse * (scaled - normed * jnp.mean(scaled * normed, axis=-1, keepdims=True)),
        gain_grad,
    )


def silu_slope(values):
    sigma = jax.nn.sigmoid(values)
    return sigma * (1.0 + values * (1.0 - sigma))


def block_scan(start, rate, steps, inputs, writes, reads):
    batch_count, length, channels = steps.shape
    piece_len = math.gcd(length, 8)
    pieces = length // piece_len

    def split(values):
        return values.reshape(batch_count, pieces, piece_len, values.shape[-1]).transpose(
            1, 0, 2, 3
        )

    def one_piece(carried, columns):
        step_c, input_c, write_c, read_c = columns
        climbing = jnp.cumsum(step_c[:, :, None, :] * rate, axis=1)
        pushed = write_c[:, :, :, None] * (step_c * input_c)[:, :, None, :]
        inner = jnp.exp(climbing) * (
            carried[:, None] + jnp.cumsum(jnp.exp(-climbing) * pushed, axis=1)
        )
        return (inner[:, -1], jnp.sum(inner * read_c[:, :, :, None], axis=2))

    final, outputs = lax.scan(
        jax.checkpoint(one_piece), start, (split(steps), split(inputs), split(writes), split(reads))
    )
    return (outputs.transpose(1, 0, 2, 3).reshape(batch_count, length, channels), final)


def on_device(
    layer_in,
    out_grad,
    doc_lengths,
    block_deal,
    norm_gains,
    query_weight,
    keyval_weight,
    attn_proj,
    mamba_in,
    conv_taps,
    conv_bias,
    step_bias,
    skip_gain,
    decay_log,
    select_proj,
    step_proj,
    mamba_proj,
    gate_weight,
    up_weight,
    down_weight,
):
    size = lax.axis_size("fsdp")
    n_ctx = lax.axis_size("ctx")
    rows = layer_in.shape[1]
    half_rows = rows // 2
    width = layer_in.shape[2]
    blocks_all = 2 * n_ctx
    group = H // KV
    chan = INNER // size
    q_cols, kv_cols = H * HD // size, 2 * KV * HD // size
    ff_cols = gate_weight.shape[1] // size
    rows_all = size * rows
    ctx_place = lax.axis_index("ctx")
    deal_flat = block_deal.reshape(-1)
    my_blocks = lax.dynamic_slice_in_dim(block_deal, ctx_place, 1, 0)[0]
    offsets = jnp.arange(half_rows, dtype=jnp.int32)
    my_places = (my_blocks[:, None] * half_rows + offsets[None, :]).reshape(-1)
    key_places = (deal_flat[:, None] * half_rows + offsets[None, :]).reshape(-1)
    lengths = doc_lengths[0]
    starts = jnp.cumsum(lengths) - lengths

    def segment(places):
        return jnp.sum((places[:, None] >= starts[None, :]).astype(jnp.int32), axis=1)

    allowed = (key_places[None, :] <= my_places[:, None]) & (
        segment(key_places)[None, :] == segment(my_places)[:, None]
    )
    inverse = jnp.argsort(deal_flat)

    def to_columns(weight, cols):
        return lax.all_to_all(weight, "fsdp", split_axis=1, concat_axis=0, tiled=True)

    gain_float = lax.all_gather(norm_gains, "fsdp", axis=1, tiled=True).astype(f32)
    depth = query_weight.shape[0]
    first_cols = jnp.concatenate(
        [
            query_weight.reshape(depth, size, q_cols),
            keyval_weight.reshape(depth, size, kv_cols),
            mamba_in[:, :INNER].reshape(depth, size, chan),
            mamba_in[:, INNER:].reshape(depth, size, chan),
        ],
        axis=2,
    ).transpose(1, 0, 2)
    first_mat = lax.all_to_all(first_cols, "fsdp", 0, 0, tiled=True).reshape(width, -1)
    ffn_cols = jnp.concatenate(
        [
            gate_weight.reshape(depth, size, ff_cols),
            up_weight.reshape(depth, size, ff_cols),
        ],
        axis=2,
    ).transpose(1, 0, 2)
    ffn_mat = lax.all_to_all(ffn_cols, "fsdp", 0, 0, tiled=True).reshape(width, -1)
    attn_mat = lax.all_gather(attn_proj, "fsdp", axis=0, tiled=True)
    qkv_mat = first_mat[:, : q_cols + kv_cols]
    entry_mat = first_mat[:, q_cols + kv_cols :]
    gate_mat, up_mat = ffn_mat[:, :ff_cols], ffn_mat[:, ff_cols:]

    stream_all = gather_rows(layer_in[0], size, 0)
    stream = layer_in[0].astype(f32)
    _, inv_in = norm_forward(stream, gain_float[0])
    normed_all, _ = norm_forward(stream_all.astype(f32), gain_float[0])
    normed_all = normed_all.astype(bf16)
    grads_all = gather_rows(out_grad[0], size, 1)

    qkv = jnp.dot(normed_all, qkv_mat, preferred_element_type=f32).astype(bf16)
    qkv = exchange(qkv.reshape(size, rows, -1), size, 2)
    queries = qkv[:, :, :q_cols].transpose(1, 0, 2).reshape(rows, H * HD)
    keyvals = qkv[:, :, q_cols:].transpose(1, 0, 2).reshape(rows, 2 * KV * HD)
    keyvals_all = gather_ctx(keyvals, n_ctx, 3).reshape(n_ctx * rows, 2 * KV * HD)
    query_groups = queries.reshape(rows, KV, group, HD).transpose(1, 0, 2, 3)
    key_groups = keyvals_all[:, : KV * HD].reshape(-1, KV, HD).transpose(1, 0, 2)
    value_groups = keyvals_all[:, KV * HD :].reshape(-1, KV, HD).transpose(1, 0, 2)

    def attend(parts):
        query_part, key_part, value_part = parts
        scores = (
            jnp.einsum("lgd,sd->gls", query_part, key_part, preferred_element_type=f32)
            * score_scale
        )
        scores = jnp.where(allowed[None], scores, -1e30)
        largest = jnp.max(scores, axis=-1, keepdims=True)
        expo = jnp.exp(scores - largest)
        total = jnp.sum(expo, axis=-1, keepdims=True)
        probs = (expo / total).astype(bf16)
        output = jnp.einsum("gls,sd->lgd", probs, value_part, preferred_element_type=f32)
        return (output, largest + jnp.log(total))

    attn_groups, log_totals = lax.map(attend, (query_groups, key_groups, value_groups))
    attn_rows = attn_groups.transpose(1, 0, 2, 3).reshape(rows, H * HD).astype(bf16)
    attn_out = jnp.dot(attn_rows, attn_mat, preferred_element_type=f32)
    attn_normed, inv_attn = norm_forward(attn_out, gain_float[1])

    entry = jnp.dot(normed_all, entry_mat, preferred_element_type=f32)
    mixer_in = entry[:, :chan].astype(bf16)
    gate_side = entry[:, chan:]
    mixer_blocks = mixer_in.reshape(size, 2, half_rows, chan)
    tails = mixer_blocks[:, :, half_rows - (CONV - 1) :]
    tails_all = gather_ctx(tails.reshape(-1, chan), n_ctx, 4)
    tails_all = tails_all.reshape(n_ctx, size, 2, CONV - 1, chan)

    def in_deal_order(values):
        return jnp.moveaxis(values, 2, 1).reshape((blocks_all,) + (size,) + values.shape[3:])

    def of_blocks(values, index):
        return jnp.moveaxis(jnp.take(values, index, axis=0), 0, 1)

    before_index = inverse[jnp.maximum(my_blocks - 1, 0)]
    has_before = my_blocks > 0
    prior_tail = jnp.where(
        has_before[None, :, None, None],
        of_blocks(in_deal_order(tails_all), before_index),
        jnp.zeros_like(tails),
    )
    padded = jnp.concatenate([prior_tail, mixer_blocks], axis=2).astype(f32)
    taps_float = conv_taps.astype(f32)
    conv_blocks_out = conv_bias.astype(f32) + sum(
        taps_float[offset] * padded[:, :, offset : offset + half_rows] for offset in range(CONV)
    )
    conv_out = conv_blocks_out.reshape(rows_all, chan)
    signal = jax.nn.silu(conv_out).astype(bf16)
    signal_float = signal.astype(f32)
    selected_part = jnp.dot(signal, select_proj, preferred_element_type=f32)
    selected = sum_rows(selected_part.astype(bf16), size, 5)
    step_low = selected[:, :RANK]
    writes = selected[:, RANK : RANK + NS].astype(f32)
    reads = selected[:, RANK + NS :].astype(f32)
    step_pre = jnp.dot(step_low, step_proj, preferred_element_type=f32) + step_bias.astype(f32)
    step_sizes = jax.nn.softplus(step_pre)
    rate = -jnp.exp(decay_log.astype(f32))
    pair = size * 2
    block_steps = step_sizes.reshape(pair, half_rows, chan)
    block_inputs = signal_float.reshape(pair, half_rows, chan)
    block_writes = writes.reshape(pair, half_rows, NS)
    block_reads = reads.reshape(pair, half_rows, NS)
    zero_state = jnp.zeros((pair, NS, chan), f32)
    _, local_end = block_scan(
        zero_state, rate, block_steps, block_inputs, block_writes, block_reads
    )
    step_totals = jnp.sum(block_steps, axis=1)
    ends_all = gather_ctx(
        jnp.concatenate([local_end, step_totals[:, None, :]], axis=1)
        .astype(bf16)
        .reshape(-1, chan),
        n_ctx,
        6,
    )
    ends_all = in_deal_order(ends_all.reshape(n_ctx, size, 2, NS + 1, chan)).astype(f32)
    ends_true = jnp.take(ends_all, inverse, axis=0)
    decays_true = jnp.exp(rate * ends_true[:, :, NS:])
    ends_true = ends_true[:, :, :NS]

    def link(carried, both):
        decay_part, end_part = both
        return (decay_part * carried + end_part, carried)

    link_zero = jnp.zeros((size, NS, chan), f32)
    _, starts_true = lax.scan(link, link_zero, (decays_true, ends_true))
    start_state = of_blocks(starts_true, my_blocks).reshape(pair, NS, chan)
    (scan_blocks, _), scan_pull = jax.vjp(
        block_scan, start_state, rate, block_steps, block_inputs, block_writes, block_reads
    )
    skip_float = skip_gain.astype(f32)
    scanned = scan_blocks.reshape(rows_all, chan) + skip_float * signal_float
    gate_act = jax.nn.silu(gate_side)
    mamba_rows = (scanned * gate_act).astype(bf16)
    mamba_part = jnp.dot(mamba_rows, mamba_proj, preferred_element_type=f32).astype(bf16)
    mamba_out = scatter_rows(mamba_part, size, 7)
    mamba_normed, inv_mamba = norm_forward(mamba_out, gain_float[2])
    middle = stream + 0.5 * (attn_normed + mamba_normed)
    ffn_normed, inv_ffn = norm_forward(middle, gain_float[3])
    ffn_low = gather_rows(ffn_normed.astype(bf16), size, 8)
    gate_pre = jnp.dot(ffn_low, gate_mat, preferred_element_type=f32)
    up_pre = jnp.dot(ffn_low, up_mat, preferred_element_type=f32)
    hidden = (jax.nn.silu(gate_pre) * up_pre).astype(bf16)
    down_part = jnp.dot(hidden, down_weight, preferred_element_type=f32).astype(bf16)
    result = middle + scatter_rows(down_part, size, 9)
    down_wgrad = jnp.einsum("lf,ld->fd", hidden, grads_all, preferred_element_type=f32)
    hidden_back = jnp.einsum("ld,fd->lf", grads_all, down_weight, preferred_element_type=f32)
    gate_back = (hidden_back * up_pre * silu_slope(gate_pre)).astype(bf16)
    up_back = (hidden_back * jax.nn.silu(gate_pre)).astype(bf16)
    gate_wgrad = jnp.einsum("ld,lf->df", ffn_low, gate_back, preferred_element_type=f32)
    up_wgrad = jnp.einsum("ld,lf->df", ffn_low, up_back, preferred_element_type=f32)
    ffn_back_part = jnp.einsum(
        "lf,df->ld", gate_back, gate_mat, preferred_element_type=f32
    ) + jnp.einsum("lf,df->ld", up_back, up_mat, preferred_element_type=f32)
    ffn_back = scatter_rows(ffn_back_part.astype(bf16), size, 10)
    middle_part, ffn_gain_grad = norm_backward(ffn_back, middle, inv_ffn, gain_float[3])
    middle_back = out_grad[0].astype(f32) + middle_part
    branch_back = 0.5 * middle_back
    attn_part, attn_gain_grad = norm_backward(branch_back, attn_out, inv_attn, gain_float[1])
    mamba_part_back, mamba_gain_grad = norm_backward(
        branch_back, mamba_out, inv_mamba, gain_float[2]
    )
    attn_back = attn_part.astype(bf16)
    mamba_back = gather_rows(mamba_part_back.astype(bf16), size, 11)
    attn_wgrad = jnp.einsum("lh,ld->hd", attn_rows, attn_back, preferred_element_type=f32)
    rows_back = jnp.einsum("ld,hd->lh", attn_back, attn_mat, preferred_element_type=f32).astype(
        bf16
    )
    mamba_wgrad = jnp.einsum("li,ld->id", mamba_rows, mamba_back, preferred_element_type=f32)
    mrows_back = jnp.einsum("ld,id->li", mamba_back, mamba_proj, preferred_element_type=f32)
    scan_back = mrows_back * gate_act
    side_back = mrows_back * scanned * silu_slope(gate_side)
    skip_grad = jnp.sum(scan_back * signal_float, axis=0)
    block_dout = scan_back.reshape(pair, half_rows, chan)
    local_back = scan_pull((block_dout, zero_state))[0]
    backs_all = gather_ctx(local_back.astype(bf16).reshape(-1, chan), n_ctx, 12)
    backs_all = in_deal_order(backs_all.reshape(n_ctx, size, 2, NS, chan)).astype(f32)
    backs_true = jnp.take(backs_all, inverse, axis=0)

    def link_back(grad_next, both):
        decay_part, back_part = both
        return (back_part + decay_part * grad_next, grad_next)

    _, ends_back_true = lax.scan(link_back, link_zero, (decays_true, backs_true), reverse=True)
    end_back = of_blocks(ends_back_true, my_blocks).reshape(pair, NS, chan)
    _, rate_back, steps_back, inputs_back, writes_back, reads_back = scan_pull(
        (block_dout, end_back)
    )
    decay_grad = rate_back * rate
    step_back = steps_back.reshape(rows_all, chan)
    signal_back = scan_back * skip_float + inputs_back.reshape(rows_all, chan)
    write_back = writes_back.reshape(rows_all, NS)
    read_back = reads_back.reshape(rows_all, NS)
    pre_back = (step_back * jax.nn.sigmoid(step_pre)).astype(bf16)
    step_wgrad = jnp.einsum("lr,li->ri", step_low, pre_back, preferred_element_type=f32)
    bias_grad = jnp.sum(pre_back.astype(f32), axis=0)
    rank_back = jnp.einsum("li,ri->lr", pre_back, step_proj, preferred_element_type=f32)
    select_back = sum_rows(
        jnp.concatenate([rank_back, write_back, read_back], axis=1).astype(bf16), size, 13
    )
    select_wgrad = jnp.einsum("li,lk->ik", signal, select_back, preferred_element_type=f32)
    signal_back = signal_back + jnp.einsum(
        "lk,ik->li", select_back, select_proj, preferred_element_type=f32
    )
    conv_back = signal_back * silu_slope(conv_out)
    conv_blocks = conv_back.reshape(size, 2, half_rows, chan)
    taps_grad = jnp.stack(
        [
            jnp.sum(conv_blocks * padded[:, :, offset : offset + half_rows], axis=(0, 1, 2))
            for offset in range(CONV)
        ]
    )
    shift_grad = jnp.sum(conv_back, axis=0)
    padded_back = sum(
        (
            jnp.pad(
                taps_float[offset] * conv_blocks,
                ((0, 0), (0, 0), (offset, CONV - 1 - offset), (0, 0)),
            )
            for offset in range(CONV)
        )
    )
    tail_back = jnp.where(has_before[None, :, None, None], padded_back[:, :, : CONV - 1], 0.0)
    tails_back_all = gather_ctx(tail_back.astype(bf16).reshape(-1, chan), n_ctx, 14)
    tails_back_all = in_deal_order(tails_back_all.reshape(n_ctx, size, 2, CONV - 1, chan))
    after_index = inverse[jnp.minimum(my_blocks + 1, blocks_all - 1)]
    has_after = my_blocks < blocks_all - 1
    incoming = jnp.where(
        has_after[None, :, None, None], of_blocks(tails_back_all, after_index).astype(f32), 0.0
    )
    mixer_back = padded_back[:, :, CONV - 1 :] + jnp.pad(
        incoming, ((0, 0), (0, 0), (half_rows - (CONV - 1), 0), (0, 0))
    )
    entry_back = jnp.concatenate([mixer_back.reshape(rows_all, chan), side_back], axis=1).astype(
        bf16
    )
    entry_wgrad = jnp.einsum("ld,lk->dk", normed_all, entry_back, preferred_element_type=f32)
    input_part = jnp.einsum("lk,dk->ld", entry_back, entry_mat, preferred_element_type=f32)

    dout_groups = rows_back.reshape(rows, KV, group, HD).transpose(1, 0, 2, 3)

    def attend_back(parts):
        query_part, key_part, value_part, dout_part, log_part = parts
        scores = (
            jnp.einsum("lgd,sd->gls", query_part, key_part, preferred_element_type=f32)
            * score_scale
        )
        scores = jnp.where(allowed[None], scores, -1e30)
        probs = jnp.exp(scores - log_part)
        value_grad = jnp.einsum(
            "gls,lgd->sd", probs.astype(bf16), dout_part, preferred_element_type=f32
        )
        prob_grad = jnp.einsum("lgd,sd->gls", dout_part, value_part, preferred_element_type=f32)
        centre = jnp.sum(probs * prob_grad, axis=-1, keepdims=True)
        score_grad = (probs * (prob_grad - centre)).astype(bf16)
        query_grad = (
            jnp.einsum("gls,sd->lgd", score_grad, key_part, preferred_element_type=f32)
            * score_scale
        )
        key_grad = (
            jnp.einsum("gls,lgd->sd", score_grad, query_part, preferred_element_type=f32)
            * score_scale
        )
        return (query_grad, key_grad, value_grad)

    query_grads, key_grads, value_grads = lax.map(
        attend_back, (query_groups, key_groups, value_groups, dout_groups, log_totals)
    )
    keyval_terms = jnp.concatenate(
        [
            key_grads.transpose(1, 0, 2).reshape(-1, KV * HD),
            value_grads.transpose(1, 0, 2).reshape(-1, KV * HD),
        ],
        axis=1,
    )
    keyval_parts = exchange(
        keyval_terms.astype(bf16).reshape(n_ctx, rows, 2 * KV * HD), n_ctx, 15, "ctx"
    )
    keyval_back = jnp.sum(keyval_parts.astype(f32), axis=0).astype(bf16)
    query_back = query_grads.transpose(1, 0, 2, 3).reshape(rows, H * HD).astype(bf16)
    qkv_back = jnp.concatenate(
        [
            query_back.reshape(rows, size, q_cols),
            keyval_back.reshape(rows, size, kv_cols),
        ],
        axis=2,
    ).transpose(1, 0, 2)
    qkv_back = exchange(qkv_back, size, 16).reshape(rows_all, -1)
    qkv_wgrad = jnp.einsum("ld,lk->dk", normed_all, qkv_back, preferred_element_type=f32)
    input_part = input_part + jnp.einsum(
        "lk,dk->ld", qkv_back, qkv_mat, preferred_element_type=f32
    )
    input_back = scatter_rows(input_part.astype(bf16), size, 17)
    stream_part, in_gain_grad = norm_backward(input_back, stream, inv_in, gain_float[0])
    stream_back = middle_back + stream_part
    gain_grad = jnp.stack([in_gain_grad, attn_gain_grad, mamba_gain_grad, ffn_gain_grad])

    def over_ctx(values):
        return lax.psum_scatter(
            values.astype(bf16), "ctx", scatter_dimension=0, tiled=True
        )

    def join(piece):
        return lax.all_gather(piece, "ctx", axis=0, tiled=True)

    def columns_home(wgrad):
        cols = wgrad.shape[1]
        cut = wgrad.reshape(size, n_ctx, depth // n_ctx, cols) if depth % n_ctx == 0 else None
        if cut is None:
            whole = lax.psum(wgrad.astype(bf16), "ctx")
            moved = lax.all_to_all(whole.reshape(size, depth, cols), "fsdp", 0, 0, tiled=True)
            return moved.transpose(1, 0, 2).astype(f32)
        piece = over_ctx(cut.transpose(1, 0, 2, 3).reshape(-1, cols))
        moved = lax.all_to_all(
            piece.reshape(size, depth // n_ctx, cols), "fsdp", 0, 0, tiled=True
        ).transpose(1, 0, 2)
        return join(moved).astype(f32)

    first_home = columns_home(jnp.concatenate([qkv_wgrad, entry_wgrad], axis=1))
    ffn_home = columns_home(jnp.concatenate([gate_wgrad, up_wgrad], axis=1))
    query_share = first_home[:, :, :q_cols].reshape(depth, -1)
    keyval_share = first_home[:, :, q_cols : q_cols + kv_cols].reshape(depth, -1)
    entry_share = jnp.concatenate(
        [
            first_home[:, :, q_cols + kv_cols : q_cols + kv_cols + chan].reshape(depth, -1),
            first_home[:, :, q_cols + kv_cols + chan :].reshape(depth, -1),
        ],
        axis=1,
    )
    gate_share = ffn_home[:, :, :ff_cols].reshape(depth, -1)
    up_share = ffn_home[:, :, ff_cols:].reshape(depth, -1)

    def all_ctx(values):
        return lax.psum(values.astype(bf16), "ctx").astype(f32)

    attn_share = all_ctx(
        lax.psum_scatter(attn_wgrad.astype(bf16), "fsdp", scatter_dimension=0, tiled=True)
    )
    gain_share = all_ctx(
        lax.psum_scatter(gain_grad.astype(bf16), "fsdp", scatter_dimension=1, tiled=True)
    )
    vectors = jnp.concatenate(
        [
            taps_grad,
            shift_grad[None],
            bias_grad[None],
            skip_grad[None],
            decay_grad,
            step_wgrad,
        ]
    )
    vectors = all_ctx(vectors)
    return (
        result.astype(bf16)[None],
        stream_back[None],
        gain_share,
        query_share,
        keyval_share,
        attn_share,
        entry_share,
        vectors[:CONV],
        vectors[CONV],
        vectors[CONV + 1],
        vectors[CONV + 2],
        vectors[CONV + 3 : CONV + 3 + NS],
        all_ctx(select_wgrad),
        vectors[CONV + 3 + NS :],
        all_ctx(mamba_wgrad),
        gate_share,
        up_share,
        all_ctx(down_wgrad),
    )


def solution(mesh):
    in_specs = (
        P("fsdp", "ctx", None),
        P("fsdp", "ctx", None),
        P("fsdp", None),
        P(),
        P(None, "fsdp"),
        P("fsdp", None),
        P("fsdp", None),
        P("fsdp", None),
        P("fsdp", None),
        P(None, "fsdp"),
        P("fsdp"),
        P("fsdp"),
        P("fsdp"),
        P(None, "fsdp"),
        P("fsdp", None),
        P(None, "fsdp"),
        P("fsdp", None),
        P("fsdp", None),
        P("fsdp", None),
        P("fsdp", None),
    )
    out_specs = (
        P("fsdp", "ctx", None),
        P("fsdp", "ctx", None),
        P(None, "fsdp"),
        P("fsdp", None),
        P("fsdp", None),
        P("fsdp", None),
        P("fsdp", None),
        P(None, "fsdp"),
        P("fsdp"),
        P("fsdp"),
        P("fsdp"),
        P(None, "fsdp"),
        P("fsdp", None),
        P(None, "fsdp"),
        P("fsdp", None),
        P("fsdp", None),
        P("fsdp", None),
        P("fsdp", None),
    )
    return jax.shard_map(
        on_device, mesh=mesh, in_specs=in_specs, out_specs=out_specs, check_vma=False
    )
```

```python
import functools
import math

import jax
import jax.numpy as jnp
from jax import lax
from jax.experimental import pallas as pl
from jax.experimental.pallas import tpu as pltpu
from jax.sharding import PartitionSpec as P

H = 25
KV = 5
HD = 64
INNER = 3200
NS = 16
RANK = 100
CONV = 4

EPS = 1e-06
score_scale = 0.125
MESH = pl.DeviceIdType.MESH
ANY = pl.BlockSpec(memory_space=pl.ANY)
VM = pl.BlockSpec(memory_space=pltpu.VMEM)
DMA = pltpu.SemaphoreType.DMA
f32 = jnp.float32
bf16 = jnp.bfloat16


def params(cid, vmem=None):
    return pltpu.CompilerParams(collective_id=cid, has_side_effects=True, vmem_limit_bytes=vmem)


def rcopy(src, dst, ssem, rsem, dev):
    return pltpu.make_async_remote_copy(
        src_ref=src, dst_ref=dst, send_sem=ssem, recv_sem=rsem, device_id=dev, device_id_type=MESH
    )


def norm_forward(values, gain):
    inverse = lax.rsqrt(jnp.mean(values * values, axis=-1, keepdims=True) + EPS)
    return (values * inverse * gain, inverse)


def norm_backward(grad, values, inverse, gain):
    normed = values * inverse
    gain_grad = jnp.sum(grad * normed, axis=0)
    scaled = grad * gain
    return (
        inverse * (scaled - normed * jnp.mean(scaled * normed, axis=-1, keepdims=True)),
        gain_grad,
    )


def silu_slope(values):
    sigma = jax.nn.sigmoid(values)
    return sigma * (1.0 + values * (1.0 - sigma))


UNROLL = 8


def steps(length, body, init):
    count = UNROLL if length % UNROLL == 0 else 1

    def some(i, carry):
        for j in range(count):
            carry = body(i * count + j, carry)
        return carry

    return lax.fori_loop(0, length // count, some, init)


def turn(refs, streams):
    return [ref.reshape(streams * ref.shape[-2], ref.shape[-1]) for ref in refs]


def spread(wr, at, out, first, streams, length):
    def body(o, carry):
        values = wr[pl.ds(o, streams, stride=length), :]
        for n in range(NS):
            out[o, n] = jnp.broadcast_to(values[:, first + n : first + n + 1], (streams, 128))
        return carry

    steps(length, body, 0)


def rows_of(ref, o, streams, length):
    return ref[pl.ds(o, streams, stride=length), :]


def scan_ends(dt, x, wr, rate2):
    everyone, _, length, chan = dt.shape
    streams = math.gcd(everyone, 8)

    def kernel(dt_ref, x_ref, wr_ref, rate_ref, o_ref, wb):
        dt_ref, x_ref, wr_ref = turn((dt_ref, x_ref, wr_ref), streams)

        @pl.when(pl.program_id(2) == 0)
        def _():
            spread(wr_ref, None, wb, 0, streams, length)

        rates = [rate_ref[n : n + 1, :] for n in range(NS)]

        def body(o, carry):
            total, states = carry
            step = rows_of(dt_ref, o, streams, length)
            pushed = step * rows_of(x_ref, o, streams, length)
            states = tuple(
                jnp.exp2(step * rates[n]) * states[n] + wb[o, n] * pushed for n in range(NS)
            )
            return (total + step, states)

        zero = jnp.zeros((streams, 128), f32)
        total, states = steps(length, body, (zero, (zero,) * NS))
        for n in range(NS):
            o_ref[n] = states[n].astype(bf16)
        o_ref[NS] = total.astype(bf16)

    tok = pl.BlockSpec((streams, None, length, 128), lambda b, g, c: (g, b, 0, c))
    return pl.pallas_call(
        kernel,
        grid=(2, everyone // streams, chan // 128),
        in_specs=[
            tok,
            tok,
            pl.BlockSpec((streams, None, length, 2 * NS), lambda b, g, c: (g, b, 0, 0)),
            pl.BlockSpec((NS, 128), lambda b, g, c: (0, c)),
        ],
        out_specs=pl.BlockSpec((None, NS + 1, streams, 128), lambda b, g, c: (b, 0, g, c)),
        out_shape=jax.ShapeDtypeStruct((2, NS + 1, everyone, chan), bf16),
        scratch_shapes=[pltpu.VMEM((length, NS, streams, 128), f32)],
        compiler_params=pltpu.CompilerParams(vmem_limit_bytes=60 << 20),
        name="scan_ends",
    )(dt, x, wr, rate2)


def scan_forward(order, dt, x, wr, rate2, ends):
    everyone, _, length, chan = dt.shape
    streams = math.gcd(everyone, 8)
    blocks = ends.shape[0]

    def kernel(order_ref, dt_ref, x_ref, wr_ref, rate_ref, ends_ref, y_ref, s_ref, wb, rb):
        dt_ref, x_ref, wr_ref = turn((dt_ref, x_ref, wr_ref), streams)
        y_ref = y_ref.reshape(streams * length, 128)
        blk = pl.program_id(0)

        @pl.when(pl.program_id(2) == 0)
        def _():
            spread(wr_ref, None, wb, 0, streams, length)
            spread(wr_ref, None, rb, NS, streams, length)

        rates = [rate_ref[n : n + 1, :] for n in range(NS)]

        def link(b, states):
            at = order_ref[b]
            total = ends_ref[at, NS].astype(f32)
            return tuple(
                jnp.exp2(total * rates[n]) * states[n] + ends_ref[at, n].astype(f32)
                for n in range(NS)
            )

        zero = jnp.zeros((streams, 128), f32)
        states = lax.fori_loop(0, order_ref[blocks + blk], link, (zero,) * NS)
        for n in range(NS):
            s_ref[n] = states[n]

        def body(o, states):
            step = rows_of(dt_ref, o, streams, length)
            pushed = step * rows_of(x_ref, o, streams, length)
            states = tuple(
                jnp.exp2(step * rates[n]) * states[n] + wb[o, n] * pushed for n in range(NS)
            )
            total = [rb[o, n] * states[n] for n in range(NS)]
            while len(total) > 1:
                total = [total[i] + total[i + 1] for i in range(0, len(total), 2)]
            y_ref[pl.ds(o, streams, stride=length), :] = total[0]
            return states

        steps(length, body, states)

    tok = pl.BlockSpec((streams, None, length, 128), lambda b, g, c, *_: (g, b, 0, c))
    return pl.pallas_call(
        kernel,
        grid_spec=pltpu.PrefetchScalarGridSpec(
            num_scalar_prefetch=1,
            grid=(2, everyone // streams, chan // 128),
            in_specs=[
                tok,
                tok,
                pl.BlockSpec((streams, None, length, 2 * NS), lambda b, g, c, *_: (g, b, 0, 0)),
                pl.BlockSpec((NS, 128), lambda b, g, c, *_: (0, c)),
                pl.BlockSpec((blocks, NS + 1, streams, 128), lambda b, g, c, *_: (0, 0, g, c)),
            ],
            out_specs=[
                tok,
                pl.BlockSpec((None, NS, streams, 128), lambda b, g, c, *_: (b, 0, g, c)),
            ],
            scratch_shapes=[pltpu.VMEM((length, NS, streams, 128), f32)] * 2,
        ),
        out_shape=[
            jax.ShapeDtypeStruct(dt.shape, f32),
            jax.ShapeDtypeStruct((2, NS, everyone, chan), f32),
        ],
        compiler_params=pltpu.CompilerParams(vmem_limit_bytes=60 << 20),
        name="scan_forward",
    )(order, dt, x, wr, rate2, ends)


def scan_backs(dt, g, wr, rate2):
    everyone, _, length, chan = dt.shape
    streams = math.gcd(everyone, 8)

    def kernel(dt_ref, g_ref, wr_ref, rate_ref, o_ref, rb):
        dt_ref, g_ref, wr_ref = turn((dt_ref, g_ref, wr_ref), streams)

        @pl.when(pl.program_id(2) == 0)
        def _():
            spread(wr_ref, None, rb, NS, streams, length)

        rates = [rate_ref[n : n + 1, :] for n in range(NS)]

        def body(i, carries):
            o = length - 1 - i
            step = rows_of(dt_ref, o, streams, length)
            grad = rows_of(g_ref, o, streams, length)
            return tuple(
                jnp.exp2(step * rates[n]) * (carries[n] + rb[o, n] * grad) for n in range(NS)
            )

        zero = jnp.zeros((streams, 128), f32)
        carries = steps(length, body, (zero,) * NS)
        for n in range(NS):
            o_ref[n] = carries[n].astype(bf16)

    tok = pl.BlockSpec((streams, None, length, 128), lambda b, g, c: (g, b, 0, c))
    return pl.pallas_call(
        kernel,
        grid=(2, everyone // streams, chan // 128),
        in_specs=[
            tok,
            tok,
            pl.BlockSpec((streams, None, length, 2 * NS), lambda b, g, c: (g, b, 0, 0)),
            pl.BlockSpec((NS, 128), lambda b, g, c: (0, c)),
        ],
        out_specs=pl.BlockSpec((None, NS, streams, 128), lambda b, g, c: (b, 0, g, c)),
        out_shape=jax.ShapeDtypeStruct((2, NS, everyone, chan), bf16),
        scratch_shapes=[pltpu.VMEM((length, NS, streams, 128), f32)],
        compiler_params=pltpu.CompilerParams(vmem_limit_bytes=60 << 20),
        name="scan_backs",
    )(dt, g, wr, rate2)


def scan_backward(order, dt, x, g, wr, rate2, starts, ends, backs):
    everyone, _, length, chan = dt.shape
    streams = math.gcd(everyone, 8)
    blocks = ends.shape[0]
    tiles = chan // 128

    def kernel(
        order_ref,
        dt_ref,
        x_ref,
        g_ref,
        wr_ref,
        rate_ref,
        start_ref,
        ends_ref,
        backs_ref,
        sb_ref,
        cw_ref,
        wrb_ref,
        dec_ref,
        wb,
        rb,
        kept,
        decays,
        wparts,
        rparts,
        sums,
    ):
        dt_ref, x_ref, g_ref, wr_ref = turn((dt_ref, x_ref, g_ref, wr_ref), streams)
        sb_ref, cw_ref, wrb_ref = turn((sb_ref, cw_ref, wrb_ref), streams)
        blk, tile = pl.program_id(0), pl.program_id(2)

        @pl.when(tile == 0)
        def _():
            spread(wr_ref, None, wb, 0, streams, length)
            spread(wr_ref, None, rb, NS, streams, length)
            sums[...] = jnp.zeros_like(sums)

        rates = [rate_ref[n : n + 1, :] for n in range(NS)]

        def forward(o, states):
            step = rows_of(dt_ref, o, streams, length)
            pushed = step * rows_of(x_ref, o, streams, length)
            new = []
            for n in range(NS):
                decay = jnp.exp2(step * rates[n])
                decays[o, n] = decay
                kept[o, n] = states[n]
                new.append(decay * states[n] + wb[o, n] * pushed)
            return tuple(new)

        last = steps(length, forward, tuple(start_ref[n] for n in range(NS)))
        for n in range(NS):
            kept[length, n] = last[n]

        def link(i, carries):
            at = order_ref[blocks - 1 - i]
            total = ends_ref[at, 0].astype(f32)
            return tuple(
                backs_ref[at, n].astype(f32) + jnp.exp2(total * rates[n]) * carries[n]
                for n in range(NS)
            )

        zero = jnp.zeros((streams, 128), f32)
        carries = lax.fori_loop(
            0, blocks - 1 - order_ref[blocks + blk], link, (zero,) * NS
        )
        for n in range(NS):
            dec_ref[n] = zero

        def body(i, carries):
            o = length - 1 - i
            step = rows_of(dt_ref, o, streams, length)
            value = rows_of(x_ref, o, streams, length)
            grad = rows_of(g_ref, o, streams, length)
            pushed = step * value
            slope, pulled, new = [], [], []
            at = pl.ds(pl.multiple_of(o * streams, streams), streams)
            for n in range(NS):
                full = carries[n] + rb[o, n] * grad
                moved = decays[o, n] * full
                new.append(moved)
                back = moved * kept[o, n]
                slope.append(back * rates[n])
                dec_ref[n] += back * step
                pulled.append(full * wb[o, n])
                wparts[at, n * 128 : (n + 1) * 128] = full * pushed
                rparts[at, n * 128 : (n + 1) * 128] = kept[o + 1, n] * grad
            while len(slope) > 1:
                slope = [slope[i] + slope[i + 1] for i in range(0, len(slope), 2)]
                pulled = [pulled[i] + pulled[i + 1] for i in range(0, len(pulled), 2)]
            sb_ref[pl.ds(o, streams, stride=length), :] = (
                slope[0] * 0.6931471805599453 + pulled[0] * value
            )
            cw_ref[pl.ds(o, streams, stride=length), :] = pulled[0]
            return tuple(new)

        steps(length, body, carries)
        source = lax.broadcasted_iota(jnp.int32, (NS * 128, 128), 0) // 128
        target = lax.broadcasted_iota(jnp.int32, (NS * 128, 128), 1)
        pick_w = jnp.where(source == target, 1.0, 0.0).astype(bf16)
        pick_r = jnp.where(source + NS == target, 1.0, 0.0).astype(bf16)
        sums[...] += jnp.dot(
            wparts[...].astype(bf16), pick_w, preferred_element_type=f32
        ) + jnp.dot(rparts[...].astype(bf16), pick_r, preferred_element_type=f32)

        @pl.when(tile == tiles - 1)
        def _():
            def out(o, carry):
                wrb_ref[pl.ds(o, streams, stride=length), :] = sums[
                    pl.ds(pl.multiple_of(o * streams, streams), streams), :
                ]
                return carry

            steps(length, out, 0)

    tok = pl.BlockSpec((streams, None, length, 128), lambda b, g, c, *_: (g, b, 0, c))
    state = pl.BlockSpec((None, NS, streams, 128), lambda b, g, c, *_: (b, 0, g, c))
    big = pltpu.VMEM((length, NS, streams, 128), f32)
    return pl.pallas_call(
        kernel,
        grid_spec=pltpu.PrefetchScalarGridSpec(
            num_scalar_prefetch=1,
            grid=(2, everyone // streams, tiles),
            in_specs=[
                tok,
                tok,
                tok,
                pl.BlockSpec((streams, None, length, 2 * NS), lambda b, g, c, *_: (g, b, 0, 0)),
                pl.BlockSpec((NS, 128), lambda b, g, c, *_: (0, c)),
                state,
                pl.BlockSpec((blocks, 1, streams, 128), lambda b, g, c, *_: (0, NS, g, c)),
                pl.BlockSpec((blocks, NS, streams, 128), lambda b, g, c, *_: (0, 0, g, c)),
            ],
            out_specs=[
                tok,
                tok,
                pl.BlockSpec((streams, None, length, 128), lambda b, g, c, *_: (g, b, 0, 0)),
                state,
            ],
            scratch_shapes=[
                big,
                big,
                pltpu.VMEM((length + 1, NS, streams, 128), f32),
                big,
                pltpu.VMEM((length * streams, NS * 128), f32),
                pltpu.VMEM((length * streams, NS * 128), f32),
                pltpu.VMEM((length * streams, 128), f32),
            ],
        ),
        out_shape=[
            jax.ShapeDtypeStruct(dt.shape, f32),
            jax.ShapeDtypeStruct(dt.shape, f32),
            jax.ShapeDtypeStruct((everyone, 2, length, 128), f32),
            jax.ShapeDtypeStruct((2, NS, everyone, chan), f32),
        ],
        compiler_params=pltpu.CompilerParams(vmem_limit_bytes=60 << 20),
        name="scan_backward",
    )(order, dt, x, g, wr, rate2, starts, ends, backs)


def up_to(value, step):
    return (value + step - 1) // step * step


def pack_columns(weights, cuts, offsets, total, size):
    depth = weights[0].shape[0]

    def kernel(*refs):
        o_ref = refs[-1]
        o_ref[...] = jnp.zeros_like(o_ref)
        for (which, first, cols), at in zip(cuts, offsets):
            for f in range(size):
                o_ref[f, :, at : at + cols] = refs[which][
                    :, first + f * cols : first + (f + 1) * cols
                ]

    return pl.pallas_call(
        kernel,
        out_shape=jax.ShapeDtypeStruct((size, depth, total), bf16),
        in_specs=[VM] * len(weights),
        out_specs=VM,
        compiler_params=pltpu.CompilerParams(vmem_limit_bytes=60 << 20),
        name="pack_columns",
    )(*weights)


def unpack_columns(home, cuts, offsets, shapes, quarter):
    n, size, depth, _ = home.shape

    def kernel(h_ref, *outs):
        for (which, first, cols), at in zip(cuts, offsets):
            for f in range(size):
                parts = []
                lo = at
                while lo < at + cols:
                    q, inside = divmod(lo, quarter)
                    hi = min(at + cols, (q + 1) * quarter)
                    parts.append((q, inside, hi - lo, lo - at))
                    lo = hi
                for q, inside, count, shift in parts:
                    to = first + f * cols + shift
                    outs[which][:, to : to + count] = h_ref[
                        q, f, :, inside : inside + count
                    ].astype(f32)

    return pl.pallas_call(
        kernel,
        out_shape=[jax.ShapeDtypeStruct(shape, f32) for shape in shapes],
        in_specs=[VM],
        out_specs=[VM] * len(shapes),
        compiler_params=pltpu.CompilerParams(vmem_limit_bytes=60 << 20),
        name="unpack_columns",
    )(home)


def weight_grad(x, dy, quarter):
    rows, width = x.shape
    n = dy.shape[1] // quarter

    def kernel(x_ref, y_ref, o_ref):
        o_ref[...] = lax.dot_general(
            x_ref[...], y_ref[...], (((0,), (0,)), ((), ())), preferred_element_type=f32
        ).astype(bf16)

    return pl.pallas_call(
        kernel,
        grid=(n,),
        in_specs=[
            pl.BlockSpec((rows, width), lambda q: (0, 0)),
            pl.BlockSpec((rows, quarter), lambda q: (0, q)),
        ],
        out_specs=pl.BlockSpec((None, width, quarter), lambda q: (q, 0, 0)),
        out_shape=jax.ShapeDtypeStruct((n, width, quarter), bf16),
        compiler_params=pltpu.CompilerParams(vmem_limit_bytes=60 << 20),
        name="weight_grad",
    )(x, dy)


class Job:
    def __init__(self, steps, ins, outs, scratch):
        self.steps, self.ins, self.outs, self.scratch = steps, ins, outs, scratch


class Place:
    def __init__(self, size):
        self.size, self.lanes = size, size // 2
        self.f, self.c = lax.axis_index("fsdp"), lax.axis_index("ctx")
        self.a, self.b = self.f // 2, lax.rem(self.f, 2)
        self.near = self.c + 1 - 2 * lax.rem(self.c, 2)
        self.far = lax.rem(self.c + 2, 4)
        self.other = lax.rem(self.near + 2, 4)

    def greet(self):
        bar = pltpu.get_barrier_semaphore()
        for d in range(1, self.size):
            peer = {"fsdp": lax.rem(self.f + d, self.size)}
            pl.semaphore_signal(bar, inc=1, device_id=peer, device_id_type=MESH)
        for peer in (self.near, self.far):
            pl.semaphore_signal(bar, inc=1, device_id={"ctx": peer}, device_id_type=MESH)
        pl.semaphore_wait(bar, self.size + 1)


def part(ref_list, jobs, field):
    out = []
    for job in jobs:
        count = len(getattr(job, field))
        out.append(ref_list[:count])
        ref_list = ref_list[count:]
    return out


def together(jobs, size, cid, name):
    n_in = sum(len(job.ins) for job in jobs)
    n_out = sum(len(job.outs) for job in jobs)

    def kernel(*refs):
        place = Place(size)
        place.greet()
        ins = part(refs[:n_in], jobs, "ins")
        outs = part(refs[n_in : n_in + n_out], jobs, "outs")
        scratch = part(refs[n_in + n_out :], jobs, "scratch")
        live = [job.steps(place, i, o, s) for job, i, o, s in zip(jobs, ins, outs, scratch)]
        while live:
            still = []
            for steps_ in live:
                try:
                    next(steps_)
                    still.append(steps_)
                except StopIteration:
                    pass
            live = still

    got = pl.pallas_call(
        kernel,
        out_shape=[shape for job in jobs for shape, _ in job.outs],
        in_specs=[spec for job in jobs for _, spec in job.ins],
        out_specs=[spec for job in jobs for _, spec in job.outs],
        scratch_shapes=[item for job in jobs for item in job.scratch],
        compiler_params=params(cid, 60 << 20),
        name=name,
    )(*[array for job in jobs for array, _ in job.ins])
    return part(got, jobs, "outs")


def like(shape, dtype):
    return jax.ShapeDtypeStruct(shape, dtype)


def gather_job(x, size):
    rows, cols = x.shape
    lanes = size // 2

    def run(p, ins, outs, scratch):
        (x_ref,), (o_ref,) = ins, outs
        lsem, up_s, up_r, dn_s, dn_r, px_s, px_r = scratch

        def piece(origin, b):
            return o_ref.at[pl.ds(pl.multiple_of((2 * origin + b) * rows, rows), rows)]

        def local():
            return pltpu.make_async_copy(x_ref, piece(p.a, p.b), lsem)

        def up(s):
            src = x_ref if s == 0 else piece(p.a - s, p.b)
            dev = {"fsdp": 2 * (p.a + 1) + p.b}
            return rcopy(src, piece(p.a - s, p.b), up_s.at[s], up_r.at[s], dev)

        def down(s):
            src = x_ref if s == 0 else piece(p.a + s, p.b)
            dev = {"fsdp": 2 * (p.a - 1) + p.b}
            return rcopy(src, piece(p.a + s, p.b), dn_s.at[s], dn_r.at[s], dev)

        def across(origin, src=None):
            src = piece(origin, p.b) if src is None else src
            dev = {"fsdp": 2 * p.a + 1 - p.b}
            return rcopy(src, piece(origin, p.b), px_s.at[origin], px_r.at[origin], dev)

        def came(ref, sem, dev):
            rcopy(ref, ref, sem, sem, dev).wait_recv()

        @pl.when(p.a < lanes - 1)
        def _():
            up(0).start()

        @pl.when(p.a > 0)
        def _():
            down(0).start()

        across(p.a, x_ref).start()
        local().start()
        yield
        for s in range(lanes - 1):
            @pl.when(p.a - 1 - s >= 0)
            def _():
                came(piece(p.a - 1 - s, p.b), up_r.at[s], {"fsdp": 2 * (p.a - 1) + p.b})

                @pl.when(p.a < lanes - 1)
                def _():
                    up(s + 1).start()

                across(p.a - 1 - s).start()

            @pl.when(p.a + 1 + s <= lanes - 1)
            def _():
                came(piece(p.a + 1 + s, p.b), dn_r.at[s], {"fsdp": 2 * (p.a + 1) + p.b})

                @pl.when(p.a > 0)
                def _():
                    down(s + 1).start()

                across(p.a + 1 + s).start()

            yield
        local().wait()
        for s in range(lanes - 1):
            @pl.when((p.a - s >= 0) & (p.a < lanes - 1))
            def _():
                up(s).wait_send()

            @pl.when((p.a + s <= lanes - 1) & (p.a > 0))
            def _():
                down(s).wait_send()

        for origin in range(lanes):
            across(origin).wait_send()
            came(piece(origin, 1 - p.b), px_r.at[origin], {"fsdp": 2 * p.a + 1 - p.b})

    return Job(
        run, [(x, ANY)], [(like((size * rows, cols), x.dtype), ANY)], [DMA] + [DMA((lanes,))] * 6
    )


def add_blocks(out, terms, dtype, rows):
    if rows % 16:
        total = terms[0][...].astype(f32)
        for ref in terms[1:]:
            total += ref[...].astype(f32)
        out[...] = total.astype(dtype)
        return
    step = 32 if rows % 32 == 0 else 16

    def body(i, carry):
        at = pl.ds(pl.multiple_of(i * step, step), step)
        total = terms[0][at, :].astype(f32)
        for ref in terms[1:]:
            total += ref[at, :].astype(f32)
        out[at, :] = total.astype(dtype)
        return carry

    lax.fori_loop(0, rows // step, body, 0)


def scatter_job(partial, size):
    rows, cols = partial.shape[1:]
    lanes = size // 2

    def run(p, ins, outs, scratch):
        (p_ref,), (o_ref,) = ins, outs
        xbuf, upb, dnb, up_s, up_r, dn_s, dn_r, px_s, px_r = scratch

        def across(dest):
            src = p_ref.at[2 * dest + 1 - p.b]
            dev = {"fsdp": 2 * p.a + 1 - p.b}
            return rcopy(src, xbuf.at[dest], px_s.at[dest], px_r.at[dest], dev)

        def up(dest):
            dev = {"fsdp": 2 * (p.a + 1) + p.b}
            return rcopy(xbuf.at[dest], upb.at[dest], up_s.at[dest], up_r.at[dest], dev)

        def down(dest):
            dev = {"fsdp": 2 * (p.a - 1) + p.b}
            return rcopy(xbuf.at[dest], dnb.at[dest], dn_s.at[dest], dn_r.at[dest], dev)

        def add_in(dest, extra):
            terms = [xbuf.at[dest], p_ref.at[2 * dest + p.b]]
            if extra is not None:
                terms.append(extra.at[dest])
            add_blocks(xbuf.at[dest], terms, bf16, rows)

        for d in range(lanes - 1, -1, -1):
            @pl.when(p.a + d <= lanes - 1)
            def _():
                across(p.a + d).start()

            if d > 0:
                @pl.when(p.a - d >= 0)
                def _():
                    across(p.a - d).start()

        yield
        for d in range(lanes - 1, 0, -1):
            @pl.when(p.a + d <= lanes - 1)
            def _():
                across(p.a + d).wait_recv()

                @pl.when(p.a > 0)
                def _():
                    up(p.a + d).wait_recv()
                    add_in(p.a + d, upb)

                @pl.when(p.a == 0)
                def _():
                    add_in(p.a + d, None)

                up(p.a + d).start()

            @pl.when(p.a - d >= 0)
            def _():
                across(p.a - d).wait_recv()

                @pl.when(p.a < lanes - 1)
                def _():
                    down(p.a - d).wait_recv()
                    add_in(p.a - d, dnb)

                @pl.when(p.a == lanes - 1)
                def _():
                    add_in(p.a - d, None)

                down(p.a - d).start()

            yield
        across(p.a).wait_recv()
        terms = [xbuf.at[p.a], p_ref.at[2 * p.a + p.b]]

        @pl.when(p.a == 0)
        def _():
            down(p.a).wait_recv()
            add_blocks(o_ref, terms + [dnb.at[p.a]], f32, rows)

        @pl.when(p.a == lanes - 1)
        def _():
            up(p.a).wait_recv()
            add_blocks(o_ref, terms + [upb.at[p.a]], f32, rows)

        @pl.when((p.a > 0) & (p.a < lanes - 1))
        def _():
            up(p.a).wait_recv()
            down(p.a).wait_recv()
            add_blocks(o_ref, terms + [upb.at[p.a], dnb.at[p.a]], f32, rows)

        for dest in range(lanes):
            across(dest).wait_send()

        for d in range(lanes - 1, 0, -1):
            @pl.when(p.a + d <= lanes - 1)
            def _():
                up(p.a + d).wait_send()

            @pl.when(p.a - d >= 0)
            def _():
                down(p.a - d).wait_send()

    return Job(
        run,
        [(partial, VM)],
        [(like((rows, cols), f32), VM)],
        [pltpu.VMEM((lanes, rows, cols), bf16)] * 3 + [DMA((lanes,))] * 6,
    )


def column_block(of, quarter):
    return pl.ds(pl.multiple_of(of * quarter, 128), quarter)


class Share:
    def __init__(self, p, view, count, sems):
        self.p, self.view, self.count = p, view, count
        self.fs, self.fr, self.ns, self.nr, self.hs, self.hr = sems

    def far(self, d, q):
        ref = self.view(d, q)
        return rcopy(ref, ref, self.fs.at[d], self.fr.at[d], {"ctx": self.p.far})

    def near(self, d, q):
        ref = self.view(d, q)
        return rcopy(ref, ref, self.ns.at[d], self.nr.at[d], {"ctx": self.p.near})

    def onward(self, d, q):
        ref = self.view(d, q)
        return rcopy(ref, ref, self.hs.at[d], self.hr.at[d], {"ctx": self.p.near})

    def send(self, d):
        self.far(d, self.p.c).start()
        self.near(d, self.p.c).start()

    def forward(self, d):
        self.far(d, self.p.far).wait_recv()
        self.onward(d, self.p.far).start()

    def finish(self):
        p = self.p
        for d in range(self.count):
            self.far(d, p.c).wait_send()
            self.near(d, p.c).wait_send()
            self.near(d, p.near).wait_recv()
            self.onward(d, p.far).wait_send()
            self.onward(d, p.other).wait_recv()


def share_sems(count):
    return [DMA((count,))] * 6


def move_job(packed, size, per_device=True):
    depth, total = packed.shape[-2:]
    quarter = total // 4

    def run(p, ins, outs, scratch):
        (p_ref,), (w_ref,) = ins, outs
        lsem, ws, wr = scratch[:3]

        def source(to):
            block = column_block(p.c, quarter)
            return p_ref.at[to, :, block] if per_device else p_ref.at[:, block]

        def view(d, q):
            return w_ref.at[lax.rem(p.f - d + size, size), :, column_block(q, quarter)]

        def local():
            return pltpu.make_async_copy(source(p.f), view(0, p.c), lsem)

        def move(d):
            to = lax.rem(p.f + d, size)
            return rcopy(source(to), view(0, p.c), ws.at[d], wr.at[d], {"fsdp": to})

        def came(d):
            ref = view(d, p.c)
            rcopy(ref, ref, ws.at[d], wr.at[d], {"fsdp": lax.rem(p.f + d, size)}).wait_recv()

        share = Share(p, view, size, scratch[3:])
        local().start()
        for d in range(1, size):
            move(d).start()
        yield
        local().wait()
        share.send(0)
        for d in range(1, size):
            came(d)
            share.send(d)
            if d % 2 == 0:
                yield
        for d in range(size):
            share.forward(d)
            if d % 4 == 3:
                yield
        share.finish()
        for d in range(1, size):
            move(d).wait_send()

    return Job(
        run,
        [(packed, ANY)],
        [(like((size, depth, total), packed.dtype), ANY)],
        [DMA, DMA((size,)), DMA((size,))] + share_sems(size),
    )


def spread_job(x, size):
    def run(p, ins, outs, scratch):
        (x_ref,), (o_ref,) = ins, outs
        lsem, ss, rs = scratch

        def copy(d):
            to = {"fsdp": lax.rem(p.f + d, size)}
            return rcopy(x_ref, o_ref.at[p.f], ss.at[d], rs.at[d], to)

        def local():
            return pltpu.make_async_copy(x_ref, o_ref.at[p.f], lsem)

        local().start()
        for d in range(1, size):
            copy(d).start()
        yield
        local().wait()
        for d in range(1, size):
            copy(d).wait()

    return Job(
        run,
        [(x, ANY)],
        [(like((size,) + x.shape, x.dtype), ANY)],
        [DMA, DMA((size,)), DMA((size,))],
    )


def exchange_job(x, size):
    def run(p, ins, outs, scratch):
        (x_ref,), (o_ref,) = ins, outs
        lsem, ss, rs = scratch

        def copy(d):
            to = lax.rem(p.f + d, size)
            return rcopy(x_ref.at[to], o_ref.at[p.f], ss.at[d], rs.at[d], {"fsdp": to})

        def local():
            return pltpu.make_async_copy(x_ref.at[p.f], o_ref.at[p.f], lsem)

        for d in range(1, size):
            copy(d).start()
        local().start()
        yield
        local().wait()
        for d in range(1, size):
            copy(d).wait()

    return Job(
        run, [(x, ANY)], [(like(x.shape, x.dtype), ANY)], [DMA, DMA((size,)), DMA((size,))]
    )


def ctx_gather_job(x):
    def run(p, ins, outs, scratch):
        (x_ref,), (o_ref,) = ins, outs
        share = Share(p, lambda d, q: o_ref.at[q], 1, scratch[1:])

        def local():
            return pltpu.make_async_copy(x_ref, o_ref.at[p.c], scratch[0])

        def first(to, ss, rs):
            return rcopy(x_ref, o_ref.at[p.c], ss.at[0], rs.at[0], {"ctx": to})

        first(p.far, share.fs, share.fr).start()
        first(p.near, share.ns, share.nr).start()
        local().start()
        yield
        share.forward(0)
        yield
        local().wait()
        share.finish()

    return Job(
        run, [(x, ANY)], [(like((4,) + x.shape, x.dtype), ANY)], [DMA] + share_sems(1)
    )


class Halve:
    def __init__(self, p, source, bufs, sems):
        self.p, self.source = p, source
        self.own, self.got, self.away, self.total = bufs
        self.ls, self.ns, self.nr, self.fs, self.fr = sems
        self.count, self.rows = self.total.shape[:2]

    def local(self, i):
        q = self.p.c if i == 0 else self.p.far
        return pltpu.make_async_copy(self.source(q), self.own.at[i], self.ls.at[i])

    def to_near(self, i):
        q = self.p.near if i == 0 else self.p.other
        return rcopy(
            self.source(q), self.got.at[i], self.ns.at[i], self.nr.at[i], {"ctx": self.p.near}
        )

    def to_far(self, j):
        return rcopy(
            self.own.at[1, j], self.away.at[j], self.fs.at[j], self.fr.at[j], {"ctx": self.p.far}
        )

    def start(self):
        for i in (1, 0):
            self.to_near(i).start()
            self.local(i).start()

    def send(self):
        self.local(1).wait()
        self.to_near(1).wait_recv()
        for j in range(self.count):
            own = self.own.at[1, j]
            add_blocks(own, [own, self.got.at[1, j]], bf16, self.rows)
            self.to_far(j).start()

    def mine(self):
        self.local(0).wait()
        self.to_near(0).wait_recv()

    def block(self, j):
        self.to_far(j).wait_recv()
        add_blocks(
            self.total.at[j],
            [self.own.at[0, j], self.got.at[0, j], self.away.at[j]],
            bf16,
            self.rows,
        )

    def finish(self):
        for i in range(2):
            self.to_near(i).wait_send()
        for j in range(self.count):
            self.to_far(j).wait_send()


def halve_scratch(count, rows, cols, total=True):
    return [
        pltpu.VMEM((2, count, rows, cols), bf16),
        pltpu.VMEM((2, count, rows, cols), bf16),
        pltpu.VMEM((count, rows, cols), bf16),
    ] + [pltpu.VMEM((count, rows, cols), bf16)] * total + [
        DMA((2,)),
        DMA((2,)),
        DMA((2,)),
        DMA((count,)),
        DMA((count,)),
    ]


def halve_job(x, columns=True):
    n, rows, cols = x.shape
    shape = (n, rows, cols // 4) if columns else (n // 4, rows, cols)

    def run(p, ins, outs, scratch):
        (x_ref,), (o_ref,) = ins, outs

        def source(q):
            if columns:
                return x_ref.at[:, :, column_block(q, shape[2])]
            return x_ref.at[pl.ds(q * shape[0], shape[0])]

        halve = Halve(p, source, list(scratch[:3]) + [o_ref], scratch[3:])
        halve.start()
        yield
        halve.send()
        yield
        halve.mine()
        for j in range(shape[0]):
            halve.block(j)
            if j % 2 == 1:
                yield
        halve.finish()

    return Job(run, [(x, ANY)], [(like(shape, bf16), VM)], halve_scratch(*shape, total=False))


def home_job(wgrad, size):
    _, depth, total = wgrad.shape
    quarter = total // 4

    def run(p, ins, outs, scratch):
        (w_ref,), (h_ref,) = ins, outs
        halve = Halve(
            p, lambda q: w_ref.at[:, :, column_block(q, quarter)], scratch[:4], scratch[4:9]
        )
        lsem, ws, wr = scratch[9:12]

        def view(d, q):
            return h_ref.at[lax.rem(p.f - d + size, size), :, column_block(q, quarter)]

        def local():
            return pltpu.make_async_copy(halve.total.at[p.f], view(0, p.c), lsem)

        def move(d):
            to = lax.rem(p.f + d, size)
            return rcopy(halve.total.at[to], view(0, p.c), ws.at[d], wr.at[d], {"fsdp": to})

        def came(d):
            ref = view(d, p.c)
            rcopy(ref, ref, ws.at[d], wr.at[d], {"fsdp": lax.rem(p.f + d, size)}).wait_recv()

        share = Share(p, view, size, scratch[12:])
        halve.start()
        yield
        halve.send()
        yield
        halve.mine()
        for j in range(size):
            halve.block(j)
            if j % 2 == 1:
                yield
        local().start()
        for d in range(1, size):
            move(d).start()
        yield
        local().wait()
        share.send(0)
        for d in range(1, size):
            came(d)
            share.send(d)
            if d % 2 == 0:
                yield
        for d in range(size):
            share.forward(d)
            if d % 4 == 3:
                yield
        share.finish()
        halve.finish()
        for d in range(1, size):
            move(d).wait_send()

    return Job(
        run,
        [(wgrad, ANY)],
        [(like((size, depth, total), bf16), ANY)],
        halve_scratch(size, depth, quarter)
        + [DMA, DMA((size,)), DMA((size,))]
        + share_sems(size),
    )


def ctx_sum_job(x):
    rows, cols = x.shape[0] // 4, x.shape[1]
    x = x.reshape(4, rows, cols)

    def run(p, ins, outs, scratch):
        (x_ref,), (o_ref,) = ins, outs
        halve = Halve(p, lambda q: x_ref.at[pl.ds(q, 1)], scratch[:4], scratch[4:9])
        share = Share(p, lambda d, q: o_ref.at[q], 1, scratch[10:])
        halve.start()
        yield
        halve.send()
        yield
        halve.mine()
        halve.block(0)
        local = pltpu.make_async_copy(halve.total.at[0], o_ref.at[p.c], scratch[9])
        local.start()
        local.wait()
        share.send(0)
        yield
        share.forward(0)
        yield
        share.finish()
        halve.finish()

    return Job(
        run,
        [(x, ANY)],
        [(like((4, rows, cols), bf16), ANY)],
        halve_scratch(1, rows, cols) + [DMA] + share_sems(1),
    )


def sum_job(partial, size):
    rows, tokens = partial.shape[0], partial.shape[1] // size

    def run(p, ins, outs, scratch):
        (p_ref,), (o_ref,) = ins, outs
        buf, ss, rs, gs, gr = scratch

        def at(i):
            return pl.ds(pl.multiple_of(i * tokens, 128), tokens)

        def first(d):
            to = lax.rem(p.f + d, size)
            return rcopy(p_ref.at[:, at(to)], buf.at[d], ss.at[d], rs.at[d], {"fsdp": to})

        def second(d):
            to = lax.rem(p.f + d, size)
            ref = o_ref.at[:, at(p.f)]
            return rcopy(ref, ref, gs.at[d], gr.at[d], {"fsdp": to})

        def came(d):
            ref = o_ref.at[:, at(lax.rem(p.f - d + size, size))]
            rcopy(ref, ref, gs.at[d], gr.at[d], {"fsdp": lax.rem(p.f + d, size)}).wait_recv()

        for d in range(1, size):
            first(d).start()
        yield
        total = p_ref[:, at(p.f)].astype(f32)
        for d in range(1, size):
            first(d).wait_recv()
            total += buf[d].astype(f32)
        o_ref[:, at(p.f)] = total.astype(bf16)
        for d in range(1, size):
            second(d).start()
        yield
        for d in range(1, size):
            came(d)
        for d in range(1, size):
            first(d).wait_send()
            second(d).wait_send()

    return Job(
        run,
        [(partial, VM)],
        [(like(partial.shape, bf16), VM)],
        [pltpu.VMEM((size, rows, tokens), bf16)] + [DMA((size,))] * 4,
    )


def all_sum_job(x, size):
    rows, cols = x.shape[1:]

    def run(p, ins, outs, scratch):
        (x_ref,), (o_ref,) = ins, outs
        buf, mid, far, ss, rs, ts, tr = scratch

        def copy(d):
            to = lax.rem(p.f + d, size)
            return rcopy(x_ref.at[to], buf.at[d], ss.at[d], rs.at[d], {"fsdp": to})

        def swap(i, to):
            return rcopy(mid.at[i], far.at[i], ts.at[i], tr.at[i], {"ctx": to})

        for d in range(1, size):
            copy(d).start()
        yield
        total = x_ref[p.f].astype(f32)
        for d in range(1, size):
            copy(d).wait_recv()
            total += buf[d].astype(f32)
        mid[0] = total.astype(bf16)
        swap(0, p.near).start()
        yield
        swap(0, p.near).wait_recv()
        mid[1] = (mid[0].astype(f32) + far[0].astype(f32)).astype(bf16)
        swap(1, p.far).start()
        yield
        swap(1, p.far).wait_recv()
        o_ref[...] = mid[1].astype(f32) + far[1].astype(f32)
        for d in range(1, size):
            copy(d).wait_send()
        swap(0, p.near).wait_send()
        swap(1, p.far).wait_send()

    return Job(
        run,
        [(x, VM)],
        [(like((rows, cols), f32), VM)],
        [pltpu.VMEM((size, rows, cols), bf16)]
        + [pltpu.VMEM((2, rows, cols), bf16)] * 2
        + [DMA((size,)), DMA((size,)), DMA((2,)), DMA((2,))],
    )


def column_grads(x, dy):
    return jnp.einsum("ld,lk->dk", x, dy, preferred_element_type=f32).astype(bf16)


def on_device(
    layer_in,
    out_grad,
    doc_lengths,
    block_deal,
    norm_gains,
    query_weight,
    keyval_weight,
    attn_proj,
    mamba_in,
    conv_taps,
    conv_bias,
    step_bias,
    skip_gain,
    decay_log,
    select_proj,
    step_proj,
    mamba_proj,
    gate_weight,
    up_weight,
    down_weight,
):
    size = lax.axis_size("fsdp")
    n_ctx = lax.axis_size("ctx")
    rows = layer_in.shape[1]
    half_rows = rows // 2
    width = layer_in.shape[2]
    blocks_all = 2 * n_ctx
    group = H // KV
    chan = INNER // size
    q_cols, kv_cols = H * HD // size, 2 * KV * HD // size
    ff_cols = gate_weight.shape[1] // size
    rows_all = size * rows
    ctx_place = lax.axis_index("ctx")
    deal_flat = block_deal.reshape(-1)
    my_blocks = lax.dynamic_slice_in_dim(block_deal, ctx_place, 1, 0)[0]
    offsets = jnp.arange(half_rows, dtype=jnp.int32)
    my_places = (my_blocks[:, None] * half_rows + offsets[None, :]).reshape(-1)
    key_places = (deal_flat[:, None] * half_rows + offsets[None, :]).reshape(-1)
    lengths = doc_lengths[0]
    starts = jnp.cumsum(lengths) - lengths

    def segment(places):
        return jnp.sum((places[:, None] >= starts[None, :]).astype(jnp.int32), axis=1)

    allowed = (key_places[None, :] <= my_places[:, None]) & (
        segment(key_places)[None, :] == segment(my_places)[:, None]
    )
    inverse = jnp.argsort(deal_flat)

    depth = query_weight.shape[0]
    chan_up, q_up, kv_up = up_to(chan, 128), up_to(q_cols, 128), up_to(kv_cols, 128)
    ff_up = up_to(ff_cols, 128)
    first_cuts = ((0, 0, q_cols), (1, 0, kv_cols), (2, 0, chan), (2, INNER, chan))
    first_at = (0, q_up, q_up + kv_up, q_up + kv_up + chan_up)
    first_total = up_to(q_up + kv_up + 2 * chan_up, 128 * n_ctx)
    ffn_cuts = ((0, 0, ff_cols), (1, 0, ff_cols))
    ffn_at = (0, ff_up)
    ffn_total = up_to(2 * ff_up, 128 * n_ctx)
    first_packed = pack_columns(
        (query_weight, keyval_weight, mamba_in), first_cuts, first_at, first_total, size
    )
    ffn_packed = pack_columns((gate_weight, up_weight), ffn_cuts, ffn_at, ffn_total, size)
    (stream_all,), (gain_all,), (first_mat,) = together(
        [gather_job(layer_in[0], size), spread_job(norm_gains, size), move_job(first_packed, size)],
        size,
        0,
        "start",
    )
    gain_float = jnp.moveaxis(gain_all, 0, 1).reshape(4, width).astype(f32)
    first_mat = first_mat.reshape(width, first_total)
    qkv_up = q_up + kv_up
    qkv_mat = first_mat[:, :qkv_up]
    entry_mat = first_mat[:, qkv_up : qkv_up + 2 * chan_up]
    ffn_quarter = ffn_total // n_ctx
    attn_wide = up_to(width, 128 * n_ctx)
    attn_packed = jnp.pad(attn_proj, ((0, 0), (0, attn_wide - width)))
    down_mat = jnp.pad(down_weight, ((0, ff_up - ff_cols), (0, 0)))
    more = chan_up - chan
    taps_mat = jnp.pad(conv_taps, ((0, 0), (0, more)))
    mamba_mat = jnp.pad(mamba_proj, ((0, more), (0, 0)))
    select_mat = jnp.pad(select_proj, ((0, more), (0, 0)))
    step_mat = jnp.pad(step_proj, ((0, 0), (0, more)))
    rate = -jnp.exp(jnp.pad(decay_log, ((0, 0), (0, more))).astype(f32))
    rate2 = rate * 1.4426950408889634
    shift_float, step_shift, skip_float = (
        jnp.pad(item, (0, more)).astype(f32) for item in (conv_bias, step_bias, skip_gain)
    )

    stream = layer_in[0].astype(f32)
    _, inv_in = norm_forward(stream, gain_float[0])
    normed_all, inv_all = norm_forward(stream_all.astype(f32), gain_float[0])
    normed_all = normed_all.astype(bf16)

    qkv = jnp.dot(normed_all, qkv_mat, preferred_element_type=f32).astype(bf16)
    ((qkv,),) = together([exchange_job(qkv.reshape(size, rows, -1), size)], size, 1, "qkv")
    queries = qkv[:, :, :q_cols].transpose(1, 0, 2).reshape(rows, H * HD)
    keyvals = qkv[:, :, q_up : q_up + kv_cols].transpose(1, 0, 2).reshape(rows, 2 * KV * HD)
    entry = jnp.dot(normed_all, entry_mat, preferred_element_type=f32)
    chan = chan_up
    mixer_in = entry[:, :chan].astype(bf16)
    gate_side = entry[:, chan:]
    mixer_blocks = mixer_in.reshape(size, 2, half_rows, chan)
    tails = mixer_blocks[:, :, half_rows - (CONV - 1) :]
    (keyvals_all,), (tails_all,) = together(
        [ctx_gather_job(keyvals), ctx_gather_job(tails.reshape(-1, chan))], size, 2, "edges"
    )
    keyvals_all = keyvals_all.reshape(n_ctx * rows, 2 * KV * HD)
    tails_all = tails_all.reshape(n_ctx, size, 2, CONV - 1, chan)

    def in_deal_order(values):
        return jnp.moveaxis(values, 2, 1).reshape((blocks_all,) + (size,) + values.shape[3:])

    def of_blocks(values, index):
        return jnp.moveaxis(jnp.take(values, index, axis=0), 0, 1)

    before_index = inverse[jnp.maximum(my_blocks - 1, 0)]
    has_before = my_blocks > 0
    prior_tail = jnp.where(
        has_before[None, :, None, None],
        of_blocks(in_deal_order(tails_all), before_index),
        jnp.zeros_like(tails),
    )
    padded = jnp.concatenate([prior_tail, mixer_blocks], axis=2).astype(f32)
    taps_float = taps_mat.astype(f32)
    conv_blocks_out = shift_float + sum(
        taps_float[offset] * padded[:, :, offset : offset + half_rows] for offset in range(CONV)
    )
    conv_out = conv_blocks_out.reshape(rows_all, chan)
    signal = jax.nn.silu(conv_out).astype(bf16)
    signal_float = signal.astype(f32)
    selected_part = jnp.einsum(
        "ik,li->kl", select_mat, signal, preferred_element_type=f32
    ).astype(bf16)
    ((selected,),) = together([sum_job(selected_part, size)], size, 3, "select")
    step_low = selected[:RANK].T
    write_read = selected[RANK:].astype(f32).T.reshape(size, 2, half_rows, 2 * NS)
    step_pre = jnp.dot(step_low, step_mat, preferred_element_type=f32) + step_shift
    step_sizes = jax.nn.softplus(step_pre)
    block_steps = step_sizes.reshape(size, 2, half_rows, chan)
    block_inputs = signal_float.reshape(size, 2, half_rows, chan)
    order = jnp.concatenate([inverse, my_blocks]).astype(jnp.int32)
    local_end = scan_ends(block_steps, block_inputs, write_read, rate2)
    (ends_all,), (grads_all,), (ffn_mat,), (attn_mat,) = together(
        [
            ctx_gather_job(local_end.reshape(-1, chan)),
            gather_job(out_grad[0], size),
            move_job(ffn_packed, size),
            move_job(attn_packed, size, False),
        ],
        size,
        4,
        "ends",
    )
    ffn_mat = ffn_mat.reshape(width, ffn_total)
    gate_mat, up_mat = ffn_mat[:, :ff_up], ffn_mat[:, ff_up : 2 * ff_up]
    attn_mat = attn_mat.reshape(width, attn_wide)[:, :width]
    ends_all = ends_all.reshape(blocks_all, NS + 1, size, chan)
    scan_blocks, start_state = scan_forward(
        order, block_steps, block_inputs, write_read, rate2, ends_all
    )
    scanned = scan_blocks.reshape(rows_all, chan) + skip_float * signal_float
    gate_act = jax.nn.silu(gate_side)
    mamba_rows = (scanned * gate_act).astype(bf16)
    mamba_part = jnp.dot(mamba_rows, mamba_mat, preferred_element_type=f32).astype(bf16)
    ((mamba_out,),) = together(
        [scatter_job(mamba_part.reshape(size, rows, width), size)], size, 5, "mamba_sum"
    )
    query_groups = queries.reshape(rows, KV, group, HD).transpose(1, 0, 2, 3)
    key_groups = keyvals_all[:, : KV * HD].reshape(-1, KV, HD).transpose(1, 0, 2)
    value_groups = keyvals_all[:, KV * HD :].reshape(-1, KV, HD).transpose(1, 0, 2)

    def attend(parts):
        query_part, key_part, value_part = parts
        scores = (
            jnp.einsum("lgd,sd->gls", query_part, key_part, preferred_element_type=f32)
            * score_scale
        )
        scores = jnp.where(allowed[None], scores, -1e30)
        largest = jnp.max(scores, axis=-1, keepdims=True)
        expo = jnp.exp(scores - largest)
        total = jnp.sum(expo, axis=-1, keepdims=True)
        probs = (expo / total).astype(bf16)
        output = jnp.einsum("gls,sd->lgd", probs, value_part, preferred_element_type=f32)
        return (output, largest + jnp.log(total))

    attn_groups, log_totals = lax.map(attend, (query_groups, key_groups, value_groups))
    attn_rows = attn_groups.transpose(1, 0, 2, 3).reshape(rows, H * HD).astype(bf16)
    attn_out = jnp.dot(attn_rows, attn_mat, preferred_element_type=f32)
    attn_normed, inv_attn = norm_forward(attn_out, gain_float[1])

    mamba_normed, inv_mamba = norm_forward(mamba_out, gain_float[2])
    middle = stream + 0.5 * (attn_normed + mamba_normed)
    ffn_normed, inv_ffn = norm_forward(middle, gain_float[3])
    ((ffn_low,),) = together(
        [gather_job(ffn_normed.astype(bf16), size)], size, 6, "ffn_rows"
    )
    gate_pre = jnp.dot(ffn_low, gate_mat, preferred_element_type=f32)
    up_pre = jnp.dot(ffn_low, up_mat, preferred_element_type=f32)
    hidden = (jax.nn.silu(gate_pre) * up_pre).astype(bf16)
    down_part = jnp.dot(hidden, down_mat, preferred_element_type=f32).astype(bf16)
    down_wgrad = jnp.einsum("lf,ld->fd", hidden, grads_all, preferred_element_type=f32)
    hidden_back = jnp.einsum("ld,fd->lf", grads_all, down_mat, preferred_element_type=f32)
    gate_back = (hidden_back * up_pre * silu_slope(gate_pre)).astype(bf16)
    up_back = (hidden_back * jax.nn.silu(gate_pre)).astype(bf16)
    ffn_wgrad = column_grads(ffn_low, jnp.concatenate([gate_back, up_back], axis=1))
    ffn_back_part = jnp.einsum(
        "lf,df->ld", gate_back, gate_mat, preferred_element_type=f32
    ) + jnp.einsum("lf,df->ld", up_back, up_mat, preferred_element_type=f32)
    (ffn_back,), (ffn_home,) = together(
        [
            scatter_job(ffn_back_part.astype(bf16).reshape(size, rows, width), size),
            home_job(ffn_wgrad.reshape(size, depth, -1), size),
        ],
        size,
        7,
        "ffn_sum",
    )
    middle_part, ffn_gain_grad = norm_backward(ffn_back, middle, inv_ffn, gain_float[3])
    middle_back = out_grad[0].astype(f32) + middle_part
    branch_back = 0.5 * middle_back
    attn_part, attn_gain_grad = norm_backward(branch_back, attn_out, inv_attn, gain_float[1])
    mamba_part_back, mamba_gain_grad = norm_backward(
        branch_back, mamba_out, inv_mamba, gain_float[2]
    )
    attn_back = attn_part.astype(bf16)
    attn_wgrad = jnp.einsum("lh,ld->hd", attn_rows, attn_back, preferred_element_type=f32)
    attn_wgrad = jnp.pad(attn_wgrad.astype(bf16), ((0, 0), (0, attn_wide - width)))
    (mamba_back,), (down_out,), (down_share,), (attn_quarter,) = together(
        [
            gather_job(mamba_part_back.astype(bf16), size),
            scatter_job(down_part.reshape(size, rows, width), size),
            ctx_sum_job(down_wgrad.astype(bf16)),
            halve_job(attn_wgrad.reshape(size, depth, attn_wide)),
        ],
        size,
        8,
        "mamba_rows",
    )
    result = middle + down_out
    rows_back = jnp.einsum("ld,hd->lh", attn_back, attn_mat, preferred_element_type=f32).astype(
        bf16
    )
    mamba_wgrad = jnp.einsum("li,ld->id", mamba_rows, mamba_back, preferred_element_type=f32)
    mrows_back = jnp.einsum("ld,id->li", mamba_back, mamba_mat, preferred_element_type=f32)
    scan_back = mrows_back * gate_act
    side_back = mrows_back * scanned * silu_slope(gate_side)
    skip_grad = jnp.sum(scan_back * signal_float, axis=0)
    block_dout = scan_back.reshape(size, 2, half_rows, chan)
    local_back = scan_backs(block_steps, block_dout, write_read, rate2)
    (backs_all,), (attn_piece,), (mamba_share,) = together(
        [
            ctx_gather_job(local_back.reshape(-1, chan)),
            scatter_job(attn_quarter, size),
            ctx_sum_job(mamba_wgrad.astype(bf16)),
        ],
        size,
        9,
        "backs",
    )
    backs_all = backs_all.reshape(blocks_all, NS, size, chan)
    step_back, carry_writes, read_write_back, decay_sums = scan_backward(
        order, block_steps, block_inputs, block_dout, write_read, rate2, start_state, ends_all, backs_all
    )
    decay_grad = rate * jnp.sum(decay_sums, axis=(0, 2))
    step_back = step_back.reshape(rows_all, chan)
    signal_back = scan_back * skip_float + step_sizes * carry_writes.reshape(rows_all, chan)
    read_write_back = read_write_back.reshape(rows_all, 128)[:, : 2 * NS]
    pre_back = (step_back * jax.nn.sigmoid(step_pre)).astype(bf16)
    step_wgrad = jnp.einsum("lr,li->ri", step_low, pre_back, preferred_element_type=f32)
    bias_grad = jnp.sum(pre_back.astype(f32), axis=0)
    rank_back = jnp.einsum("li,ri->lr", pre_back, step_mat, preferred_element_type=f32)
    select_part = jnp.concatenate([rank_back, read_write_back], axis=1).astype(bf16).T
    (select_back,), (attn_home,) = together(
        [sum_job(select_part, size), ctx_gather_job(attn_piece.astype(bf16))],
        size,
        10,
        "select_back",
    )
    select_back = select_back.T
    select_wgrad = jnp.einsum("li,lk->ik", signal, select_back, preferred_element_type=f32)
    signal_back = signal_back + jnp.einsum(
        "lk,ik->li", select_back, select_mat, preferred_element_type=f32
    )
    conv_back = signal_back * silu_slope(conv_out)
    conv_blocks = conv_back.reshape(size, 2, half_rows, chan)
    taps_grad = jnp.stack(
        [
            jnp.sum(conv_blocks * padded[:, :, offset : offset + half_rows], axis=(0, 1, 2))
            for offset in range(CONV)
        ]
    )
    shift_grad = jnp.sum(conv_back, axis=0)
    padded_back = sum(
        (
            jnp.pad(
                taps_float[offset] * conv_blocks,
                ((0, 0), (0, 0), (offset, CONV - 1 - offset), (0, 0)),
            )
            for offset in range(CONV)
        )
    )
    tail_back = jnp.where(has_before[None, :, None, None], padded_back[:, :, : CONV - 1], 0.0)
    dout_groups = rows_back.reshape(rows, KV, group, HD).transpose(1, 0, 2, 3)

    def attend_back(parts):
        query_part, key_part, value_part, dout_part, log_part = parts
        scores = (
            jnp.einsum("lgd,sd->gls", query_part, key_part, preferred_element_type=f32)
            * score_scale
        )
        scores = jnp.where(allowed[None], scores, -1e30)
        probs = jnp.exp(scores - log_part)
        value_grad = jnp.einsum(
            "gls,lgd->sd", probs.astype(bf16), dout_part, preferred_element_type=f32
        )
        prob_grad = jnp.einsum("lgd,sd->gls", dout_part, value_part, preferred_element_type=f32)
        centre = jnp.sum(probs * prob_grad, axis=-1, keepdims=True)
        score_grad = (probs * (prob_grad - centre)).astype(bf16)
        query_grad = (
            jnp.einsum("gls,sd->lgd", score_grad, key_part, preferred_element_type=f32)
            * score_scale
        )
        key_grad = (
            jnp.einsum("gls,lgd->sd", score_grad, query_part, preferred_element_type=f32)
            * score_scale
        )
        return (query_grad, key_grad, value_grad)

    query_grads, key_grads, value_grads = lax.map(
        attend_back, (query_groups, key_groups, value_groups, dout_groups, log_totals)
    )
    keyval_terms = jnp.concatenate(
        [
            key_grads.transpose(1, 0, 2).reshape(-1, KV * HD),
            value_grads.transpose(1, 0, 2).reshape(-1, KV * HD),
        ],
        axis=1,
    )
    (tails_back_all,), (keyval_back,) = together(
        [
            ctx_gather_job(tail_back.astype(bf16).reshape(-1, chan)),
            halve_job(keyval_terms.astype(bf16).reshape(n_ctx, rows, 2 * KV * HD), False),
        ],
        size,
        11,
        "edges_back",
    )
    keyval_back = keyval_back[0]
    query_back = query_grads.transpose(1, 0, 2, 3).reshape(rows, H * HD).astype(bf16)
    qkv_back = jnp.concatenate(
        [
            jnp.pad(query_back.reshape(rows, size, q_cols), ((0, 0), (0, 0), (0, q_up - q_cols))),
            jnp.pad(
                keyval_back.reshape(rows, size, kv_cols), ((0, 0), (0, 0), (0, kv_up - kv_cols))
            ),
        ],
        axis=2,
    ).transpose(1, 0, 2)
    tails_back_all = in_deal_order(tails_back_all.reshape(n_ctx, size, 2, CONV - 1, chan))
    after_index = inverse[jnp.minimum(my_blocks + 1, blocks_all - 1)]
    has_after = my_blocks < blocks_all - 1
    incoming = jnp.where(
        has_after[None, :, None, None], of_blocks(tails_back_all, after_index).astype(f32), 0.0
    )
    mixer_back = padded_back[:, :, CONV - 1 :] + jnp.pad(
        incoming, ((0, 0), (0, 0), (half_rows - (CONV - 1), 0), (0, 0))
    )
    entry_back = jnp.concatenate([mixer_back.reshape(rows_all, chan), side_back], axis=1).astype(
        bf16
    )
    input_part = jnp.einsum("lk,dk->ld", entry_back, entry_mat, preferred_element_type=f32)

    ((qkv_back,),) = together([exchange_job(qkv_back, size)], size, 12, "qkv_back")
    qkv_back = qkv_back.reshape(rows_all, -1)
    first_back = [qkv_back, entry_back]
    if first_total > qkv_up + 2 * chan_up:
        first_back.append(jnp.zeros((rows_all, first_total - qkv_up - 2 * chan_up), bf16))
    first_wgrad = column_grads(normed_all, jnp.concatenate(first_back, axis=1))
    input_part = input_part + jnp.einsum(
        "lk,dk->ld", qkv_back, qkv_mat, preferred_element_type=f32
    )
    low_part = input_part.astype(bf16)
    normed_float = stream_all.astype(f32) * inv_all
    in_gain_grad = jnp.sum(low_part.astype(f32) * normed_float, axis=0)
    gain_grad = jnp.stack([in_gain_grad, attn_gain_grad, mamba_gain_grad, ffn_gain_grad])
    gain_parts = jnp.moveaxis(gain_grad.reshape(4, size, -1), 1, 0).astype(bf16)
    small = jnp.concatenate(
        [
            taps_grad,
            shift_grad[None],
            bias_grad[None],
            skip_grad[None],
            decay_grad,
            step_wgrad,
            select_wgrad.T,
        ]
    )
    n_small = small.shape[0]
    small = jnp.pad(small, ((0, up_to(n_small, 64) - n_small), (0, 0))).astype(bf16)
    (input_back,), (first_home,), (small,), (gain_share,) = together(
        [
            scatter_job(low_part.reshape(size, rows, width), size),
            home_job(first_wgrad.reshape(size, depth, first_total), size),
            ctx_sum_job(small),
            all_sum_job(gain_parts, size),
        ],
        size,
        13,
        "finish",
    )
    stream_part, _ = norm_backward(input_back, stream, inv_in, gain_float[0])
    stream_back = middle_back + stream_part
    gate_share, up_share = unpack_columns(
        ffn_home[None], ffn_cuts, ffn_at, (gate_weight.shape, up_weight.shape), ffn_total
    )
    query_share, keyval_share, entry_share = unpack_columns(
        first_home[None],
        first_cuts,
        first_at,
        (query_weight.shape, keyval_weight.shape, mamba_in.shape),
        first_total,
    )
    chan = conv_bias.shape[0]
    vectors = small.reshape(-1, chan_up)[:, :chan].astype(f32)
    attn_share = jnp.moveaxis(attn_home, 0, 1).reshape(depth, attn_wide)[:, :width].astype(f32)
    mamba_share = mamba_share.reshape(-1, width)[:chan].astype(f32)
    down_share = down_share.reshape(-1, width)[:ff_cols].astype(f32)
    return (
        result.astype(bf16)[None],
        stream_back[None],
        gain_share,
        query_share,
        keyval_share,
        attn_share,
        entry_share,
        vectors[:CONV],
        vectors[CONV],
        vectors[CONV + 1],
        vectors[CONV + 2],
        vectors[CONV + 3 : CONV + 3 + NS],
        vectors[CONV + 3 + NS + RANK : n_small].T,
        vectors[CONV + 3 + NS : CONV + 3 + NS + RANK],
        mamba_share,
        gate_share,
        up_share,
        down_share,
    )


def solution(mesh):
    in_specs = (
        P("fsdp", "ctx", None),
        P("fsdp", "ctx", None),
        P("fsdp", None),
        P(),
        P(None, "fsdp"),
        P("fsdp", None),
        P("fsdp", None),
        P("fsdp", None),
        P("fsdp", None),
        P(None, "fsdp"),
        P("fsdp"),
        P("fsdp"),
        P("fsdp"),
        P(None, "fsdp"),
        P("fsdp", None),
        P(None, "fsdp"),
        P("fsdp", None),
        P("fsdp", None),
        P("fsdp", None),
        P("fsdp", None),
    )
    out_specs = (
        P("fsdp", "ctx", None),
        P("fsdp", "ctx", None),
        P(None, "fsdp"),
        P("fsdp", None),
        P("fsdp", None),
        P("fsdp", None),
        P("fsdp", None),
        P(None, "fsdp"),
        P("fsdp"),
        P("fsdp"),
        P("fsdp"),
        P(None, "fsdp"),
        P("fsdp", None),
        P(None, "fsdp"),
        P("fsdp", None),
        P("fsdp", None),
        P("fsdp", None),
        P("fsdp", None),
    )
    return jax.shard_map(
        on_device, mesh=mesh, in_specs=in_specs, out_specs=out_specs, check_vma=False
    )
```

```python
import functools
import math

import jax
import jax.numpy as jnp
from jax import lax
from jax.experimental import pallas as pl
from jax.experimental.pallas import tpu as pltpu
from jax.sharding import PartitionSpec as P

H = 25
KV = 5
HD = 64
INNER = 3200
NS = 16
RANK = 100
CONV = 4

EPS = 1e-06
score_scale = 0.125
MESH = pl.DeviceIdType.MESH
ANY = pl.BlockSpec(memory_space=pl.ANY)
VM = pl.BlockSpec(memory_space=pltpu.VMEM)
DMA = pltpu.SemaphoreType.DMA
f32 = jnp.float32
bf16 = jnp.bfloat16


def params(cid, vmem=None):
    return pltpu.CompilerParams(collective_id=cid, has_side_effects=True, vmem_limit_bytes=vmem)


def rcopy(src, dst, ssem, rsem, dev):
    return pltpu.make_async_remote_copy(
        src_ref=src, dst_ref=dst, send_sem=ssem, recv_sem=rsem, device_id=dev, device_id_type=MESH
    )


def norm_forward(values, gain):
    inverse = lax.rsqrt(jnp.mean(values * values, axis=-1, keepdims=True) + EPS)
    return (values * inverse * gain, inverse)


def norm_backward(grad, values, inverse, gain):
    normed = values * inverse
    gain_grad = jnp.sum(grad * normed, axis=0)
    scaled = grad * gain
    return (
        inverse * (scaled - normed * jnp.mean(scaled * normed, axis=-1, keepdims=True)),
        gain_grad,
    )


def silu_slope(values):
    sigma = jax.nn.sigmoid(values)
    return sigma * (1.0 + values * (1.0 - sigma))


def up_to(value, step):
    return (value + step - 1) // step * step


def pack_columns(refs, out, cuts, offsets, size):
    out[...] = jnp.zeros_like(out)
    for (which, first, cols), at in zip(cuts, offsets):
        for f in range(size):
            out[f, :, at : at + cols] = refs[which][:, first + f * cols : first + (f + 1) * cols]


def unpack_pieces(home, outs, cuts, offsets, size):
    for (which, first, cols), at in zip(cuts, offsets):
        for f in range(size):
            outs[which][:, first + f * cols : first + (f + 1) * cols] = home[
                f, :, at : at + cols
            ].astype(f32)


def unpack_columns(home, cuts, offsets, shapes, size):
    def kernel(h_ref, *outs):
        unpack_pieces(h_ref, outs, cuts, offsets, size)

    return pl.pallas_call(
        kernel,
        out_shape=[jax.ShapeDtypeStruct(shape, f32) for shape in shapes],
        in_specs=[VM],
        out_specs=[VM] * len(shapes),
        compiler_params=pltpu.CompilerParams(vmem_limit_bytes=60 << 20),
        name="unpack_columns",
    )(home)


class Job:
    def __init__(self, steps, ins, outs, scratch):
        self.steps, self.ins, self.outs, self.scratch = steps, ins, outs, scratch


class Place:
    def __init__(self, size):
        self.size, self.lanes = size, size // 2
        self.f, self.c = lax.axis_index("fsdp"), lax.axis_index("ctx")
        self.a, self.b = self.f // 2, lax.rem(self.f, 2)
        self.near = self.c + 1 - 2 * lax.rem(self.c, 2)
        self.far = lax.rem(self.c + 2, 4)
        self.other = lax.rem(self.near + 2, 4)

    def greet(self):
        bar = pltpu.get_barrier_semaphore()
        for d in range(1, self.size):
            peer = {"fsdp": lax.rem(self.f + d, self.size)}
            pl.semaphore_signal(bar, inc=1, device_id=peer, device_id_type=MESH)
        for peer in (self.near, self.far):
            pl.semaphore_signal(bar, inc=1, device_id={"ctx": peer}, device_id_type=MESH)
        pl.semaphore_wait(bar, self.size + 1)


def part(ref_list, jobs, field):
    out = []
    for job in jobs:
        count = len(getattr(job, field))
        out.append(ref_list[:count])
        ref_list = ref_list[count:]
    return out


class Moving:
    def __init__(self, live):
        self.live = live

    def step(self, which):
        if which < len(self.live) and self.live[which] is not None:
            try:
                next(self.live[which])
            except StopIteration:
                self.live[which] = None

    def drain(self):
        while any(item is not None for item in self.live):
            for which in range(len(self.live)):
                self.step(which)


def together(jobs, size, cid, name, order=()):
    n_in = sum(len(job.ins) for job in jobs)
    n_out = sum(len(job.outs) for job in jobs)

    def kernel(*refs):
        place = Place(size)
        place.greet()
        ins = part(refs[:n_in], jobs, "ins")
        outs = part(refs[n_in : n_in + n_out], jobs, "outs")
        scratch = part(refs[n_in + n_out :], jobs, "scratch")
        moving = Moving(
            [job.steps(place, i, o, s) for job, i, o, s in zip(jobs, ins, outs, scratch)]
        )
        for which in order:
            moving.step(which)
        moving.drain()

    got = pl.pallas_call(
        kernel,
        out_shape=[shape for job in jobs for shape, _ in job.outs],
        in_specs=[spec for job in jobs for _, spec in job.ins],
        out_specs=[spec for job in jobs for _, spec in job.outs],
        scratch_shapes=[item for job in jobs for item in job.scratch],
        compiler_params=params(cid, 60 << 20),
        name=name,
    )(*[array for job in jobs for array, _ in job.ins])
    return part(got, jobs, "outs")


def like(shape, dtype):
    return jax.ShapeDtypeStruct(shape, dtype)


def gather_job(x, size, shared=False):
    rows, cols = x.shape
    lanes = size // 2

    def run(p, ins, outs, scratch):
        (x_ref,), (o_ref,) = ins, outs
        lsem, up_s, up_r, dn_s, dn_r, px_s, px_r = scratch[:7]

        def view(i, q):
            return o_ref.at[i, :, column_block(q, cols // 4)]

        def piece(origin, b):
            i = 2 * origin + b
            return view(i, p.c) if shared else o_ref.at[i]

        def own():
            return x_ref.at[:, column_block(p.c, cols // 4)] if shared else x_ref

        share = Share(p, view, size, scratch[7:]) if shared else None

        def local():
            return pltpu.make_async_copy(own(), piece(p.a, p.b), lsem)

        def up(s):
            src = own() if s == 0 else piece(p.a - s, p.b)
            dev = {"fsdp": 2 * (p.a + 1) + p.b}
            return rcopy(src, piece(p.a - s, p.b), up_s.at[s], up_r.at[s], dev)

        def down(s):
            src = own() if s == 0 else piece(p.a + s, p.b)
            dev = {"fsdp": 2 * (p.a - 1) + p.b}
            return rcopy(src, piece(p.a + s, p.b), dn_s.at[s], dn_r.at[s], dev)

        def across(origin, src=None):
            src = piece(origin, p.b) if src is None else src
            dev = {"fsdp": 2 * p.a + 1 - p.b}
            return rcopy(src, piece(origin, p.b), px_s.at[origin], px_r.at[origin], dev)

        def came(ref, sem, dev):
            rcopy(ref, ref, sem, sem, dev).wait_recv()

        def arrived(origin, b, src=None):
            if shared:
                share.send(2 * origin + b, src)

        local().start()

        @pl.when(p.a < lanes - 1)
        def _():
            up(0).start()

        @pl.when(p.a > 0)
        def _():
            down(0).start()

        across(p.a, own()).start()
        if shared:
            arrived(p.a, p.b, own())
        yield
        for s in range(lanes - 1):
            @pl.when(p.a - 1 - s >= 0)
            def _():
                came(piece(p.a - 1 - s, p.b), up_r.at[s], {"fsdp": 2 * (p.a - 1) + p.b})

                @pl.when(p.a < lanes - 1)
                def _():
                    up(s + 1).start()

                across(p.a - 1 - s).start()
                arrived(p.a - 1 - s, p.b)

            @pl.when(p.a + 1 + s <= lanes - 1)
            def _():
                came(piece(p.a + 1 + s, p.b), dn_r.at[s], {"fsdp": 2 * (p.a + 1) + p.b})

                @pl.when(p.a > 0)
                def _():
                    down(s + 1).start()

                across(p.a + 1 + s).start()
                arrived(p.a + 1 + s, p.b)

            yield
        local().wait()
        for origin in range(lanes):
            came(piece(origin, 1 - p.b), px_r.at[origin], {"fsdp": 2 * p.a + 1 - p.b})
            arrived(origin, 1 - p.b)
        if shared:
            yield
            for i in range(size):
                share.forward(i)
            yield
            share.finish()
        for s in range(lanes - 1):
            @pl.when((p.a - s >= 0) & (p.a < lanes - 1))
            def _():
                up(s).wait_send()

            @pl.when((p.a + s <= lanes - 1) & (p.a > 0))
            def _():
                down(s).wait_send()

        for origin in range(lanes):
            across(origin).wait_send()

    return Job(
        run,
        [(x, ANY)],
        [(like((size, rows, cols), x.dtype), ANY)],
        [DMA] + [DMA((lanes,))] * 6 + (share_sems(size) if shared else []),
    )


def add_blocks(out, terms, dtype, rows):
    if rows % 16:
        total = terms[0][...].astype(f32)
        for ref in terms[1:]:
            total += ref[...].astype(f32)
        out[...] = total.astype(dtype)
        return
    step = 32 if rows % 32 == 0 else 16

    def body(i, carry):
        at = pl.ds(pl.multiple_of(i * step, step), step)
        total = terms[0][at, :].astype(f32)
        for ref in terms[1:]:
            total += ref[at, :].astype(f32)
        out[at, :] = total.astype(dtype)
        return carry

    lax.fori_loop(0, rows // step, body, 0)


def scatter_job(partial, size, held=None):
    rows, cols = partial.shape[1:]
    lanes = size // 2

    def run(p, ins, outs, scratch):
        (o_ref,) = outs
        p_ref = held[0] if held is not None else ins[0]
        xbuf, upb, dnb, up_s, up_r, dn_s, dn_r, px_s, px_r = scratch[:9]

        def own(dest):
            return p_ref.at[2 * dest + p.b] if held is not None else scratch[9].at[dest]

        def local(dest):
            return pltpu.make_async_copy(
                p_ref.at[2 * dest + p.b], scratch[9].at[dest], scratch[10].at[dest]
            )

        def across(dest):
            src = p_ref.at[2 * dest + 1 - p.b]
            dev = {"fsdp": 2 * p.a + 1 - p.b}
            return rcopy(src, xbuf.at[dest], px_s.at[dest], px_r.at[dest], dev)

        def up(dest):
            dev = {"fsdp": 2 * (p.a + 1) + p.b}
            return rcopy(xbuf.at[dest], upb.at[dest], up_s.at[dest], up_r.at[dest], dev)

        def down(dest):
            dev = {"fsdp": 2 * (p.a - 1) + p.b}
            return rcopy(xbuf.at[dest], dnb.at[dest], dn_s.at[dest], dn_r.at[dest], dev)

        def add_in(dest, extra):
            terms = [xbuf.at[dest], own(dest)]
            if extra is not None:
                terms.append(extra.at[dest])
            add_blocks(xbuf.at[dest], terms, bf16, rows)

        if held is None:
            for dest in range(lanes):
                local(dest).start()
        for d in range(lanes - 1, -1, -1):
            @pl.when(p.a + d <= lanes - 1)
            def _():
                across(p.a + d).start()

            if d > 0:
                @pl.when(p.a - d >= 0)
                def _():
                    across(p.a - d).start()

        yield
        if held is None:
            for dest in range(lanes):
                local(dest).wait()
        for d in range(lanes - 1, 0, -1):
            @pl.when(p.a + d <= lanes - 1)
            def _():
                across(p.a + d).wait_recv()

                @pl.when(p.a > 0)
                def _():
                    up(p.a + d).wait_recv()
                    add_in(p.a + d, upb)

                @pl.when(p.a == 0)
                def _():
                    add_in(p.a + d, None)

                up(p.a + d).start()

            @pl.when(p.a - d >= 0)
            def _():
                across(p.a - d).wait_recv()

                @pl.when(p.a < lanes - 1)
                def _():
                    down(p.a - d).wait_recv()
                    add_in(p.a - d, dnb)

                @pl.when(p.a == lanes - 1)
                def _():
                    add_in(p.a - d, None)

                down(p.a - d).start()

            yield
        across(p.a).wait_recv()
        terms = [xbuf.at[p.a], own(p.a)]

        @pl.when(p.a == 0)
        def _():
            down(p.a).wait_recv()
            add_blocks(o_ref, terms + [dnb.at[p.a]], f32, rows)

        @pl.when(p.a == lanes - 1)
        def _():
            up(p.a).wait_recv()
            add_blocks(o_ref, terms + [upb.at[p.a]], f32, rows)

        @pl.when((p.a > 0) & (p.a < lanes - 1))
        def _():
            up(p.a).wait_recv()
            down(p.a).wait_recv()
            add_blocks(o_ref, terms + [upb.at[p.a], dnb.at[p.a]], f32, rows)

        for dest in range(lanes):
            across(dest).wait_send()

        for d in range(lanes - 1, 0, -1):
            @pl.when(p.a + d <= lanes - 1)
            def _():
                up(p.a + d).wait_send()

            @pl.when(p.a - d >= 0)
            def _():
                down(p.a - d).wait_send()

    return Job(
        run,
        [(partial, ANY)] if held is None else [],
        [(like((rows, cols), f32), VM)],
        [pltpu.VMEM((lanes, rows, cols), bf16)] * 3
        + [DMA((lanes,))] * 6
        + ([pltpu.VMEM((lanes, rows, cols), bf16), DMA((lanes,))] if held is None else []),
    )


def column_block(of, quarter):
    return pl.ds(pl.multiple_of(of * quarter, 128), quarter)


class Share:
    def __init__(self, p, view, count, sems):
        self.p, self.view, self.count = p, view, count
        self.fs, self.fr, self.ns, self.nr, self.hs, self.hr = sems

    def far(self, d, q, src=None):
        ref = self.view(d, q)
        src = ref if src is None else src
        return rcopy(src, ref, self.fs.at[d], self.fr.at[d], {"ctx": self.p.far})

    def near(self, d, q, src=None):
        ref = self.view(d, q)
        src = ref if src is None else src
        return rcopy(src, ref, self.ns.at[d], self.nr.at[d], {"ctx": self.p.near})

    def onward(self, d, q):
        ref = self.view(d, q)
        return rcopy(ref, ref, self.hs.at[d], self.hr.at[d], {"ctx": self.p.near})

    def send(self, d, src=None):
        self.far(d, self.p.c, src).start()
        self.near(d, self.p.c, src).start()

    def forward(self, d):
        self.far(d, self.p.far).wait_recv()
        self.onward(d, self.p.far).start()

    def finish(self):
        p = self.p
        for d in range(self.count):
            self.far(d, p.c).wait_send()
            self.near(d, p.c).wait_send()
            self.near(d, p.near).wait_recv()
            self.onward(d, p.far).wait_send()
            self.onward(d, p.other).wait_recv()


def share_sems(count):
    return [DMA((count,))] * 6


def move_job(packed, size, held=None):
    depth, total = packed.shape[-2:]
    quarter = total // 4

    def run(p, ins, outs, scratch):
        (w_ref,) = outs
        p_ref = held[0] if held is not None else ins[0]
        lsem, ws, wr = scratch[:3]

        def source(to):
            return p_ref.at[to, :, column_block(p.c, quarter)]

        def view(d, q):
            return w_ref.at[lax.rem(p.f - d + size, size), :, column_block(q, quarter)]

        def local():
            return pltpu.make_async_copy(source(p.f), view(0, p.c), lsem)

        def move(d):
            to = lax.rem(p.f + d, size)
            return rcopy(source(to), view(0, p.c), ws.at[d], wr.at[d], {"fsdp": to})

        def came(d):
            ref = view(d, p.c)
            rcopy(ref, ref, ws.at[d], wr.at[d], {"fsdp": lax.rem(p.f + d, size)}).wait_recv()

        share = Share(p, view, size, scratch[3:])
        local().start()
        for d in range(1, size):
            move(d).start()
        share.send(0, source(p.f))
        yield
        for d in range(1, size):
            came(d)
            share.send(d)
            if d % 2 == 0:
                yield
        for d in range(size):
            share.forward(d)
            if d % 4 == 3:
                yield
        local().wait()
        share.finish()
        for d in range(1, size):
            move(d).wait_send()

    return Job(
        run,
        [(packed, ANY)] if held is None else [],
        [(like((size, depth, total), packed.dtype), ANY)],
        [DMA, DMA((size,)), DMA((size,))] + share_sems(size),
    )


def spread_job(x, size):
    def run(p, ins, outs, scratch):
        (x_ref,), (o_ref,) = ins, outs
        lsem, ss, rs = scratch

        def copy(d):
            to = {"fsdp": lax.rem(p.f + d, size)}
            return rcopy(x_ref, o_ref.at[p.f], ss.at[d], rs.at[d], to)

        def local():
            return pltpu.make_async_copy(x_ref, o_ref.at[p.f], lsem)

        local().start()
        for d in range(1, size):
            copy(d).start()
        yield
        local().wait()
        for d in range(1, size):
            copy(d).wait()

    return Job(
        run,
        [(x, ANY)],
        [(like((size,) + x.shape, x.dtype), ANY)],
        [DMA, DMA((size,)), DMA((size,))],
    )


def exchange_job(x, size, rows=None):
    blocks = x.shape if rows is None else (size, rows, x.shape[1] // size)

    def run(p, ins, outs, scratch):
        (x_ref,), (o_ref,) = ins, outs
        lsem, ss, rs = scratch

        def block(to):
            if rows is None:
                return x_ref.at[to]
            return x_ref.at[:rows, column_block(to, blocks[2])]

        def copy(d):
            to = lax.rem(p.f + d, size)
            return rcopy(block(to), o_ref.at[p.f], ss.at[d], rs.at[d], {"fsdp": to})

        def local():
            return pltpu.make_async_copy(block(p.f), o_ref.at[p.f], lsem)

        local().start()
        for d in range(1, size):
            copy(d).start()
        yield
        local().wait()
        for d in range(1, size):
            copy(d).wait()

    return Job(
        run, [(x, ANY)], [(like(blocks, x.dtype), ANY)], [DMA, DMA((size,)), DMA((size,))]
    )


def ctx_gather_job(x):
    def run(p, ins, outs, scratch):
        (x_ref,), (o_ref,) = ins, outs
        share = Share(p, lambda d, q: o_ref.at[q], 1, scratch[1:])

        def local():
            return pltpu.make_async_copy(x_ref, o_ref.at[p.c], scratch[0])

        def first(to, ss, rs):
            return rcopy(x_ref, o_ref.at[p.c], ss.at[0], rs.at[0], {"ctx": to})

        local().start()
        first(p.far, share.fs, share.fr).start()
        first(p.near, share.ns, share.nr).start()
        yield
        share.forward(0)
        yield
        local().wait()
        share.finish()

    return Job(
        run, [(x, ANY)], [(like((4,) + x.shape, x.dtype), ANY)], [DMA] + share_sems(1)
    )


class Halve:
    def __init__(self, p, source, bufs, sems):
        self.p, self.source = p, source
        self.own, self.got, self.away, self.total = bufs
        self.ls, self.ns, self.nr, self.fs, self.fr = sems
        self.count, self.rows = self.total.shape[:2]

    def local(self, i):
        q = self.p.c if i == 0 else self.p.far
        return pltpu.make_async_copy(self.source(q), self.own.at[i], self.ls.at[i])

    def to_near(self, i):
        q = self.p.near if i == 0 else self.p.other
        return rcopy(
            self.source(q), self.got.at[i], self.ns.at[i], self.nr.at[i], {"ctx": self.p.near}
        )

    def index(self, k):
        return lax.rem(self.p.f + k, self.count) if self.count == self.p.size else k

    def to_far(self, k):
        j = self.index(k)
        return rcopy(
            self.own.at[1, j], self.away.at[j], self.fs.at[k], self.fr.at[k], {"ctx": self.p.far}
        )

    def start(self):
        for i in (1, 0):
            self.local(i).start()
        for i in (1, 0):
            self.to_near(i).start()

    def send(self):
        self.local(1).wait()
        self.to_near(1).wait_recv()
        for k in range(self.count):
            own = self.own.at[1, self.index(k)]
            add_blocks(own, [own, self.got.at[1, self.index(k)]], bf16, self.rows)
            self.to_far(k).start()

    def mine(self):
        self.local(0).wait()
        self.to_near(0).wait_recv()

    def block(self, k):
        self.to_far(k).wait_recv()
        j = self.index(k)
        add_blocks(
            self.total.at[j],
            [self.own.at[0, j], self.got.at[0, j], self.away.at[j]],
            bf16,
            self.rows,
        )

    def finish(self):
        for i in range(2):
            self.to_near(i).wait_send()
        for j in range(self.count):
            self.to_far(j).wait_send()


def halve_scratch(count, rows, cols, total=True):
    return [
        pltpu.VMEM((2, count, rows, cols), bf16),
        pltpu.VMEM((2, count, rows, cols), bf16),
        pltpu.VMEM((count, rows, cols), bf16),
    ] + [pltpu.VMEM((count, rows, cols), bf16)] * total + [
        DMA((2,)),
        DMA((2,)),
        DMA((2,)),
        DMA((count,)),
        DMA((count,)),
    ]


def halve_job(x, columns=True):
    n, rows, cols = x.shape
    shape = (n, rows, cols // 4) if columns else (n // 4, rows, cols)

    def run(p, ins, outs, scratch):
        (x_ref,), (o_ref,) = ins, outs

        def source(q):
            if columns:
                return x_ref.at[:, :, column_block(q, shape[2])]
            return x_ref.at[pl.ds(q * shape[0], shape[0])]

        halve = Halve(p, source, list(scratch[:3]) + [o_ref], scratch[3:])
        halve.start()
        yield
        halve.send()
        yield
        halve.mine()
        for j in range(shape[0]):
            halve.block(j)
            if j % 2 == 1:
                yield
        halve.finish()

    return Job(run, [(x, ANY)], [(like(shape, bf16), VM)], halve_scratch(*shape, total=False))


def home_job(wgrad, size):
    _, depth, total = wgrad.shape
    quarter = total // 4

    def run(p, ins, outs, scratch):
        (w_ref,), (h_ref,) = ins, outs
        halve = Halve(
            p, lambda q: w_ref.at[:, :, column_block(q, quarter)], scratch[:4], scratch[4:9]
        )
        lsem, ws, wr = scratch[9:12]

        def view(d, q):
            return h_ref.at[lax.rem(p.f - d + size, size), :, column_block(q, quarter)]

        def local():
            return pltpu.make_async_copy(halve.total.at[p.f], view(0, p.c), lsem)

        def move(d):
            to = lax.rem(p.f + d, size)
            return rcopy(halve.total.at[to], view(0, p.c), ws.at[d], wr.at[d], {"fsdp": to})

        def came(d):
            ref = view(d, p.c)
            rcopy(ref, ref, ws.at[d], wr.at[d], {"fsdp": lax.rem(p.f + d, size)}).wait_recv()

        share = Share(p, view, size, scratch[12:])
        halve.start()
        yield
        halve.send()
        yield
        halve.mine()
        for k in range(size):
            halve.block(k)
            if k == 0:
                local().start()
                share.send(0, halve.total.at[p.f])
            else:
                move(k).start()
            if k % 2 == 1:
                yield
        for d in range(1, size):
            came(d)
            share.send(d)
            if d % 2 == 0:
                yield
        for d in range(size):
            share.forward(d)
            if d % 4 == 3:
                yield
        local().wait()
        share.finish()
        halve.finish()
        for d in range(1, size):
            move(d).wait_send()

    return Job(
        run,
        [(wgrad, ANY)],
        [(like((size, depth, total), bf16), ANY)],
        halve_scratch(size, depth, quarter)
        + [DMA, DMA((size,)), DMA((size,))]
        + share_sems(size),
    )


def deliver_job(piece, size):
    _, depth, quarter = piece.shape

    def run(p, ins, outs, scratch):
        (x_ref,), (h_ref,) = ins, outs
        lsem, ws, wr = scratch[:3]

        def view(d, q):
            return h_ref.at[lax.rem(p.f - d + size, size), :, column_block(q, quarter)]

        def local():
            return pltpu.make_async_copy(x_ref.at[p.f], view(0, p.c), lsem)

        def move(d):
            to = lax.rem(p.f + d, size)
            return rcopy(x_ref.at[to], view(0, p.c), ws.at[d], wr.at[d], {"fsdp": to})

        def came(d):
            ref = view(d, p.c)
            rcopy(ref, ref, ws.at[d], wr.at[d], {"fsdp": lax.rem(p.f + d, size)}).wait_recv()

        share = Share(p, view, size, scratch[3:])
        local().start()
        for d in range(1, size):
            move(d).start()
        share.send(0, x_ref.at[p.f])
        yield
        for d in range(1, size):
            came(d)
            share.send(d)
            if d % 4 == 3:
                yield
        for d in range(size):
            share.forward(d)
            if d % 4 == 3:
                yield
        local().wait()
        share.finish()
        for d in range(1, size):
            move(d).wait_send()

    return Job(
        run,
        [(piece, ANY)],
        [(like((size, depth, 4 * quarter), bf16), ANY)],
        [DMA, DMA((size,)), DMA((size,))] + share_sems(size),
    )


def ctx_sum_job(x):
    rows, cols = x.shape[0] // 4, x.shape[1]
    x = x.reshape(4, rows, cols)

    def run(p, ins, outs, scratch):
        (x_ref,), (o_ref,) = ins, outs
        halve = Halve(p, lambda q: x_ref.at[pl.ds(q, 1)], scratch[:4], scratch[4:9])
        share = Share(p, lambda d, q: o_ref.at[q], 1, scratch[10:])
        halve.start()
        yield
        halve.send()
        yield
        halve.mine()
        halve.block(0)
        share.send(0, halve.total.at[0])

        def local():
            return pltpu.make_async_copy(halve.total.at[0], o_ref.at[p.c], scratch[9])

        local().start()
        yield
        share.forward(0)
        yield
        local().wait()
        share.finish()
        halve.finish()

    return Job(
        run,
        [(x, ANY)],
        [(like((4, rows, cols), bf16), ANY)],
        halve_scratch(1, rows, cols) + [DMA] + share_sems(1),
    )


def sum_job(partial, size):
    rows, tokens = partial.shape[0], partial.shape[1] // size

    def run(p, ins, outs, scratch):
        (p_ref,), (o_ref,) = ins, outs
        buf, ss, rs, gs, gr = scratch

        def at(i):
            return pl.ds(pl.multiple_of(i * tokens, 128), tokens)

        def first(d):
            to = lax.rem(p.f + d, size)
            return rcopy(p_ref.at[:, at(to)], buf.at[d], ss.at[d], rs.at[d], {"fsdp": to})

        def second(d):
            to = lax.rem(p.f + d, size)
            ref = o_ref.at[:, at(p.f)]
            return rcopy(ref, ref, gs.at[d], gr.at[d], {"fsdp": to})

        def came(d):
            ref = o_ref.at[:, at(lax.rem(p.f - d + size, size))]
            rcopy(ref, ref, gs.at[d], gr.at[d], {"fsdp": lax.rem(p.f + d, size)}).wait_recv()

        for d in range(1, size):
            first(d).start()
        yield
        total = p_ref[:, at(p.f)].astype(f32)
        for d in range(1, size):
            first(d).wait_recv()
            total += buf[d].astype(f32)
        o_ref[:, at(p.f)] = total.astype(bf16)
        for d in range(1, size):
            second(d).start()
        yield
        for d in range(1, size):
            came(d)
        for d in range(1, size):
            first(d).wait_send()
            second(d).wait_send()

    return Job(
        run,
        [(partial, VM)],
        [(like(partial.shape, bf16), VM)],
        [pltpu.VMEM((size, rows, tokens), bf16)] + [DMA((size,))] * 4,
    )


def all_sum_job(x, size, held):
    rows, cols = x.shape[1:]

    def run(p, ins, outs, scratch):
        (o_ref,), x_ref = outs, held[0]
        buf, mid, far, ss, rs, ts, tr = scratch

        def copy(d):
            to = lax.rem(p.f + d, size)
            return rcopy(x_ref.at[to], buf.at[d], ss.at[d], rs.at[d], {"fsdp": to})

        def swap(i, to):
            return rcopy(mid.at[i], far.at[i], ts.at[i], tr.at[i], {"ctx": to})

        for d in range(1, size):
            copy(d).start()
        yield
        total = x_ref[p.f]
        for d in range(1, size):
            copy(d).wait_recv()
            total += buf[d]
        mid[0] = total
        swap(0, p.near).start()
        yield
        swap(0, p.near).wait_recv()
        mid[1] = mid[0] + far[0]
        swap(1, p.far).start()
        yield
        swap(1, p.far).wait_recv()
        o_ref[...] = mid[1] + far[1]
        for d in range(1, size):
            copy(d).wait_send()
        swap(0, p.near).wait_send()
        swap(1, p.far).wait_send()

    return Job(
        run,
        [],
        [(like((rows, cols), f32), VM)],
        [pltpu.VMEM((size, rows, cols), f32)]
        + [pltpu.VMEM((2, rows, cols), f32)] * 2
        + [DMA((size,)), DMA((size,)), DMA((2,)), DMA((2,))],
    )


UNROLL = 8
LN2 = 0.6931471805599453


def steps(length, body, init):
    count = UNROLL if length % UNROLL == 0 else 1

    def some(i, carry):
        for j in range(count):
            carry = body(i * count + j, carry)
        return carry

    return lax.fori_loop(0, length // count, some, init)


class Scan:
    def __init__(self, streams, length, chan):
        self.width = math.gcd(streams, 8)
        self.groups, self.tiles, self.length = streams // self.width, chan // 128, length
        self.pieces = 2 * self.groups * self.tiles

    def piece(self, i):
        tile = lax.rem(i, self.tiles)
        rest = i // self.tiles
        return lax.rem(rest, self.groups), rest // self.groups, tile

    def lanes(self, tile):
        return pl.ds(pl.multiple_of(tile * 128, 128), 128)

    def rows(self, group, block, o):
        first = group * (self.width * 2 * self.length) + block * self.length + o
        return pl.ds(first, self.width, stride=2 * self.length)

    def spread(self, wr, group, block, out, column):
        def body(o, carry):
            values = wr[self.rows(group, block, o), :]
            for n in range(NS):
                out[o, n] = jnp.broadcast_to(
                    values[:, column + n : column + n + 1], (self.width, 128)
                )
            return carry

        steps(self.length, body, 0)

    def tiled(self):
        return pltpu.VMEM((self.tiles, self.groups * self.width * 2 * self.length, 128), f32)

    def tile_copies(self, flat, tiled, sems, out=False):
        copies = []
        for t in range(self.tiles):
            there = flat.at[:, t * 128 : (t + 1) * 128]
            pair = (tiled.at[t], there) if out else (there, tiled.at[t])
            copies.append(pltpu.make_async_copy(*pair, sems.at[t]))
        return copies

    def zero(self):
        return jnp.zeros((self.width, 128), f32)

    def link(self, order, b, ends, group, lanes, rates):
        at = order[b]
        total = ends[at, group, NS, :, lanes].astype(f32)
        return at, [jnp.exp2(total * rate) for rate in rates]

    def link_shape(self, blocks, chan, extra):
        return (blocks, self.groups, NS + extra, self.width, chan)


def hosted(loops, jobs, size, cid, name, ins, outs, scratch, plan):
    n_in, n_out = len(ins), len(outs)
    job_in = sum(len(job.ins) for job in jobs)
    job_out = sum(len(job.outs) for job in jobs)

    def kernel(*refs):
        place = Place(size)
        place.greet()
        own_in, refs = refs[:n_in], refs[n_in:]
        ins_, refs = part(refs[:job_in], jobs, "ins"), refs[job_in:]
        own_out, refs = refs[:n_out], refs[n_out:]
        outs_, refs = part(refs[:job_out], jobs, "outs"), refs[job_out:]
        own_scratch, refs = refs[: len(scratch)], refs[len(scratch) :]
        scratch_ = part(refs, jobs, "scratch")
        moving = Moving(
            [job.steps(place, i, o, s) for job, i, o, s in zip(jobs, ins_, outs_, scratch_)]
        )
        for at, stage in enumerate(loops(place, own_in, own_out, own_scratch)):
            for which in plan.get(at, ()):
                moving.step(which)
            if callable(stage):
                stage()
                continue
            count, body = stage

            def whole(i, carry):
                body(i)
                for k in range(count):
                    if plan.get((at, k)):
                        @pl.when(i == k)
                        def _():
                            for which in plan[at, k]:
                                moving.step(which)

                return carry

            lax.fori_loop(0, count, whole, 0)
        for which in plan.get("end", ()):
            moving.step(which)
        moving.drain()

    got = pl.pallas_call(
        kernel,
        out_shape=[shape for shape, _ in outs] + [shape for job in jobs for shape, _ in job.outs],
        in_specs=[spec for _, spec in ins] + [spec for job in jobs for _, spec in job.ins],
        out_specs=[spec for _, spec in outs] + [spec for job in jobs for _, spec in job.outs],
        scratch_shapes=list(scratch) + [item for job in jobs for item in job.scratch],
        compiler_params=params(cid, 63 << 20),
        name=name,
    )(*[array for array, _ in ins], *[array for job in jobs for array, _ in job.ins])
    return got[:n_out], part(got[n_out:], jobs, "outs")


SM = pl.BlockSpec(memory_space=pltpu.SMEM)


def scan_forward(order, dt, x, wr, rate2, streams, jobs, size, cid, plan):
    chan = dt.shape[1]
    scan = Scan(streams, dt.shape[0] // streams // 2, chan)
    blocks = order.shape[0] - 2
    length = scan.length

    def loops(p, ins, outs, scratch):
        order_ref, dt_flat, x_flat, wr_ref, rate_ref = ins
        y_flat, s_ref, ends_ref = outs
        wb, rb, dt_ref, x_ref, y_ref, dt_sem, x_sem, y_sem = scratch[:8]
        share = Share(p, lambda d, q: ends_ref.at[pl.ds(2 * q, 2)], 1, scratch[8:])

        def load():
            copies = scan.tile_copies(dt_flat, dt_ref, dt_sem)
            copies += scan.tile_copies(x_flat, x_ref, x_sem)
            for copy in copies:
                copy.start()
            for copy in copies:
                copy.wait()

        def store():
            copies = scan.tile_copies(y_flat, y_ref, y_sem, True)
            for copy in copies:
                copy.start()
            for copy in copies:
                copy.wait()

        def ends(i):
            group, block, tile = scan.piece(i)
            lanes = scan.lanes(tile)

            @pl.when(tile == 0)
            def _():
                scan.spread(wr_ref, group, block, wb, 0)

            rates = [rate_ref[n : n + 1, lanes] for n in range(NS)]

            def body(o, carry):
                total, states = carry
                at = scan.rows(group, block, o)
                step = dt_ref[tile, at, :]
                pushed = step * x_ref[tile, at, :]
                states = tuple(
                    jnp.exp2(step * rates[n]) * states[n] + wb[o, n] * pushed for n in range(NS)
                )
                return (total + step, states)

            total, states = steps(length, body, (scan.zero(), (scan.zero(),) * NS))
            mine = 2 * p.c + block
            for n in range(NS):
                ends_ref[mine, group, n, :, lanes] = states[n].astype(bf16)
            ends_ref[mine, group, NS, :, lanes] = total.astype(bf16)

        def send():
            share.send(0)

        def arrive():
            share.forward(0)
            share.finish()

        def forward(i):
            group, block, tile = scan.piece(i)
            lanes = scan.lanes(tile)

            @pl.when(tile == 0)
            def _():
                scan.spread(wr_ref, group, block, wb, 0)
                scan.spread(wr_ref, group, block, rb, NS)

            rates = [rate_ref[n : n + 1, lanes] for n in range(NS)]
            mine = order_ref[blocks + block]

            def link(b, states):
                at, decays = scan.link(order_ref, b, ends_ref, group, lanes, rates)
                return tuple(
                    jnp.where(
                        b < mine,
                        decays[n] * states[n] + ends_ref[at, group, n, :, lanes].astype(f32),
                        states[n],
                    )
                    for n in range(NS)
                )

            states = lax.fori_loop(0, blocks - 1, link, (scan.zero(),) * NS)
            for n in range(NS):
                s_ref[block, group, n, :, lanes] = states[n]

            def body(o, states):
                at = scan.rows(group, block, o)
                step = dt_ref[tile, at, :]
                pushed = step * x_ref[tile, at, :]
                states = tuple(
                    jnp.exp2(step * rates[n]) * states[n] + wb[o, n] * pushed for n in range(NS)
                )
                total = [rb[o, n] * states[n] for n in range(NS)]
                while len(total) > 1:
                    total = [total[j] + total[j + 1] for j in range(0, len(total), 2)]
                y_ref[tile, at, :] = total[0]
                return states

            steps(length, body, states)

        return [load, (scan.pieces, ends), send, arrive, (scan.pieces, forward), store]

    spread = pltpu.VMEM((length, NS, scan.width, 128), f32)
    return hosted(
        loops,
        jobs,
        size,
        cid,
        "scan_forward",
        [(order, SM), (dt, ANY), (x, ANY), (wr, VM), (rate2, VM)],
        [
            (like(dt.shape, f32), ANY),
            (like(scan.link_shape(2, chan, 0), f32), VM),
            (like(scan.link_shape(blocks, chan, 1), bf16), VM),
        ],
        [spread, spread] + [scan.tiled()] * 3 + [DMA((scan.tiles,))] * 3 + share_sems(1),
        plan,
    )


def scan_backward(order, dt, x, g, wr, rate2, starts, ends, streams, jobs, size, cid, plan):
    chan = dt.shape[1]
    scan = Scan(streams, dt.shape[0] // streams // 2, chan)
    blocks = order.shape[0] - 2
    length, width = scan.length, scan.width

    def loops(p, ins, outs, scratch):
        order_ref, dt_flat, x_flat, g_flat, wr_ref, rate_ref, start_ref, ends_ref = ins
        sb_flat, cw_flat, wrb_ref, dec_ref = outs
        backs_ref, wb, rb, kept, decays, wparts, rparts, sums = scratch[:8]
        dt_ref, x_ref, g_ref, sb_ref, cw_ref, dt_sem, x_sem, g_sem, sb_sem, cw_sem = scratch[8:18]
        share = Share(p, lambda d, q: backs_ref.at[pl.ds(2 * q, 2)], 1, scratch[18:])

        def load():
            copies = scan.tile_copies(dt_flat, dt_ref, dt_sem)
            copies += scan.tile_copies(x_flat, x_ref, x_sem)
            copies += scan.tile_copies(g_flat, g_ref, g_sem)
            for copy in copies:
                copy.start()
            for copy in copies:
                copy.wait()

        def store():
            copies = scan.tile_copies(sb_flat, sb_ref, sb_sem, True)
            copies += scan.tile_copies(cw_flat, cw_ref, cw_sem, True)
            for copy in copies:
                copy.start()
            for copy in copies:
                copy.wait()

        def backs(i):
            group, block, tile = scan.piece(i)
            lanes = scan.lanes(tile)

            @pl.when(tile == 0)
            def _():
                scan.spread(wr_ref, group, block, rb, NS)

            rates = [rate_ref[n : n + 1, lanes] for n in range(NS)]

            def body(j, carries):
                o = length - 1 - j
                at = scan.rows(group, block, o)
                step = dt_ref[tile, at, :]
                grad = g_ref[tile, at, :]
                return tuple(
                    jnp.exp2(step * rates[n]) * (carries[n] + rb[o, n] * grad) for n in range(NS)
                )

            carries = steps(length, body, (scan.zero(),) * NS)
            mine = 2 * p.c + block
            for n in range(NS):
                backs_ref[mine, group, n, :, lanes] = carries[n].astype(bf16)

        def send():
            share.send(0)

        def arrive():
            share.forward(0)
            share.finish()

        def backward(i):
            group, block, tile = scan.piece(i)
            lanes = scan.lanes(tile)

            @pl.when(tile == 0)
            def _():
                scan.spread(wr_ref, group, block, wb, 0)
                scan.spread(wr_ref, group, block, rb, NS)
                sums[...] = jnp.zeros_like(sums)

            rates = [rate_ref[n : n + 1, lanes] for n in range(NS)]

            def forward(o, states):
                at = scan.rows(group, block, o)
                step = dt_ref[tile, at, :]
                pushed = step * x_ref[tile, at, :]
                new = []
                for n in range(NS):
                    decay = jnp.exp2(step * rates[n])
                    decays[o, n] = decay
                    kept[o, n] = states[n]
                    new.append(decay * states[n] + wb[o, n] * pushed)
                return tuple(new)

            first = tuple(start_ref[block, group, n, :, lanes] for n in range(NS))
            last = steps(length, forward, first)
            for n in range(NS):
                kept[length, n] = last[n]

            mine = order_ref[blocks + block]

            def link(j, carries):
                b = blocks - 1 - j
                at, decay = scan.link(order_ref, b, ends_ref, group, lanes, rates)
                return tuple(
                    jnp.where(
                        b > mine,
                        backs_ref[at, group, n, :, lanes].astype(f32) + decay[n] * carries[n],
                        carries[n],
                    )
                    for n in range(NS)
                )

            carries = lax.fori_loop(0, blocks - 1, link, (scan.zero(),) * NS)
            for n in range(NS):
                dec_ref[block, group, n, :, lanes] = scan.zero()

            def body(j, carries):
                o = length - 1 - j
                at = scan.rows(group, block, o)
                step = dt_ref[tile, at, :]
                value = x_ref[tile, at, :]
                grad = g_ref[tile, at, :]
                pushed = step * value
                slope, pulled, new = [], [], []
                to = pl.ds(pl.multiple_of(o * width, width), width)
                for n in range(NS):
                    full = carries[n] + rb[o, n] * grad
                    moved = decays[o, n] * full
                    new.append(moved)
                    back = moved * kept[o, n]
                    slope.append(back * rates[n])
                    dec_ref[block, group, n, :, lanes] += back * step
                    pulled.append(full * wb[o, n])
                    wparts[to, n * 128 : (n + 1) * 128] = full * pushed
                    rparts[to, n * 128 : (n + 1) * 128] = kept[o + 1, n] * grad
                while len(slope) > 1:
                    slope = [slope[j] + slope[j + 1] for j in range(0, len(slope), 2)]
                    pulled = [pulled[j] + pulled[j + 1] for j in range(0, len(pulled), 2)]
                sb_ref[tile, at, :] = slope[0] * LN2 + pulled[0] * value
                cw_ref[tile, at, :] = pulled[0]
                return tuple(new)

            steps(length, body, carries)
            source = lax.broadcasted_iota(jnp.int32, (NS * 128, 128), 0) // 128
            target = lax.broadcasted_iota(jnp.int32, (NS * 128, 128), 1)
            pick_w = jnp.where(source == target, 1.0, 0.0).astype(bf16)
            pick_r = jnp.where(source + NS == target, 1.0, 0.0).astype(bf16)
            sums[...] += jnp.dot(
                wparts[...].astype(bf16), pick_w, preferred_element_type=f32
            ) + jnp.dot(rparts[...].astype(bf16), pick_r, preferred_element_type=f32)

            @pl.when(tile == scan.tiles - 1)
            def _():
                def out(o, carry):
                    wrb_ref[scan.rows(group, block, o), :] = sums[
                        pl.ds(pl.multiple_of(o * width, width), width), :
                    ]
                    return carry

                steps(length, out, 0)

        return [load, (scan.pieces, backs), send, arrive, (scan.pieces, backward), store]

    spread = pltpu.VMEM((length, NS, width, 128), f32)
    parts = pltpu.VMEM((length * width, NS * 128), f32)
    return hosted(
        loops,
        jobs,
        size,
        cid,
        "scan_backward",
        [
            (order, SM), (dt, ANY), (x, ANY), (g, ANY), (wr, VM), (rate2, VM), (starts, VM), (ends, VM),
        ],
        [
            (like(dt.shape, f32), ANY),
            (like(dt.shape, f32), ANY),
            (like((dt.shape[0], 128), f32), VM),
            (like(scan.link_shape(2, chan, 0), f32), VM),
        ],
        [
            pltpu.VMEM(scan.link_shape(blocks, chan, 0), bf16),
            spread,
            spread,
            pltpu.VMEM((length + 1, NS, width, 128), f32),
            spread,
            parts,
            parts,
            pltpu.VMEM((length * width, 128), f32),
        ]
        + [scan.tiled()] * 5
        + [DMA((scan.tiles,))] * 5
        + share_sems(1),
        plan,
    )


def attention_forward(q_t, k, v_t, bias_t, jobs, size, cid, plan):
    rows = q_t.shape[1]
    group = H // KV

    def loops(p, ins, outs, scratch):
        q_ref, k_ref, v_ref, bias_ref = ins
        o_ref, log_ref = outs

        def head(h):
            at = pl.ds(pl.multiple_of(h * HD, HD), HD)
            g = h // group
            scores = (
                jnp.dot(k_ref[g], q_ref[at, :], preferred_element_type=f32) * score_scale
                + bias_ref[...]
            )
            largest = jnp.max(scores, axis=0, keepdims=True)
            expo = jnp.exp(scores - largest)
            total = jnp.sum(expo, axis=0, keepdims=True)
            probs = (expo * (1.0 / total)).astype(bf16)
            values = v_ref[pl.ds(pl.multiple_of(g * HD, HD), HD), :]
            o_ref[at, :] = jnp.dot(values, probs, preferred_element_type=f32).astype(bf16)
            log_ref[pl.ds(h, 1), :] = largest + jnp.log(total)

        return [(H, head)]

    return hosted(
        loops,
        jobs,
        size,
        cid,
        "attention_forward",
        [(q_t, VM), (k, VM), (v_t, VM), (bias_t, VM)],
        [(like(q_t.shape, bf16), VM), (like((H, rows), f32), VM)],
        [],
        plan,
    )


def attention_backward(q_t, k, k_t, v, bias_t, log_total, dout_t, jobs, size, cid, plan):
    group = H // KV
    keys = k.shape[1]

    def loops(p, ins, outs, scratch):
        q_ref, k_ref, kt_ref, v_ref, bias_ref, log_ref, do_ref = ins
        dq_ref, dkv_ref = outs
        contract = (((1,), (1,)), ((), ()))

        def zero():
            dkv_ref[...] = jnp.zeros_like(dkv_ref)

        def head(h):
            at = pl.ds(pl.multiple_of(h * HD, HD), HD)
            g = h // group
            to_k = pl.ds(pl.multiple_of(g * HD, HD), HD)
            to_v = pl.ds(pl.multiple_of((KV + g) * HD, HD), HD)
            query, dout = q_ref[at, :], do_ref[at, :]
            scores = (
                jnp.dot(k_ref[g], query, preferred_element_type=f32) * score_scale + bias_ref[...]
            )
            probs = jnp.exp(scores - log_ref[pl.ds(h, 1), :])
            back = jnp.dot(v_ref[g], dout, preferred_element_type=f32)
            centre = jnp.sum(probs * back, axis=0, keepdims=True)
            score_back = (probs * (back - centre)).astype(bf16)
            dq_ref[at, :] = (
                jnp.dot(kt_ref[to_k, :], score_back, preferred_element_type=f32) * score_scale
            ).astype(bf16)
            dkv_ref[to_k, :] += score_scale * lax.dot_general(
                query, score_back, contract, preferred_element_type=f32
            )
            dkv_ref[to_v, :] += lax.dot_general(
                dout, probs.astype(bf16), contract, preferred_element_type=f32
            )

        return [zero, (H, head)]

    return hosted(
        loops,
        jobs,
        size,
        cid,
        "attention_backward",
        [
            (q_t, VM), (k, VM), (k_t, VM), (v, VM), (bias_t, VM), (log_total, VM), (dout_t, VM),
        ],
        [(like(q_t.shape, bf16), VM), (like((2 * KV * HD, keys), f32), VM)],
        [],
        plan,
    )


def start_exchange(rows_in, gains, first, ffn, first_pack, ffn_pack, size, cid):
    depth = first[0].shape[0]
    n_first = len(first)
    weights = list(first) + list(ffn)
    (first_cuts, first_at, first_total), (ffn_cuts, ffn_at, ffn_total) = first_pack, ffn_pack
    held = []

    def loops(p, ins, outs, scratch):
        (packed_ref,) = outs
        mine, sems = scratch[1 : 1 + len(weights)], scratch[-1]
        held.append(scratch[0])

        def load(which):
            return pltpu.make_async_copy(ins[which], mine[which], sems.at[which])

        def begin():
            for which in range(len(weights)):
                load(which).start()

        def pack_first():
            for which in range(n_first):
                load(which).wait()
            pack_columns(mine[:n_first], scratch[0], first_cuts, first_at, size)

        def pack_ffn():
            for which in range(n_first, len(weights)):
                load(which).wait()
            pack_columns(mine[n_first:], packed_ref, ffn_cuts, ffn_at, size)

        return [begin, pack_first, pack_ffn]

    packed = like((size, depth, first_total), bf16)
    return hosted(
        loops,
        [gather_job(rows_in, size), spread_job(gains, size), move_job(packed, size, held)],
        size,
        cid,
        "start",
        [(item, ANY) for item in weights],
        [(like((size, depth, ffn_total), bf16), VM)],
        [pltpu.VMEM(packed.shape, bf16)]
        + [pltpu.VMEM(item.shape, bf16) for item in weights]
        + [DMA((len(weights),))],
        PLAN_START,
    )


def ffn_sums(low, back, hidden, grads, jobs, size, cid):
    rows, width = low.shape
    total, units = back.shape[1], hidden.shape[1]
    depth, quarter = width // size, total // 4
    contract = (((0,), (0,)), ((), ()))

    def loops(p, ins, outs, scratch):
        low_ref, back_ref, hidden_ref, grads_ref = ins
        quarter_ref, down_ref = outs
        whole = scratch[0]
        halve = Halve(
            p,
            lambda q: whole.at[:, :, column_block(q, quarter)],
            list(scratch[1:4]) + [quarter_ref],
            scratch[4:],
        )

        def tile(i):
            lanes = column_block(i, 128)
            got = lax.dot_general(
                low_ref[...], back_ref[:, lanes], contract, preferred_element_type=f32
            )
            for f in range(size):
                whole[f, :, lanes] = got[f * depth : (f + 1) * depth, :].astype(bf16)

        def down_tile(i):
            lanes = column_block(i, 128)
            down_ref[pl.ds(pl.multiple_of(i * 128, 128), 128), :] = lax.dot_general(
                hidden_ref[:, lanes], grads_ref[...], contract, preferred_element_type=f32
            ).astype(bf16)

        def sums():
            halve.mine()
            for k in range(size):
                halve.block(k)
            halve.finish()

        return [
            (total // 128, tile), halve.start, halve.send, (units // 128, down_tile), sums,
        ]

    return hosted(
        loops,
        jobs,
        size,
        cid,
        "ffn_sums",
        [(low, VM), (back, VM), (hidden, VM), (grads, VM)],
        [(like((size, depth, quarter), bf16), VM), (like((units, width), bf16), VM)],
        [pltpu.VMEM((size, depth, total), bf16)] + halve_scratch(size, depth, quarter, False),
        PLAN_FFN,
    )


def finish(wgrad, back, mat, normed, gain, gain_rows, small, ffn_home, ffn_pack, shapes, size, cid):
    rows_all, total = back.shape
    width = mat.shape[0]
    rows = rows_all // size
    cuts, offsets = ffn_pack
    held_rows, held_gains = [], []
    contract = (((1,), (1,)), ((), ()))
    n_out = len(shapes)

    def loops(p, ins, outs, scratch):
        back_ref, mat_ref, normed_ref, gain_ref, gain_rows_ref, home_ref = ins
        part_ref, total_ref, gains_ref, home_sem, out_sem, home_in = scratch[:6]
        laid = scratch[6:]
        held_rows.append(part_ref)
        held_gains.append(gains_ref)

        def fetch():
            return pltpu.make_async_copy(home_ref, home_in, home_sem)

        def store(i):
            return pltpu.make_async_copy(laid[i], outs[i], out_sem.at[i])

        def begin():
            fetch().start()
            total_ref[...] = jnp.zeros_like(total_ref)

        def block(i):
            at = pl.ds(pl.multiple_of(i * rows, rows), rows)
            got = lax.dot_general(
                back_ref[at, :], mat_ref[...], contract, preferred_element_type=f32
            ).astype(bf16)
            part_ref[i] = got
            product = got.astype(f32) * normed_ref[at, :].astype(f32)
            total_ref[...] += jnp.sum(product, axis=0, keepdims=True)

        def gains():
            gains_ref[...] = gain_rows_ref[...]
            first = (total_ref[...] / gain_ref[...]).astype(f32)
            cols = width // size
            for f in range(size):
                gains_ref[f, 0:1, :] = first[:, f * cols : (f + 1) * cols]

        def lay_out():
            fetch().wait()
            unpack_pieces(home_in, laid, cuts, offsets, size)
            for i in range(n_out):
                store(i).start()

        def stored():
            for i in range(n_out):
                store(i).wait()

        return [begin, (size, block), gains, lay_out, stored]

    part_shape = like((size, rows, width), bf16)
    return hosted(
        loops,
        [
            scatter_job(part_shape, size, held_rows),
            home_job(wgrad, size),
            ctx_sum_job(small),
            all_sum_job(gain_rows, size, held_gains),
        ],
        size,
        cid,
        "finish",
        [(back, VM), (mat, VM), (normed, VM), (gain, VM), (gain_rows, VM), (ffn_home, ANY)],
        [(like(shape, f32), ANY) for shape in shapes],
        [
            pltpu.VMEM(part_shape.shape, bf16),
            pltpu.VMEM((1, width), f32),
            pltpu.VMEM(gain_rows.shape, f32),
            DMA,
            DMA((n_out,)),
            pltpu.VMEM(ffn_home.shape, bf16),
        ]
        + [pltpu.VMEM(shape, f32) for shape in shapes],
        PLAN_FINISH,
    )


PLAN_START = {1: (0, 1), 2: (0, 2), "end": (0, 2)}
PLAN_FORWARD = {
    1: (2, 1),
    (1, 3): (2,),
    (1, 6): (2,),
    2: (0,),
    (4, 0): (2, 1, 1, 1),
    (4, 1): (0, 2),
    (4, 3): (0, 1),
    (4, 5): (0, 1, 2),
    (4, 7): (0,),
}
PLAN_ATTEND = {0: (0,), (0, 6): (0,), (0, 14): (0,), (0, 22): (0,)}
PLAN_FFN = {0: (0,), (0, 7): (0,), 1: (0,), (3, 1): (0,)}
PLAN_ATTEND_BACK = {
    0: (0, 1),
    (1, 5): (1,),
    (1, 9): (0,),
    (1, 16): (0,),
    "end": (0, 1, 1, 1, 0),
}
PLAN_FINISH = {
    1: (1,),
    (1, 1): (1,),
    (1, 3): (1,),
    (1, 5): (1,),
    (1, 7): (1,),
    2: (1, 0, 2),
    3: (0, 1, 3, 2),
    4: (0, 1, 3, 1, 0, 2),
    "end": (1, 1, 0, 3),
}
PLAN_BACKWARD = {
    1: (4, 0, 3),
    (1, 3): (3,),
    (1, 4): (4,),
    (1, 7): (4,),
    3: (),
    (4, 0): (4, 0),
    (4, 1): (4, 1, 0, 3),
    (4, 2): (1, 0, 2),
    (4, 3): (1, 0, 2),
    (4, 4): (1, 0, 3),
    (4, 5): (1, 2),
    (4, 6): (1, 3),
    (4, 7): (2,),
}


def column_grads(x, dy):
    return jnp.einsum("ld,lk->dk", x, dy, preferred_element_type=f32).astype(bf16)


def on_device(
    layer_in,
    out_grad,
    doc_lengths,
    block_deal,
    norm_gains,
    query_weight,
    keyval_weight,
    attn_proj,
    mamba_in,
    conv_taps,
    conv_bias,
    step_bias,
    skip_gain,
    decay_log,
    select_proj,
    step_proj,
    mamba_proj,
    gate_weight,
    up_weight,
    down_weight,
):
    size = lax.axis_size("fsdp")
    n_ctx = lax.axis_size("ctx")
    rows = layer_in.shape[1]
    half_rows = rows // 2
    width = layer_in.shape[2]
    blocks_all = 2 * n_ctx
    group = H // KV
    chan = INNER // size
    q_cols, kv_cols = H * HD // size, 2 * KV * HD // size
    ff_cols = gate_weight.shape[1] // size
    rows_all = size * rows
    ctx_place = lax.axis_index("ctx")
    deal_flat = block_deal.reshape(-1)
    my_blocks = lax.dynamic_slice_in_dim(block_deal, ctx_place, 1, 0)[0]
    offsets = jnp.arange(half_rows, dtype=jnp.int32)
    my_places = (my_blocks[:, None] * half_rows + offsets[None, :]).reshape(-1)
    key_places = (deal_flat[:, None] * half_rows + offsets[None, :]).reshape(-1)
    lengths = doc_lengths[0]
    starts = jnp.cumsum(lengths) - lengths

    def segment(places):
        return jnp.sum((places[:, None] >= starts[None, :]).astype(jnp.int32), axis=1)

    allowed = (key_places[:, None] <= my_places[None, :]) & (
        segment(key_places)[:, None] == segment(my_places)[None, :]
    )
    bias_t = jnp.where(allowed, 0.0, -1e30).astype(f32)
    inverse = jnp.argsort(deal_flat)

    depth = query_weight.shape[0]
    chan_up, qkv_up = up_to(chan, 128), up_to(q_cols + kv_cols, 128)
    ff_up = up_to(ff_cols, 128)
    first_cuts = ((0, 0, q_cols), (1, 0, kv_cols), (2, 0, chan), (2, INNER, chan))
    first_at = (0, q_cols, qkv_up, qkv_up + chan_up)
    first_total = up_to(qkv_up + 2 * chan_up, 128 * n_ctx)
    ffn_cuts = ((0, 0, ff_cols), (1, 0, ff_cols))
    ffn_at = (0, ff_up)
    ffn_total = up_to(2 * ff_up, 128 * n_ctx)
    (ffn_packed,), ((stream_all,), (gain_all,), (first_mat,)) = start_exchange(
        layer_in[0],
        norm_gains,
        (query_weight, keyval_weight, mamba_in),
        (gate_weight, up_weight),
        (first_cuts, first_at, first_total),
        (ffn_cuts, ffn_at, ffn_total),
        size,
        0,
    )
    stream_all = stream_all.reshape(rows_all, width)
    gain_float = jnp.moveaxis(gain_all, 0, 1).reshape(4, width).astype(f32)
    first_mat = first_mat.reshape(width, first_total)
    qkv_mat = first_mat[:, :qkv_up]
    entry_mat = first_mat[:, qkv_up : qkv_up + 2 * chan_up]
    ffn_quarter = ffn_total // n_ctx
    attn_wide = up_to(width, 128 * n_ctx)
    attn_packed = jnp.pad(attn_proj, ((0, 0), (0, attn_wide - width)))
    down_mat = jnp.pad(down_weight, ((0, ff_up - ff_cols), (0, 0)))
    more = chan_up - chan
    taps_mat = jnp.pad(conv_taps, ((0, 0), (0, more)))
    mamba_mat = jnp.pad(mamba_proj, ((0, more), (0, 0)))
    select_mat = jnp.pad(select_proj, ((0, more), (0, 0)))
    step_mat = jnp.pad(step_proj, ((0, 0), (0, more)))
    rate = -jnp.exp(jnp.pad(decay_log, ((0, 0), (0, more))).astype(f32))
    rate2 = rate * 1.4426950408889634
    shift_float, step_shift, skip_float = (
        jnp.pad(item, (0, more)).astype(f32) for item in (conv_bias, step_bias, skip_gain)
    )

    stream = layer_in[0].astype(f32)
    _, inv_in = norm_forward(stream, gain_float[0])
    normed_all, inv_all = norm_forward(stream_all.astype(f32), gain_float[0])
    normed_all = normed_all.astype(bf16)

    qkv_t = jnp.einsum("dk,ld->kl", qkv_mat, normed_all, preferred_element_type=f32).astype(bf16)
    entry = jnp.dot(normed_all, entry_mat, preferred_element_type=f32)
    chan = chan_up
    mixer_in = entry[:, :chan].astype(bf16)
    gate_side = entry[:, chan:]
    mixer_blocks = mixer_in.reshape(size, 2, half_rows, chan)
    tails = mixer_blocks[:, :, half_rows - (CONV - 1) :]
    (qkv,), (tails_all,) = together(
        [exchange_job(qkv_t, size, up_to(q_cols + kv_cols, 8)), ctx_gather_job(tails.reshape(-1, chan))],
        size,
        1,
        "edges",
    )
    query_t = qkv[:, :q_cols].reshape(H * HD, rows)
    keyval_t = qkv[:, q_cols : q_cols + kv_cols].reshape(2 * KV * HD, rows)
    tails_all = tails_all.reshape(n_ctx, size, 2, CONV - 1, chan)

    def in_deal_order(values):
        return jnp.moveaxis(values, 2, 1).reshape((blocks_all,) + (size,) + values.shape[3:])

    def of_blocks(values, index):
        return jnp.moveaxis(jnp.take(values, index, axis=0), 0, 1)

    before_index = inverse[jnp.maximum(my_blocks - 1, 0)]
    has_before = my_blocks > 0
    prior_tail = jnp.where(
        has_before[None, :, None, None],
        of_blocks(in_deal_order(tails_all), before_index),
        jnp.zeros_like(tails),
    )
    padded = jnp.concatenate([prior_tail, mixer_blocks], axis=2).astype(f32)
    taps_float = taps_mat.astype(f32)
    conv_blocks_out = shift_float + sum(
        taps_float[offset] * padded[:, :, offset : offset + half_rows] for offset in range(CONV)
    )
    conv_out = conv_blocks_out.reshape(rows_all, chan)
    signal = jax.nn.silu(conv_out).astype(bf16)
    signal_float = signal.astype(f32)
    selected_part = jnp.einsum(
        "ik,li->kl", select_mat, signal, preferred_element_type=f32
    ).astype(bf16)
    (selected,), (keyvals_all,) = together(
        [sum_job(selected_part, size), ctx_gather_job(keyval_t)], size, 3, "select"
    )
    keyvals_t = keyvals_all.transpose(1, 0, 2).reshape(2 * KV * HD, n_ctx * rows)
    keyvals = keyvals_t.reshape(2 * KV, HD, n_ctx * rows).transpose(0, 2, 1)
    key_groups, value_groups = keyvals[:KV], keyvals[KV:]
    step_low = selected[:RANK].T
    write_read = jnp.pad(selected[RANK:], ((0, 128 - 2 * NS), (0, 0))).T.astype(f32)
    step_pre = jnp.dot(step_low, step_mat, preferred_element_type=f32) + step_shift
    step_sizes = jax.nn.softplus(step_pre)
    order = jnp.concatenate([inverse, my_blocks]).astype(jnp.int32)
    (scan_rows, start_state, ends_all), ((grads_all,), (ffn_mat,), (attn_mat,)) = scan_forward(
        order,
        step_sizes,
        signal_float,
        write_read,
        rate2,
        size,
        [
            gather_job(out_grad[0], size),
            move_job(ffn_packed, size),
            gather_job(attn_packed, size, True),
        ],
        size,
        4,
        PLAN_FORWARD,
    )
    grads_all = grads_all.reshape(rows_all, width)
    ffn_mat = ffn_mat.reshape(width, ffn_total)
    gate_mat, up_mat = ffn_mat[:, :ff_up], ffn_mat[:, ff_up : 2 * ff_up]
    attn_mat = attn_mat.reshape(width, attn_wide)[:, :width]
    scanned = scan_rows + skip_float * signal_float
    gate_act = jax.nn.silu(gate_side)
    mamba_rows = (scanned * gate_act).astype(bf16)
    mamba_part = jnp.dot(mamba_rows, mamba_mat, preferred_element_type=f32).astype(bf16)
    (attn_rows_t, log_totals), ((mamba_out,),) = attention_forward(
        query_t,
        key_groups,
        keyvals_t[KV * HD :],
        bias_t,
        [scatter_job(mamba_part.reshape(size, rows, width), size)],
        size,
        5,
        PLAN_ATTEND,
    )
    attn_out = jnp.einsum("hl,hd->ld", attn_rows_t, attn_mat, preferred_element_type=f32)
    attn_normed, inv_attn = norm_forward(attn_out, gain_float[1])

    mamba_normed, inv_mamba = norm_forward(mamba_out, gain_float[2])
    middle = stream + 0.5 * (attn_normed + mamba_normed)
    ffn_normed, inv_ffn = norm_forward(middle, gain_float[3])
    ((ffn_low,),) = together(
        [gather_job(ffn_normed.astype(bf16), size)], size, 6, "ffn_rows"
    )
    ffn_low = ffn_low.reshape(rows_all, width)
    gate_pre = jnp.dot(ffn_low, gate_mat, preferred_element_type=f32)
    up_pre = jnp.dot(ffn_low, up_mat, preferred_element_type=f32)
    hidden = (jax.nn.silu(gate_pre) * up_pre).astype(bf16)
    down_part = jnp.dot(hidden, down_mat, preferred_element_type=f32).astype(bf16)
    hidden_back = jnp.einsum("ld,fd->lf", grads_all, down_mat, preferred_element_type=f32)
    gate_back = (hidden_back * up_pre * silu_slope(gate_pre)).astype(bf16)
    up_back = (hidden_back * jax.nn.silu(gate_pre)).astype(bf16)
    ffn_back_part = jnp.einsum(
        "lf,df->ld", gate_back, gate_mat, preferred_element_type=f32
    ) + jnp.einsum("lf,df->ld", up_back, up_mat, preferred_element_type=f32)
    ffn_back_low = jnp.concatenate([gate_back, up_back], axis=1)
    ffn_back_low = jnp.pad(ffn_back_low, ((0, 0), (0, ffn_total - 2 * ff_up)))
    ffn_jobs = [scatter_job(ffn_back_part.astype(bf16).reshape(size, rows, width), size)]
    fits = size <= 8
    (ffn_quarter_sum, down_wgrad), ffn_back = ffn_sums(
        ffn_low, ffn_back_low, hidden, grads_all, ffn_jobs * fits, size, 7
    )
    if not fits:
        ffn_back = together(ffn_jobs, size, 14, "ffn_sum")
    ffn_back = ffn_back[0][0]
    middle_part, ffn_gain_grad = norm_backward(ffn_back, middle, inv_ffn, gain_float[3])
    middle_back = out_grad[0].astype(f32) + middle_part
    branch_back = 0.5 * middle_back
    attn_part, attn_gain_grad = norm_backward(branch_back, attn_out, inv_attn, gain_float[1])
    mamba_part_back, mamba_gain_grad = norm_backward(
        branch_back, mamba_out, inv_mamba, gain_float[2]
    )
    attn_back = attn_part.astype(bf16)
    attn_wgrad = jnp.einsum("hl,ld->hd", attn_rows_t, attn_back, preferred_element_type=f32)
    attn_wgrad = jnp.pad(attn_wgrad.astype(bf16), ((0, 0), (0, attn_wide - width)))
    dout_t = jnp.einsum("hd,ld->hl", attn_mat, attn_back, preferred_element_type=f32).astype(bf16)
    (query_back_t, keyval_terms), ((mamba_back,), (attn_quarter,)) = (
        attention_backward(
            query_t,
            key_groups,
            keyvals_t[: KV * HD],
            value_groups,
            bias_t,
            log_totals,
            dout_t,
            [
                gather_job(mamba_part_back.astype(bf16), size),
                halve_job(attn_wgrad.reshape(size, depth, attn_wide)),
            ],
            size,
            8,
            PLAN_ATTEND_BACK,
        )
    )
    mamba_back = mamba_back.reshape(rows_all, width)
    mamba_wgrad = jnp.einsum("li,ld->id", mamba_rows, mamba_back, preferred_element_type=f32)
    mrows_back = jnp.einsum("ld,id->li", mamba_back, mamba_mat, preferred_element_type=f32)
    scan_back = mrows_back * gate_act
    side_back = mrows_back * scanned * silu_slope(gate_side)
    skip_grad = jnp.sum(scan_back * signal_float, axis=0)
    down_jobs = [scatter_job(down_part.reshape(size, rows, width), size)]
    (
        (step_back, carry_writes, read_write_back, decay_sums),
        ((ffn_home,), (attn_piece,), (mamba_share,), (down_share,), *down_out),
    ) = scan_backward(
        order,
        step_sizes,
        signal_float,
        scan_back,
        write_read,
        rate2,
        start_state,
        ends_all,
        size,
        [
            deliver_job(ffn_quarter_sum, size),
            scatter_job(attn_quarter, size),
            ctx_sum_job(mamba_wgrad.astype(bf16)),
            ctx_sum_job(down_wgrad),
        ]
        + down_jobs * fits,
        size,
        9,
        PLAN_BACKWARD,
    )
    if not fits:
        down_out = together(down_jobs, size, 15, "down_sum")
    result = middle + down_out[0][0]
    decay_grad = rate * jnp.sum(decay_sums, axis=(0, 1, 3))
    signal_back = scan_back * skip_float + step_sizes * carry_writes
    read_write_back = read_write_back[:, : 2 * NS]
    pre_back = (step_back * jax.nn.sigmoid(step_pre)).astype(bf16)
    step_wgrad = jnp.einsum("lr,li->ri", step_low, pre_back, preferred_element_type=f32)
    bias_grad = jnp.sum(pre_back.astype(f32), axis=0)
    rank_back = jnp.einsum("li,ri->lr", pre_back, step_mat, preferred_element_type=f32)
    select_part = jnp.concatenate([rank_back, read_write_back], axis=1).astype(bf16).T
    (select_back,), (attn_home,), (keyval_back,) = together(
        [
            sum_job(select_part, size),
            ctx_gather_job(attn_piece.astype(bf16)),
            halve_job(keyval_terms.astype(bf16)[None]),
        ],
        size,
        10,
        "select_back",
    )
    select_back = select_back.T
    select_wgrad = jnp.einsum("li,lk->ik", signal, select_back, preferred_element_type=f32)
    signal_back = signal_back + jnp.einsum(
        "lk,ik->li", select_back, select_mat, preferred_element_type=f32
    )
    conv_back = signal_back * silu_slope(conv_out)
    conv_blocks = conv_back.reshape(size, 2, half_rows, chan)
    taps_grad = jnp.stack(
        [
            jnp.sum(conv_blocks * padded[:, :, offset : offset + half_rows], axis=(0, 1, 2))
            for offset in range(CONV)
        ]
    )
    shift_grad = jnp.sum(conv_back, axis=0)
    padded_back = sum(
        (
            jnp.pad(
                taps_float[offset] * conv_blocks,
                ((0, 0), (0, 0), (offset, CONV - 1 - offset), (0, 0)),
            )
            for offset in range(CONV)
        )
    )
    tail_back = jnp.where(has_before[None, :, None, None], padded_back[:, :, : CONV - 1], 0.0)
    keyval_back_t = keyval_back.reshape(size, kv_cols, rows)
    qkv_back_t = jnp.concatenate([query_back_t.reshape(size, q_cols, rows), keyval_back_t], axis=1)
    pad_rows = up_to(q_cols + kv_cols, 8) - q_cols - kv_cols
    qkv_back_t = jnp.pad(qkv_back_t, ((0, 0), (0, pad_rows), (0, 0)))
    (tails_back_all,), (qkv_back,) = together(
        [ctx_gather_job(tail_back.astype(bf16).reshape(-1, chan)), exchange_job(qkv_back_t, size)],
        size,
        11,
        "edges_back",
    )
    qkv_back = qkv_back.transpose(0, 2, 1).reshape(rows_all, -1)
    qkv_back = jnp.pad(qkv_back, ((0, 0), (0, qkv_up - qkv_back.shape[1])))
    tails_back_all = in_deal_order(tails_back_all.reshape(n_ctx, size, 2, CONV - 1, chan))
    after_index = inverse[jnp.minimum(my_blocks + 1, blocks_all - 1)]
    has_after = my_blocks < blocks_all - 1
    incoming = jnp.where(
        has_after[None, :, None, None], of_blocks(tails_back_all, after_index).astype(f32), 0.0
    )
    mixer_back = padded_back[:, :, CONV - 1 :] + jnp.pad(
        incoming, ((0, 0), (0, 0), (half_rows - (CONV - 1), 0), (0, 0))
    )
    entry_back = jnp.concatenate([mixer_back.reshape(rows_all, chan), side_back], axis=1).astype(
        bf16
    )
    first_back = [qkv_back, entry_back]
    if first_total > qkv_up + 2 * chan_up:
        first_back.append(jnp.zeros((rows_all, first_total - qkv_up - 2 * chan_up), bf16))
    first_back = jnp.concatenate(first_back, axis=1)
    first_wgrad = column_grads(normed_all, first_back)
    gain_rows = jnp.stack(
        [jnp.zeros_like(attn_gain_grad), attn_gain_grad, mamba_gain_grad, ffn_gain_grad]
    )
    gain_rows = jnp.moveaxis(gain_rows.reshape(4, size, -1), 1, 0)
    small = jnp.concatenate(
        [
            taps_grad,
            shift_grad[None],
            bias_grad[None],
            skip_grad[None],
            decay_grad,
            step_wgrad,
            select_wgrad.T,
        ]
    )
    n_small = small.shape[0]
    small = jnp.pad(small, ((0, up_to(n_small, 64) - n_small), (0, 0))).astype(bf16)
    (gate_share, up_share), ((input_back,), (first_home,), (small,), (gain_share,)) = finish(
        first_wgrad.reshape(size, depth, first_total),
        first_back,
        first_mat,
        normed_all,
        gain_float[:1],
        gain_rows,
        small,
        ffn_home,
        (ffn_cuts, ffn_at),
        (gate_weight.shape, up_weight.shape),
        size,
        13,
    )
    stream_part, _ = norm_backward(input_back, stream, inv_in, gain_float[0])
    stream_back = middle_back + stream_part
    query_share, keyval_share, entry_share = unpack_columns(
        first_home,
        first_cuts,
        first_at,
        (query_weight.shape, keyval_weight.shape, mamba_in.shape),
        size,
    )
    chan = conv_bias.shape[0]
    vectors = small.reshape(-1, chan_up)[:, :chan].astype(f32)
    attn_share = jnp.moveaxis(attn_home, 0, 1).reshape(depth, attn_wide)[:, :width].astype(f32)
    mamba_share = mamba_share.reshape(-1, width)[:chan].astype(f32)
    down_share = down_share.reshape(-1, width)[:ff_cols].astype(f32)
    return (
        result.astype(bf16)[None],
        stream_back[None],
        gain_share,
        query_share,
        keyval_share,
        attn_share,
        entry_share,
        vectors[:CONV],
        vectors[CONV],
        vectors[CONV + 1],
        vectors[CONV + 2],
        vectors[CONV + 3 : CONV + 3 + NS],
        vectors[CONV + 3 + NS + RANK : n_small].T,
        vectors[CONV + 3 + NS : CONV + 3 + NS + RANK],
        mamba_share,
        gate_share,
        up_share,
        down_share,
    )


def solution(mesh):
    in_specs = (
        P("fsdp", "ctx", None),
        P("fsdp", "ctx", None),
        P("fsdp", None),
        P(),
        P(None, "fsdp"),
        P("fsdp", None),
        P("fsdp", None),
        P("fsdp", None),
        P("fsdp", None),
        P(None, "fsdp"),
        P("fsdp"),
        P("fsdp"),
        P("fsdp"),
        P(None, "fsdp"),
        P("fsdp", None),
        P(None, "fsdp"),
        P("fsdp", None),
        P("fsdp", None),
        P("fsdp", None),
        P("fsdp", None),
    )
    out_specs = (
        P("fsdp", "ctx", None),
        P("fsdp", "ctx", None),
        P(None, "fsdp"),
        P("fsdp", None),
        P("fsdp", None),
        P("fsdp", None),
        P("fsdp", None),
        P(None, "fsdp"),
        P("fsdp"),
        P("fsdp"),
        P("fsdp"),
        P(None, "fsdp"),
        P("fsdp", None),
        P(None, "fsdp"),
        P("fsdp", None),
        P("fsdp", None),
        P("fsdp", None),
        P("fsdp", None),
    )
    return jax.shard_map(
        on_device, mesh=mesh, in_specs=in_specs, out_specs=out_specs, check_vma=False
    )
```

```python
import functools
import math

import jax
import jax.numpy as jnp
from jax import lax
from jax.experimental import pallas as pl
from jax.experimental.pallas import tpu as pltpu
from jax.sharding import PartitionSpec as P

H = 25
KV = 5
HD = 64
INNER = 3200
NS = 16
RANK = 100
CONV = 4

EPS = 1e-06
score_scale = 0.125
MESH = pl.DeviceIdType.MESH
ANY = pl.BlockSpec(memory_space=pl.ANY)
VM = pl.BlockSpec(memory_space=pltpu.VMEM)
DMA = pltpu.SemaphoreType.DMA
f32 = jnp.float32
bf16 = jnp.bfloat16


def params(cid, vmem=None):
    return pltpu.CompilerParams(collective_id=cid, has_side_effects=True, vmem_limit_bytes=vmem)


def rcopy(src, dst, ssem, rsem, dev):
    return pltpu.make_async_remote_copy(
        src_ref=src, dst_ref=dst, send_sem=ssem, recv_sem=rsem, device_id=dev, device_id_type=MESH
    )


def norm_forward(values, gain):
    inverse = lax.rsqrt(jnp.mean(values * values, axis=-1, keepdims=True) + EPS)
    return (values * inverse * gain, inverse)


def norm_backward(grad, values, inverse, gain):
    normed = values * inverse
    gain_grad = jnp.sum(grad * normed, axis=0)
    scaled = grad * gain
    return (
        inverse * (scaled - normed * jnp.mean(scaled * normed, axis=-1, keepdims=True)),
        gain_grad,
    )


def silu_slope(values):
    sigma = jax.nn.sigmoid(values)
    return sigma * (1.0 + values * (1.0 - sigma))


def up_to(value, step):
    return (value + step - 1) // step * step


def pack_columns(refs, out, cuts, offsets, size):
    out[...] = jnp.zeros_like(out)
    for (which, first, cols), at in zip(cuts, offsets):
        for f in range(size):
            out[f, :, at : at + cols] = refs[which][:, first + f * cols : first + (f + 1) * cols]


def unpack_pieces(home, outs, cuts, offsets, size):
    for (which, first, cols), at in zip(cuts, offsets):
        for f in range(size):
            outs[which][:, first + f * cols : first + (f + 1) * cols] = home[
                f, :, at : at + cols
            ].astype(f32)


def unpack_columns(home, cuts, offsets, shapes, size):
    def kernel(h_ref, *outs):
        unpack_pieces(h_ref, outs, cuts, offsets, size)

    return pl.pallas_call(
        kernel,
        out_shape=[jax.ShapeDtypeStruct(shape, f32) for shape in shapes],
        in_specs=[VM],
        out_specs=[VM] * len(shapes),
        compiler_params=pltpu.CompilerParams(vmem_limit_bytes=60 << 20),
        name="unpack_columns",
    )(home)


class Job:
    def __init__(self, steps, ins, outs, scratch):
        self.steps, self.ins, self.outs, self.scratch = steps, ins, outs, scratch


class Place:
    def __init__(self, size):
        self.size, self.lanes = size, size // 2
        self.f, self.c = lax.axis_index("fsdp"), lax.axis_index("ctx")
        self.a, self.b = self.f // 2, lax.rem(self.f, 2)
        self.near = self.c + 1 - 2 * lax.rem(self.c, 2)
        self.far = lax.rem(self.c + 2, 4)
        self.other = lax.rem(self.near + 2, 4)

    def greet(self):
        bar = pltpu.get_barrier_semaphore()
        for d in range(1, self.size):
            peer = {"fsdp": lax.rem(self.f + d, self.size)}
            pl.semaphore_signal(bar, inc=1, device_id=peer, device_id_type=MESH)
        for peer in (self.near, self.far):
            pl.semaphore_signal(bar, inc=1, device_id={"ctx": peer}, device_id_type=MESH)
        pl.semaphore_wait(bar, self.size + 1)


def part(ref_list, jobs, field):
    out = []
    for job in jobs:
        count = len(getattr(job, field))
        out.append(ref_list[:count])
        ref_list = ref_list[count:]
    return out


class Moving:
    def __init__(self, live):
        self.live = live

    def step(self, which):
        if which < len(self.live) and self.live[which] is not None:
            try:
                next(self.live[which])
            except StopIteration:
                self.live[which] = None

    def drain(self):
        while any(item is not None for item in self.live):
            for which in range(len(self.live)):
                self.step(which)


def together(jobs, size, cid, name, order=()):
    n_in = sum(len(job.ins) for job in jobs)
    n_out = sum(len(job.outs) for job in jobs)

    def kernel(*refs):
        place = Place(size)
        place.greet()
        ins = part(refs[:n_in], jobs, "ins")
        outs = part(refs[n_in : n_in + n_out], jobs, "outs")
        scratch = part(refs[n_in + n_out :], jobs, "scratch")
        moving = Moving(
            [job.steps(place, i, o, s) for job, i, o, s in zip(jobs, ins, outs, scratch)]
        )
        for which in order:
            moving.step(which)
        moving.drain()

    got = pl.pallas_call(
        kernel,
        out_shape=[shape for job in jobs for shape, _ in job.outs],
        in_specs=[spec for job in jobs for _, spec in job.ins],
        out_specs=[spec for job in jobs for _, spec in job.outs],
        scratch_shapes=[item for job in jobs for item in job.scratch],
        compiler_params=params(cid, 60 << 20),
        name=name,
    )(*[array for job in jobs for array, _ in job.ins])
    return part(got, jobs, "outs")


def like(shape, dtype):
    return jax.ShapeDtypeStruct(shape, dtype)


def gather_job(x, size, shared=False):
    rows, cols = x.shape
    lanes = size // 2

    def run(p, ins, outs, scratch):
        (x_ref,), (o_ref,) = ins, outs
        lsem, up_s, up_r, dn_s, dn_r, px_s, px_r = scratch[:7]

        def view(i, q):
            return o_ref.at[i, :, column_block(q, cols // 4)]

        def piece(origin, b):
            i = 2 * origin + b
            return view(i, p.c) if shared else o_ref.at[i]

        def own():
            return x_ref.at[:, column_block(p.c, cols // 4)] if shared else x_ref

        share = Share(p, view, size, scratch[7:]) if shared else None

        def local():
            return pltpu.make_async_copy(own(), piece(p.a, p.b), lsem)

        def up(s):
            src = own() if s == 0 else piece(p.a - s, p.b)
            dev = {"fsdp": 2 * (p.a + 1) + p.b}
            return rcopy(src, piece(p.a - s, p.b), up_s.at[s], up_r.at[s], dev)

        def down(s):
            src = own() if s == 0 else piece(p.a + s, p.b)
            dev = {"fsdp": 2 * (p.a - 1) + p.b}
            return rcopy(src, piece(p.a + s, p.b), dn_s.at[s], dn_r.at[s], dev)

        def across(origin, src=None):
            src = piece(origin, p.b) if src is None else src
            dev = {"fsdp": 2 * p.a + 1 - p.b}
            return rcopy(src, piece(origin, p.b), px_s.at[origin], px_r.at[origin], dev)

        def came(ref, sem, dev):
            rcopy(ref, ref, sem, sem, dev).wait_recv()

        def arrived(origin, b, src=None):
            if shared:
                share.send(2 * origin + b, src)

        local().start()

        @pl.when(p.a < lanes - 1)
        def _():
            up(0).start()

        @pl.when(p.a > 0)
        def _():
            down(0).start()

        across(p.a, own()).start()
        if shared:
            arrived(p.a, p.b, own())
        yield
        for s in range(lanes - 1):
            @pl.when(p.a - 1 - s >= 0)
            def _():
                came(piece(p.a - 1 - s, p.b), up_r.at[s], {"fsdp": 2 * (p.a - 1) + p.b})

                @pl.when(p.a < lanes - 1)
                def _():
                    up(s + 1).start()

                across(p.a - 1 - s).start()
                arrived(p.a - 1 - s, p.b)

            @pl.when(p.a + 1 + s <= lanes - 1)
            def _():
                came(piece(p.a + 1 + s, p.b), dn_r.at[s], {"fsdp": 2 * (p.a + 1) + p.b})

                @pl.when(p.a > 0)
                def _():
                    down(s + 1).start()

                across(p.a + 1 + s).start()
                arrived(p.a + 1 + s, p.b)

            yield
        local().wait()
        for origin in range(lanes):
            came(piece(origin, 1 - p.b), px_r.at[origin], {"fsdp": 2 * p.a + 1 - p.b})
            arrived(origin, 1 - p.b)
        if shared:
            yield
            for i in range(size):
                share.forward(i)
            yield
            share.finish()
        for s in range(lanes - 1):
            @pl.when((p.a - s >= 0) & (p.a < lanes - 1))
            def _():
                up(s).wait_send()

            @pl.when((p.a + s <= lanes - 1) & (p.a > 0))
            def _():
                down(s).wait_send()

        for origin in range(lanes):
            across(origin).wait_send()

    return Job(
        run,
        [(x, ANY)],
        [(like((size, rows, cols), x.dtype), ANY)],
        [DMA] + [DMA((lanes,))] * 6 + (share_sems(size) if shared else []),
    )


def add_blocks(out, terms, dtype, rows):
    if rows % 16:
        total = terms[0][...].astype(f32)
        for ref in terms[1:]:
            total += ref[...].astype(f32)
        out[...] = total.astype(dtype)
        return
    step = 32 if rows % 32 == 0 else 16

    def body(i, carry):
        at = pl.ds(pl.multiple_of(i * step, step), step)
        total = terms[0][at, :].astype(f32)
        for ref in terms[1:]:
            total += ref[at, :].astype(f32)
        out[at, :] = total.astype(dtype)
        return carry

    lax.fori_loop(0, rows // step, body, 0)


def scatter_job(partial, size, held=None):
    rows, cols = partial.shape[1:]
    lanes = size // 2

    def run(p, ins, outs, scratch):
        (o_ref,) = outs
        p_ref = held[0] if held is not None else ins[0]
        xbuf, upb, dnb, up_s, up_r, dn_s, dn_r, px_s, px_r = scratch[:9]

        def own(dest):
            return p_ref.at[2 * dest + p.b] if held is not None else scratch[9].at[dest]

        def local(dest):
            return pltpu.make_async_copy(
                p_ref.at[2 * dest + p.b], scratch[9].at[dest], scratch[10].at[dest]
            )

        def across(dest):
            src = p_ref.at[2 * dest + 1 - p.b]
            dev = {"fsdp": 2 * p.a + 1 - p.b}
            return rcopy(src, xbuf.at[dest], px_s.at[dest], px_r.at[dest], dev)

        def up(dest):
            dev = {"fsdp": 2 * (p.a + 1) + p.b}
            return rcopy(xbuf.at[dest], upb.at[dest], up_s.at[dest], up_r.at[dest], dev)

        def down(dest):
            dev = {"fsdp": 2 * (p.a - 1) + p.b}
            return rcopy(xbuf.at[dest], dnb.at[dest], dn_s.at[dest], dn_r.at[dest], dev)

        def add_in(dest, extra):
            terms = [xbuf.at[dest], own(dest)]
            if extra is not None:
                terms.append(extra.at[dest])
            add_blocks(xbuf.at[dest], terms, bf16, rows)

        if held is None:
            for dest in range(lanes):
                local(dest).start()
        for d in range(lanes - 1, -1, -1):
            @pl.when(p.a + d <= lanes - 1)
            def _():
                across(p.a + d).start()

            if d > 0:
                @pl.when(p.a - d >= 0)
                def _():
                    across(p.a - d).start()

        yield
        if held is None:
            for dest in range(lanes):
                local(dest).wait()
        for d in range(lanes - 1, 0, -1):
            @pl.when(p.a + d <= lanes - 1)
            def _():
                across(p.a + d).wait_recv()

                @pl.when(p.a > 0)
                def _():
                    up(p.a + d).wait_recv()
                    add_in(p.a + d, upb)

                @pl.when(p.a == 0)
                def _():
                    add_in(p.a + d, None)

                up(p.a + d).start()

            @pl.when(p.a - d >= 0)
            def _():
                across(p.a - d).wait_recv()

                @pl.when(p.a < lanes - 1)
                def _():
                    down(p.a - d).wait_recv()
                    add_in(p.a - d, dnb)

                @pl.when(p.a == lanes - 1)
                def _():
                    add_in(p.a - d, None)

                down(p.a - d).start()

            yield
        across(p.a).wait_recv()
        terms = [xbuf.at[p.a], own(p.a)]

        @pl.when(p.a == 0)
        def _():
            down(p.a).wait_recv()
            add_blocks(o_ref, terms + [dnb.at[p.a]], f32, rows)

        @pl.when(p.a == lanes - 1)
        def _():
            up(p.a).wait_recv()
            add_blocks(o_ref, terms + [upb.at[p.a]], f32, rows)

        @pl.when((p.a > 0) & (p.a < lanes - 1))
        def _():
            up(p.a).wait_recv()
            down(p.a).wait_recv()
            add_blocks(o_ref, terms + [upb.at[p.a], dnb.at[p.a]], f32, rows)

        for dest in range(lanes):
            across(dest).wait_send()

        for d in range(lanes - 1, 0, -1):
            @pl.when(p.a + d <= lanes - 1)
            def _():
                up(p.a + d).wait_send()

            @pl.when(p.a - d >= 0)
            def _():
                down(p.a - d).wait_send()

    return Job(
        run,
        [(partial, ANY)] if held is None else [],
        [(like((rows, cols), f32), VM)],
        [pltpu.VMEM((lanes, rows, cols), bf16)] * 3
        + [DMA((lanes,))] * 6
        + ([pltpu.VMEM((lanes, rows, cols), bf16), DMA((lanes,))] if held is None else []),
    )


def column_block(of, quarter):
    return pl.ds(pl.multiple_of(of * quarter, 128), quarter)


class Share:
    def __init__(self, p, view, count, sems):
        self.p, self.view, self.count = p, view, count
        self.fs, self.fr, self.ns, self.nr, self.hs, self.hr = sems

    def far(self, d, q, src=None):
        ref = self.view(d, q)
        src = ref if src is None else src
        return rcopy(src, ref, self.fs.at[d], self.fr.at[d], {"ctx": self.p.far})

    def near(self, d, q, src=None):
        ref = self.view(d, q)
        src = ref if src is None else src
        return rcopy(src, ref, self.ns.at[d], self.nr.at[d], {"ctx": self.p.near})

    def onward(self, d, q):
        ref = self.view(d, q)
        return rcopy(ref, ref, self.hs.at[d], self.hr.at[d], {"ctx": self.p.near})

    def send(self, d, src=None):
        self.far(d, self.p.c, src).start()
        self.near(d, self.p.c, src).start()

    def forward(self, d):
        self.far(d, self.p.far).wait_recv()
        self.onward(d, self.p.far).start()

    def finish(self):
        p = self.p
        for d in range(self.count):
            self.far(d, p.c).wait_send()
            self.near(d, p.c).wait_send()
            self.near(d, p.near).wait_recv()
            self.onward(d, p.far).wait_send()
            self.onward(d, p.other).wait_recv()


def share_sems(count):
    return [DMA((count,))] * 6


def move_job(packed, size, held=None):
    depth, total = packed.shape[-2:]
    quarter = total // 4

    def run(p, ins, outs, scratch):
        (w_ref,) = outs
        p_ref = held[0] if held is not None else ins[0]
        lsem, ws, wr = scratch[:3]

        def source(to):
            return p_ref.at[to, :, column_block(p.c, quarter)]

        def view(d, q):
            return w_ref.at[lax.rem(p.f - d + size, size), :, column_block(q, quarter)]

        def local():
            return pltpu.make_async_copy(source(p.f), view(0, p.c), lsem)

        def move(d):
            to = lax.rem(p.f + d, size)
            return rcopy(source(to), view(0, p.c), ws.at[d], wr.at[d], {"fsdp": to})

        def came(d):
            ref = view(d, p.c)
            rcopy(ref, ref, ws.at[d], wr.at[d], {"fsdp": lax.rem(p.f + d, size)}).wait_recv()

        share = Share(p, view, size, scratch[3:])
        local().start()
        for d in range(1, size):
            move(d).start()
        share.send(0, source(p.f))
        yield
        for d in range(1, size):
            came(d)
            share.send(d)
            if d % 2 == 0:
                yield
        for d in range(size):
            share.forward(d)
            if d % 4 == 3:
                yield
        local().wait()
        share.finish()
        for d in range(1, size):
            move(d).wait_send()

    return Job(
        run,
        [(packed, ANY)] if held is None else [],
        [(like((size, depth, total), packed.dtype), ANY)],
        [DMA, DMA((size,)), DMA((size,))] + share_sems(size),
    )


def spread_job(x, size):
    def run(p, ins, outs, scratch):
        (x_ref,), (o_ref,) = ins, outs
        lsem, ss, rs = scratch

        def copy(d):
            to = {"fsdp": lax.rem(p.f + d, size)}
            return rcopy(x_ref, o_ref.at[p.f], ss.at[d], rs.at[d], to)

        def local():
            return pltpu.make_async_copy(x_ref, o_ref.at[p.f], lsem)

        local().start()
        for d in range(1, size):
            copy(d).start()
        yield
        local().wait()
        for d in range(1, size):
            copy(d).wait()

    return Job(
        run,
        [(x, ANY)],
        [(like((size,) + x.shape, x.dtype), ANY)],
        [DMA, DMA((size,)), DMA((size,))],
    )


def exchange_job(x, size, rows=None):
    blocks = x.shape if rows is None else (size, rows, x.shape[1] // size)

    def run(p, ins, outs, scratch):
        (x_ref,), (o_ref,) = ins, outs
        lsem, ss, rs = scratch

        def block(to):
            if rows is None:
                return x_ref.at[to]
            return x_ref.at[:rows, column_block(to, blocks[2])]

        def copy(d):
            to = lax.rem(p.f + d, size)
            return rcopy(block(to), o_ref.at[p.f], ss.at[d], rs.at[d], {"fsdp": to})

        def local():
            return pltpu.make_async_copy(block(p.f), o_ref.at[p.f], lsem)

        local().start()
        for d in range(1, size):
            copy(d).start()
        yield
        local().wait()
        for d in range(1, size):
            copy(d).wait()

    return Job(
        run, [(x, ANY)], [(like(blocks, x.dtype), ANY)], [DMA, DMA((size,)), DMA((size,))]
    )


def ctx_gather_job(x):
    def run(p, ins, outs, scratch):
        (x_ref,), (o_ref,) = ins, outs
        share = Share(p, lambda d, q: o_ref.at[q], 1, scratch[1:])

        def local():
            return pltpu.make_async_copy(x_ref, o_ref.at[p.c], scratch[0])

        def first(to, ss, rs):
            return rcopy(x_ref, o_ref.at[p.c], ss.at[0], rs.at[0], {"ctx": to})

        local().start()
        first(p.far, share.fs, share.fr).start()
        first(p.near, share.ns, share.nr).start()
        yield
        share.forward(0)
        yield
        local().wait()
        share.finish()

    return Job(
        run, [(x, ANY)], [(like((4,) + x.shape, x.dtype), ANY)], [DMA] + share_sems(1)
    )


class Halve:
    def __init__(self, p, source, bufs, sems, here=False):
        self.p, self.source, self.here = p, source, here
        self.own, self.got, self.away, self.total = bufs
        self.ls, self.ns, self.nr, self.fs, self.fr = sems
        self.count, self.rows = self.total.shape[:2]

    def local(self, i):
        q = self.p.c if i == 0 else self.p.far
        return pltpu.make_async_copy(self.source(q), self.own.at[i], self.ls.at[i])

    def mine_of(self, i, j):
        if self.here:
            return self.source(self.p.c if i == 0 else self.p.far).at[j]
        return self.own.at[i, j]

    def to_near(self, i):
        q = self.p.near if i == 0 else self.p.other
        return rcopy(
            self.source(q), self.got.at[i], self.ns.at[i], self.nr.at[i], {"ctx": self.p.near}
        )

    def index(self, k):
        return lax.rem(self.p.f + k, self.count) if self.count == self.p.size else k

    def to_far(self, k):
        j = self.index(k)
        return rcopy(
            self.own.at[1, j], self.away.at[j], self.fs.at[k], self.fr.at[k], {"ctx": self.p.far}
        )

    def start(self):
        if not self.here:
            for i in (1, 0):
                self.local(i).start()
        for i in (1, 0):
            self.to_near(i).start()

    def send(self):
        if not self.here:
            self.local(1).wait()
        self.to_near(1).wait_recv()
        for k in range(self.count):
            j = self.index(k)
            terms = [self.mine_of(1, j), self.got.at[1, j]]
            add_blocks(self.own.at[1, j], terms, bf16, self.rows)
            self.to_far(k).start()

    def mine(self):
        if not self.here:
            self.local(0).wait()
        self.to_near(0).wait_recv()

    def block(self, k):
        self.to_far(k).wait_recv()
        j = self.index(k)
        add_blocks(
            self.total.at[j],
            [self.mine_of(0, j), self.got.at[0, j], self.away.at[j]],
            bf16,
            self.rows,
        )

    def finish(self):
        for i in range(2):
            self.to_near(i).wait_send()
        for j in range(self.count):
            self.to_far(j).wait_send()


def halve_scratch(count, rows, cols, total=True):
    return [
        pltpu.VMEM((2, count, rows, cols), bf16),
        pltpu.VMEM((2, count, rows, cols), bf16),
        pltpu.VMEM((count, rows, cols), bf16),
    ] + [pltpu.VMEM((count, rows, cols), bf16)] * total + [
        DMA((2,)),
        DMA((2,)),
        DMA((2,)),
        DMA((count,)),
        DMA((count,)),
    ]


def halve_job(x, columns=True):
    n, rows, cols = x.shape
    shape = (n, rows, cols // 4) if columns else (n // 4, rows, cols)

    def run(p, ins, outs, scratch):
        (x_ref,), (o_ref,) = ins, outs

        def source(q):
            if columns:
                return x_ref.at[:, :, column_block(q, shape[2])]
            return x_ref.at[pl.ds(q * shape[0], shape[0])]

        halve = Halve(p, source, list(scratch[:3]) + [o_ref], scratch[3:])
        halve.start()
        yield
        halve.send()
        yield
        halve.mine()
        for j in range(shape[0]):
            halve.block(j)
            if j % 2 == 1:
                yield
        halve.finish()

    return Job(run, [(x, ANY)], [(like(shape, bf16), VM)], halve_scratch(*shape, total=False))


def home_job(wgrad, size):
    _, depth, total = wgrad.shape
    quarter = total // 4

    def run(p, ins, outs, scratch):
        (w_ref,), (h_ref,) = ins, outs
        halve = Halve(
            p, lambda q: w_ref.at[:, :, column_block(q, quarter)], scratch[:4], scratch[4:9]
        )
        lsem, ws, wr = scratch[9:12]

        def view(d, q):
            return h_ref.at[lax.rem(p.f - d + size, size), :, column_block(q, quarter)]

        def local():
            return pltpu.make_async_copy(halve.total.at[p.f], view(0, p.c), lsem)

        def move(d):
            to = lax.rem(p.f + d, size)
            return rcopy(halve.total.at[to], view(0, p.c), ws.at[d], wr.at[d], {"fsdp": to})

        def came(d):
            ref = view(d, p.c)
            rcopy(ref, ref, ws.at[d], wr.at[d], {"fsdp": lax.rem(p.f + d, size)}).wait_recv()

        share = Share(p, view, size, scratch[12:])
        halve.start()
        yield
        halve.send()
        yield
        halve.mine()
        for k in range(size):
            halve.block(k)
            if k == 0:
                local().start()
                share.send(0, halve.total.at[p.f])
            else:
                move(k).start()
            if k % 2 == 1:
                yield
        for d in range(1, size):
            came(d)
            share.send(d)
            if d % 2 == 0:
                yield
        for d in range(size):
            share.forward(d)
            if d % 4 == 3:
                yield
        local().wait()
        share.finish()
        halve.finish()
        for d in range(1, size):
            move(d).wait_send()

    return Job(
        run,
        [(wgrad, ANY)],
        [(like((size, depth, total), bf16), ANY)],
        halve_scratch(size, depth, quarter)
        + [DMA, DMA((size,)), DMA((size,))]
        + share_sems(size),
    )


def deliver_job(piece, size):
    _, depth, quarter = piece.shape

    def run(p, ins, outs, scratch):
        (x_ref,), (h_ref,) = ins, outs
        lsem, ws, wr = scratch[:3]

        def view(d, q):
            return h_ref.at[lax.rem(p.f - d + size, size), :, column_block(q, quarter)]

        def local():
            return pltpu.make_async_copy(x_ref.at[p.f], view(0, p.c), lsem)

        def move(d):
            to = lax.rem(p.f + d, size)
            return rcopy(x_ref.at[to], view(0, p.c), ws.at[d], wr.at[d], {"fsdp": to})

        def came(d):
            ref = view(d, p.c)
            rcopy(ref, ref, ws.at[d], wr.at[d], {"fsdp": lax.rem(p.f + d, size)}).wait_recv()

        share = Share(p, view, size, scratch[3:])
        local().start()
        for d in range(1, size):
            move(d).start()
        share.send(0, x_ref.at[p.f])
        yield
        for d in range(1, size):
            came(d)
            share.send(d)
            if d % 4 == 3:
                yield
        for d in range(size):
            share.forward(d)
            if d % 4 == 3:
                yield
        local().wait()
        share.finish()
        for d in range(1, size):
            move(d).wait_send()

    return Job(
        run,
        [(piece, ANY)],
        [(like((size, depth, 4 * quarter), bf16), ANY)],
        [DMA, DMA((size,)), DMA((size,))] + share_sems(size),
    )


def ctx_sum_job(x, used=None):
    rows, cols = (x.shape[0] if used is None else used) // 4, x.shape[1]
    x = x[None]

    def run(p, ins, outs, scratch):
        (x_ref,), (o_ref,) = ins, outs
        def source(q):
            return x_ref.at[:, pl.ds(pl.multiple_of(q * rows, 16), rows)]

        halve = Halve(p, source, scratch[:4], scratch[4:9])
        share = Share(p, lambda d, q: o_ref.at[q], 1, scratch[10:])
        halve.start()
        yield
        halve.send()
        yield
        halve.mine()
        halve.block(0)
        share.send(0, halve.total.at[0])

        def local():
            return pltpu.make_async_copy(halve.total.at[0], o_ref.at[p.c], scratch[9])

        local().start()
        yield
        share.forward(0)
        yield
        local().wait()
        share.finish()
        halve.finish()

    return Job(
        run,
        [(x, ANY)],
        [(like((4, rows, cols), bf16), ANY)],
        halve_scratch(1, rows, cols) + [DMA] + share_sems(1),
    )


def sum_job(partial, size):
    rows, tokens = partial.shape[0], partial.shape[1] // size

    def run(p, ins, outs, scratch):
        (p_ref,), (o_ref,) = ins, outs
        buf, ss, rs, gs, gr = scratch

        def at(i):
            return pl.ds(pl.multiple_of(i * tokens, 128), tokens)

        def first(d):
            to = lax.rem(p.f + d, size)
            return rcopy(p_ref.at[:, at(to)], buf.at[d], ss.at[d], rs.at[d], {"fsdp": to})

        def second(d):
            to = lax.rem(p.f + d, size)
            ref = o_ref.at[:, at(p.f)]
            return rcopy(ref, ref, gs.at[d], gr.at[d], {"fsdp": to})

        def came(d):
            ref = o_ref.at[:, at(lax.rem(p.f - d + size, size))]
            rcopy(ref, ref, gs.at[d], gr.at[d], {"fsdp": lax.rem(p.f + d, size)}).wait_recv()

        for d in range(1, size):
            first(d).start()
        yield
        total = p_ref[:, at(p.f)].astype(f32)
        for d in range(1, size):
            first(d).wait_recv()
            total += buf[d].astype(f32)
        o_ref[:, at(p.f)] = total.astype(bf16)
        for d in range(1, size):
            second(d).start()
        yield
        for d in range(1, size):
            came(d)
        for d in range(1, size):
            first(d).wait_send()
            second(d).wait_send()

    return Job(
        run,
        [(partial, VM)],
        [(like(partial.shape, bf16), VM)],
        [pltpu.VMEM((size, rows, tokens), bf16)] + [DMA((size,))] * 4,
    )


def all_sum_job(x, size, held):
    rows, cols = x.shape[1:]

    def run(p, ins, outs, scratch):
        (o_ref,), x_ref = outs, held[0]
        buf, mid, far, ss, rs, ts, tr = scratch

        def copy(d):
            to = lax.rem(p.f + d, size)
            return rcopy(x_ref.at[to], buf.at[d], ss.at[d], rs.at[d], {"fsdp": to})

        def swap(i, to):
            return rcopy(mid.at[i], far.at[i], ts.at[i], tr.at[i], {"ctx": to})

        for d in range(1, size):
            copy(d).start()
        yield
        total = x_ref[p.f]
        for d in range(1, size):
            copy(d).wait_recv()
            total += buf[d]
        mid[0] = total
        swap(0, p.near).start()
        yield
        swap(0, p.near).wait_recv()
        mid[1] = mid[0] + far[0]
        swap(1, p.far).start()
        yield
        swap(1, p.far).wait_recv()
        o_ref[...] = mid[1] + far[1]
        for d in range(1, size):
            copy(d).wait_send()
        swap(0, p.near).wait_send()
        swap(1, p.far).wait_send()

    return Job(
        run,
        [],
        [(like((rows, cols), f32), VM)],
        [pltpu.VMEM((size, rows, cols), f32)]
        + [pltpu.VMEM((2, rows, cols), f32)] * 2
        + [DMA((size,)), DMA((size,)), DMA((2,)), DMA((2,))],
    )


UNROLL = 8
LN2 = 0.6931471805599453


def steps(length, body, init):
    count = UNROLL if length % UNROLL == 0 else 1

    def some(i, carry):
        for j in range(count):
            carry = body(i * count + j, carry)
        return carry

    return lax.fori_loop(0, length // count, some, init)


class Product:
    def __init__(self, left, right, size, transposed=False):
        rows_all = left.shape[0]
        width = right.shape[0 if transposed else 1]
        self.size, self.rows, self.transposed = size, rows_all // size, transposed
        self.shape = like((size, self.rows, width), bf16)
        self.ins = [(left, VM), (right, VM)]
        self.scratch = [pltpu.VMEM(self.shape.shape, bf16)]
        self.held = []

    def stages(self, p, left, right, out, also=None):
        self.held.append(out)
        contract = (((1,), (1 if self.transposed else 0,)), ((), ()))

        def block(i):
            at = pl.ds(pl.multiple_of(i * self.rows, self.rows), self.rows)
            got = lax.dot_general(
                left[at, :], right[...], contract, preferred_element_type=f32
            ).astype(bf16)
            out[i] = got
            if also is not None:
                also(at, got)

        def partner(k):
            block(2 * k + 1 - p.b)

        def own(k):
            block(2 * k + p.b)

        return [(self.size // 2, partner), (self.size // 2, own)]


class Scan:
    def __init__(self, streams, length, chan):
        self.width = math.gcd(streams, 8)
        self.groups, self.tiles, self.length = streams // self.width, chan // 128, length
        self.pieces = 2 * self.groups * self.tiles

    def piece(self, i):
        tile = lax.rem(i, self.tiles)
        rest = i // self.tiles
        return lax.rem(rest, self.groups), rest // self.groups, tile

    def lanes(self, tile):
        return pl.ds(pl.multiple_of(tile * 128, 128), 128)

    def rows(self, group, block, o):
        first = group * (self.width * 2 * self.length) + block * self.length + o
        return pl.ds(first, self.width, stride=2 * self.length)

    def spread(self, wr, group, block, out, column):
        def body(o, carry):
            values = wr[self.rows(group, block, o), :]
            for n in range(NS):
                out[o, n] = jnp.broadcast_to(
                    values[:, column + n : column + n + 1], (self.width, 128)
                )
            return carry

        steps(self.length, body, 0)

    def tiled(self):
        return pltpu.VMEM((self.tiles, self.groups * self.width * 2 * self.length, 128), f32)

    def tile_copies(self, flat, tiled, sems, out=False):
        copies = []
        for t in range(self.tiles):
            there = flat.at[:, t * 128 : (t + 1) * 128]
            pair = (tiled.at[t], there) if out else (there, tiled.at[t])
            copies.append(pltpu.make_async_copy(*pair, sems.at[t]))
        return copies

    def zero(self):
        return jnp.zeros((self.width, 128), f32)

    def link(self, order, b, ends, group, lanes, rates):
        at = order[b]
        total = ends[at, group, NS, :, lanes].astype(f32)
        return at, [jnp.exp2(total * rate) for rate in rates]

    def link_shape(self, blocks, chan, extra):
        return (blocks, self.groups, NS + extra, self.width, chan)


def hosted(loops, jobs, size, cid, name, ins, outs, scratch, plan):
    n_in, n_out = len(ins), len(outs)
    job_in = sum(len(job.ins) for job in jobs)
    job_out = sum(len(job.outs) for job in jobs)

    def kernel(*refs):
        place = Place(size)
        place.greet()
        own_in, refs = refs[:n_in], refs[n_in:]
        ins_, refs = part(refs[:job_in], jobs, "ins"), refs[job_in:]
        own_out, refs = refs[:n_out], refs[n_out:]
        outs_, refs = part(refs[:job_out], jobs, "outs"), refs[job_out:]
        own_scratch, refs = refs[: len(scratch)], refs[len(scratch) :]
        scratch_ = part(refs, jobs, "scratch")
        moving = Moving(
            [job.steps(place, i, o, s) for job, i, o, s in zip(jobs, ins_, outs_, scratch_)]
        )
        for at, stage in enumerate(loops(place, own_in, own_out, own_scratch)):
            for which in plan.get(at, ()):
                moving.step(which)
            if callable(stage):
                stage()
                continue
            count, body = stage

            def whole(i, carry):
                body(i)
                for k in range(count):
                    if plan.get((at, k)):
                        @pl.when(i == k)
                        def _():
                            for which in plan[at, k]:
                                moving.step(which)

                return carry

            lax.fori_loop(0, count, whole, 0)
        for which in plan.get("end", ()):
            moving.step(which)
        moving.drain()

    got = pl.pallas_call(
        kernel,
        out_shape=[shape for shape, _ in outs] + [shape for job in jobs for shape, _ in job.outs],
        in_specs=[spec for _, spec in ins] + [spec for job in jobs for _, spec in job.ins],
        out_specs=[spec for _, spec in outs] + [spec for job in jobs for _, spec in job.outs],
        scratch_shapes=list(scratch) + [item for job in jobs for item in job.scratch],
        compiler_params=params(cid, 63 << 20),
        name=name,
    )(*[array for array, _ in ins], *[array for job in jobs for array, _ in job.ins])
    return got[:n_out], part(got[n_out:], jobs, "outs")


SM = pl.BlockSpec(memory_space=pltpu.SMEM)


def scan_forward(order, dt, x, wr, rate2, streams, jobs, size, cid, plan):
    chan = dt.shape[1]
    scan = Scan(streams, dt.shape[0] // streams // 2, chan)
    blocks = order.shape[0] - 2
    length = scan.length

    def loops(p, ins, outs, scratch):
        order_ref, dt_flat, x_flat, wr_ref, rate_ref = ins
        y_flat, s_ref, ends_ref = outs
        wb, rb, dt_ref, x_ref, y_ref, dt_sem, x_sem, y_sem = scratch[:8]
        share = Share(p, lambda d, q: ends_ref.at[pl.ds(2 * q, 2)], 1, scratch[8:])

        def load():
            copies = scan.tile_copies(dt_flat, dt_ref, dt_sem)
            copies += scan.tile_copies(x_flat, x_ref, x_sem)
            for copy in copies:
                copy.start()
            for copy in copies:
                copy.wait()

        def store():
            copies = scan.tile_copies(y_flat, y_ref, y_sem, True)
            for copy in copies:
                copy.start()
            for copy in copies:
                copy.wait()

        def ends(i):
            group, block, tile = scan.piece(i)
            lanes = scan.lanes(tile)

            @pl.when(tile == 0)
            def _():
                scan.spread(wr_ref, group, block, wb, 0)

            rates = [rate_ref[n : n + 1, lanes] for n in range(NS)]

            def body(o, carry):
                total, states = carry
                at = scan.rows(group, block, o)
                step = dt_ref[tile, at, :]
                pushed = step * x_ref[tile, at, :]
                states = tuple(
                    jnp.exp2(step * rates[n]) * states[n] + wb[o, n] * pushed for n in range(NS)
                )
                return (total + step, states)

            total, states = steps(length, body, (scan.zero(), (scan.zero(),) * NS))
            mine = 2 * p.c + block
            for n in range(NS):
                ends_ref[mine, group, n, :, lanes] = states[n].astype(bf16)
            ends_ref[mine, group, NS, :, lanes] = total.astype(bf16)

        def send():
            share.send(0)

        def arrive():
            share.forward(0)
            share.finish()

        def forward(i):
            group, block, tile = scan.piece(i)
            lanes = scan.lanes(tile)

            @pl.when(tile == 0)
            def _():
                scan.spread(wr_ref, group, block, wb, 0)
                scan.spread(wr_ref, group, block, rb, NS)

            rates = [rate_ref[n : n + 1, lanes] for n in range(NS)]
            mine = order_ref[blocks + block]

            def link(b, states):
                at, decays = scan.link(order_ref, b, ends_ref, group, lanes, rates)
                return tuple(
                    jnp.where(
                        b < mine,
                        decays[n] * states[n] + ends_ref[at, group, n, :, lanes].astype(f32),
                        states[n],
                    )
                    for n in range(NS)
                )

            states = lax.fori_loop(0, blocks - 1, link, (scan.zero(),) * NS)
            for n in range(NS):
                s_ref[block, group, n, :, lanes] = states[n]

            def body(o, states):
                at = scan.rows(group, block, o)
                step = dt_ref[tile, at, :]
                pushed = step * x_ref[tile, at, :]
                states = tuple(
                    jnp.exp2(step * rates[n]) * states[n] + wb[o, n] * pushed for n in range(NS)
                )
                total = [rb[o, n] * states[n] for n in range(NS)]
                while len(total) > 1:
                    total = [total[j] + total[j + 1] for j in range(0, len(total), 2)]
                y_ref[tile, at, :] = total[0]
                return states

            steps(length, body, states)

        return [load, (scan.pieces, ends), send, arrive, (scan.pieces, forward), store]

    spread = pltpu.VMEM((length, NS, scan.width, 128), f32)
    return hosted(
        loops,
        jobs,
        size,
        cid,
        "scan_forward",
        [(order, SM), (dt, ANY), (x, ANY), (wr, VM), (rate2, VM)],
        [
            (like(dt.shape, f32), ANY),
            (like(scan.link_shape(2, chan, 0), f32), VM),
            (like(scan.link_shape(blocks, chan, 1), bf16), VM),
        ],
        [spread, spread] + [scan.tiled()] * 3 + [DMA((scan.tiles,))] * 3 + share_sems(1),
        plan,
    )


def scan_backward(
    order, dt, x, g, wr, rate2, starts, ends, product, streams, jobs, size, cid, plan
):
    chan = dt.shape[1]
    scan = Scan(streams, dt.shape[0] // streams // 2, chan)
    blocks = order.shape[0] - 2
    length, width = scan.length, scan.width

    def loops(p, ins, outs, scratch):
        order_ref, dt_flat, x_flat, g_flat, wr_ref, rate_ref, start_ref, ends_ref = ins[:8]
        sb_flat, cw_flat, wrb_ref, dec_ref = outs
        backs_ref, wb, rb, kept, decays, wparts, rparts, sums = scratch[:8]
        dt_ref, x_ref, g_ref, sb_ref, cw_ref, dt_sem, x_sem, g_sem, sb_sem, cw_sem = scratch[8:18]
        share = Share(p, lambda d, q: backs_ref.at[pl.ds(2 * q, 2)], 1, scratch[18:24])
        extra = product.stages(p, *ins[8:], scratch[24]) if product else []

        def load():
            copies = scan.tile_copies(dt_flat, dt_ref, dt_sem)
            copies += scan.tile_copies(x_flat, x_ref, x_sem)
            copies += scan.tile_copies(g_flat, g_ref, g_sem)
            for copy in copies:
                copy.start()
            for copy in copies:
                copy.wait()

        def store():
            copies = scan.tile_copies(sb_flat, sb_ref, sb_sem, True)
            copies += scan.tile_copies(cw_flat, cw_ref, cw_sem, True)
            for copy in copies:
                copy.start()
            for copy in copies:
                copy.wait()

        def backs(i):
            group, block, tile = scan.piece(i)
            lanes = scan.lanes(tile)

            @pl.when(tile == 0)
            def _():
                scan.spread(wr_ref, group, block, rb, NS)

            rates = [rate_ref[n : n + 1, lanes] for n in range(NS)]

            def body(j, carries):
                o = length - 1 - j
                at = scan.rows(group, block, o)
                step = dt_ref[tile, at, :]
                grad = g_ref[tile, at, :]
                return tuple(
                    jnp.exp2(step * rates[n]) * (carries[n] + rb[o, n] * grad) for n in range(NS)
                )

            carries = steps(length, body, (scan.zero(),) * NS)
            mine = 2 * p.c + block
            for n in range(NS):
                backs_ref[mine, group, n, :, lanes] = carries[n].astype(bf16)

        def send():
            share.send(0)

        def arrive():
            share.forward(0)
            share.finish()

        def both(i):
            @pl.when(lax.rem(i, 2) == 0)
            def _():
                again(i // 2)

            @pl.when(lax.rem(i, 2) == 1)
            def _():
                backward(i // 2)

        def again(i):
            group, block, tile = scan.piece(i)
            lanes = scan.lanes(tile)

            @pl.when(tile == 0)
            def _():
                scan.spread(wr_ref, group, block, wb, 0)
                scan.spread(wr_ref, group, block, rb, NS)
                sums[...] = jnp.zeros_like(sums)

            rates = [rate_ref[n : n + 1, lanes] for n in range(NS)]

            def forward(o, states):
                at = scan.rows(group, block, o)
                step = dt_ref[tile, at, :]
                pushed = step * x_ref[tile, at, :]
                new = []
                for n in range(NS):
                    decay = jnp.exp2(step * rates[n])
                    decays[o, n] = decay
                    kept[o, n] = states[n]
                    new.append(decay * states[n] + wb[o, n] * pushed)
                return tuple(new)

            first = tuple(start_ref[block, group, n, :, lanes] for n in range(NS))
            last = steps(length, forward, first)
            for n in range(NS):
                kept[length, n] = last[n]

        def backward(i):
            group, block, tile = scan.piece(i)
            lanes = scan.lanes(tile)
            rates = [rate_ref[n : n + 1, lanes] for n in range(NS)]
            mine = order_ref[blocks + block]

            def link(j, carries):
                b = blocks - 1 - j
                at, decay = scan.link(order_ref, b, ends_ref, group, lanes, rates)
                return tuple(
                    jnp.where(
                        b > mine,
                        backs_ref[at, group, n, :, lanes].astype(f32) + decay[n] * carries[n],
                        carries[n],
                    )
                    for n in range(NS)
                )

            carries = lax.fori_loop(0, blocks - 1, link, (scan.zero(),) * NS)
            for n in range(NS):
                dec_ref[block, group, n, :, lanes] = scan.zero()

            def body(j, carries):
                o = length - 1 - j
                at = scan.rows(group, block, o)
                step = dt_ref[tile, at, :]
                value = x_ref[tile, at, :]
                grad = g_ref[tile, at, :]
                pushed = step * value
                slope, pulled, new = [], [], []
                to = pl.ds(pl.multiple_of(o * width, width), width)
                for n in range(NS):
                    full = carries[n] + rb[o, n] * grad
                    moved = decays[o, n] * full
                    new.append(moved)
                    back = moved * kept[o, n]
                    slope.append(back * rates[n])
                    dec_ref[block, group, n, :, lanes] += back * step
                    pulled.append(full * wb[o, n])
                    wparts[to, n * 128 : (n + 1) * 128] = full * pushed
                    rparts[to, n * 128 : (n + 1) * 128] = kept[o + 1, n] * grad
                while len(slope) > 1:
                    slope = [slope[j] + slope[j + 1] for j in range(0, len(slope), 2)]
                    pulled = [pulled[j] + pulled[j + 1] for j in range(0, len(pulled), 2)]
                sb_ref[tile, at, :] = slope[0] * LN2 + pulled[0] * value
                cw_ref[tile, at, :] = pulled[0]
                return tuple(new)

            steps(length, body, carries)
            source = lax.broadcasted_iota(jnp.int32, (NS * 128, 128), 0) // 128
            target = lax.broadcasted_iota(jnp.int32, (NS * 128, 128), 1)
            pick_w = jnp.where(source == target, 1.0, 0.0).astype(bf16)
            pick_r = jnp.where(source + NS == target, 1.0, 0.0).astype(bf16)
            sums[...] += jnp.dot(
                wparts[...].astype(bf16), pick_w, preferred_element_type=f32
            ) + jnp.dot(rparts[...].astype(bf16), pick_r, preferred_element_type=f32)

            @pl.when(tile == scan.tiles - 1)
            def _():
                def out(o, carry):
                    wrb_ref[scan.rows(group, block, o), :] = sums[
                        pl.ds(pl.multiple_of(o * width, width), width), :
                    ]
                    return carry

                steps(length, out, 0)

        return extra + [load, (scan.pieces, backs), send, arrive, (2 * scan.pieces, both), store]

    spread = pltpu.VMEM((length, NS, width, 128), f32)
    parts = pltpu.VMEM((length * width, NS * 128), f32)
    return hosted(
        loops,
        jobs,
        size,
        cid,
        "scan_backward",
        [
            (order, SM), (dt, ANY), (x, ANY), (g, ANY), (wr, VM), (rate2, VM), (starts, VM), (ends, VM),
        ]
        + (product.ins if product else []),
        [
            (like(dt.shape, f32), ANY),
            (like(dt.shape, f32), ANY),
            (like((dt.shape[0], 128), f32), VM),
            (like(scan.link_shape(2, chan, 0), f32), VM),
        ],
        [
            pltpu.VMEM(scan.link_shape(blocks, chan, 0), bf16),
            spread,
            spread,
            pltpu.VMEM((length + 1, NS, width, 128), f32),
            spread,
            parts,
            parts,
            pltpu.VMEM((length * width, 128), f32),
        ]
        + [scan.tiled()] * 5
        + [DMA((scan.tiles,))] * 5
        + share_sems(1)
        + (product.scratch if product else []),
        plan,
    )


def attention_forward(q_t, k, v_t, bias_t, product, jobs, size, cid, plan):
    rows = q_t.shape[1]
    group = H // KV

    def loops(p, ins, outs, scratch):
        q_ref, k_ref, v_ref, bias_ref = ins[:4]
        o_ref, log_ref = outs

        def head(h):
            at = pl.ds(pl.multiple_of(h * HD, HD), HD)
            g = h // group
            scores = (
                jnp.dot(k_ref[g], q_ref[at, :], preferred_element_type=f32) * score_scale
                + bias_ref[...]
            )
            largest = jnp.max(scores, axis=0, keepdims=True)
            expo = jnp.exp(scores - largest)
            total = jnp.sum(expo, axis=0, keepdims=True)
            probs = (expo * (1.0 / total)).astype(bf16)
            values = v_ref[pl.ds(pl.multiple_of(g * HD, HD), HD), :]
            o_ref[at, :] = jnp.dot(values, probs, preferred_element_type=f32).astype(bf16)
            log_ref[pl.ds(h, 1), :] = largest + jnp.log(total)

        return product.stages(p, *ins[4:], scratch[0]) + [(H, head)]

    return hosted(
        loops,
        jobs,
        size,
        cid,
        "attention_forward",
        [(q_t, VM), (k, VM), (v_t, VM), (bias_t, VM)] + product.ins,
        [(like(q_t.shape, bf16), VM), (like((H, rows), f32), VM)],
        product.scratch,
        plan,
    )


def attention_backward(q_t, k, k_t, v, bias_t, log_total, dout_t, jobs, size, cid, plan):
    group = H // KV
    keys = k.shape[1]

    def loops(p, ins, outs, scratch):
        q_ref, k_ref, kt_ref, v_ref, bias_ref, log_ref, do_ref = ins
        dq_ref, dkv_ref = outs
        contract = (((1,), (1,)), ((), ()))

        def zero():
            dkv_ref[...] = jnp.zeros_like(dkv_ref)

        def head(h):
            at = pl.ds(pl.multiple_of(h * HD, HD), HD)
            g = h // group
            to_k = pl.ds(pl.multiple_of(g * HD, HD), HD)
            to_v = pl.ds(pl.multiple_of((KV + g) * HD, HD), HD)
            query, dout = q_ref[at, :], do_ref[at, :]
            scores = (
                jnp.dot(k_ref[g], query, preferred_element_type=f32) * score_scale + bias_ref[...]
            )
            probs = jnp.exp(scores - log_ref[pl.ds(h, 1), :])
            back = jnp.dot(v_ref[g], dout, preferred_element_type=f32)
            centre = jnp.sum(probs * back, axis=0, keepdims=True)
            score_back = (probs * (back - centre)).astype(bf16)
            dq_ref[at, :] = (
                jnp.dot(kt_ref[to_k, :], score_back, preferred_element_type=f32) * score_scale
            ).astype(bf16)
            dkv_ref[to_k, :] += score_scale * lax.dot_general(
                query, score_back, contract, preferred_element_type=f32
            )
            dkv_ref[to_v, :] += lax.dot_general(
                dout, probs.astype(bf16), contract, preferred_element_type=f32
            )

        return [zero, (H, head)]

    return hosted(
        loops,
        jobs,
        size,
        cid,
        "attention_backward",
        [
            (q_t, VM), (k, VM), (k_t, VM), (v, VM), (bias_t, VM), (log_total, VM), (dout_t, VM),
        ],
        [(like(q_t.shape, bf16), VM), (like((2 * KV * HD, keys), f32), VM)],
        [],
        plan,
    )


def start_exchange(rows_in, gains, first, ffn, first_pack, ffn_pack, size, cid):
    depth = first[0].shape[0]
    n_first = len(first)
    weights = list(first) + list(ffn)
    (first_cuts, first_at, first_total), (ffn_cuts, ffn_at, ffn_total) = first_pack, ffn_pack
    held = []

    def loops(p, ins, outs, scratch):
        (packed_ref,) = outs
        mine, sems = scratch[1 : 1 + len(weights)], scratch[-1]
        held.append(scratch[0])

        def load(which):
            return pltpu.make_async_copy(ins[which], mine[which], sems.at[which])

        def begin():
            for which in range(len(weights)):
                load(which).start()

        def pack_first():
            for which in range(n_first):
                load(which).wait()
            pack_columns(mine[:n_first], scratch[0], first_cuts, first_at, size)

        def pack_ffn():
            for which in range(n_first, len(weights)):
                load(which).wait()
            pack_columns(mine[n_first:], packed_ref, ffn_cuts, ffn_at, size)

        return [begin, pack_first, pack_ffn]

    packed = like((size, depth, first_total), bf16)
    return hosted(
        loops,
        [gather_job(rows_in, size), spread_job(gains, size), move_job(packed, size, held)],
        size,
        cid,
        "start",
        [(item, ANY) for item in weights],
        [(like((size, depth, ffn_total), bf16), VM)],
        [pltpu.VMEM(packed.shape, bf16)]
        + [pltpu.VMEM(item.shape, bf16) for item in weights]
        + [DMA((len(weights),))],
        PLAN_START,
    )


def ffn_sums(low, back, hidden, grads, product, jobs, size, cid):
    rows, width = low.shape
    total, units = back.shape[1], hidden.shape[1]
    depth, quarter = width // size, total // 4
    contract = (((0,), (0,)), ((), ()))

    def loops(p, ins, outs, scratch):
        low_ref, back_ref, hidden_ref, grads_ref = ins[:4]
        quarter_ref, down_ref = outs
        whole = scratch[0]
        halve = Halve(
            p,
            lambda q: whole.at[:, :, column_block(q, quarter)],
            list(scratch[1:4]) + [quarter_ref],
            scratch[4:9],
            True,
        )
        per = quarter // 128
        extra = product.stages(p, back_ref, ins[4], scratch[9]) if product else []

        def tile_of(first, second):
            def tile(i):
                tile_at(jnp.where(i < per, first * per + i, second * per + i - per))

            return tile

        def tile_at(i):
            lanes = column_block(i, 128)
            got = lax.dot_general(
                low_ref[...], back_ref[:, lanes], contract, preferred_element_type=f32
            )
            for f in range(size):
                whole[f, :, lanes] = got[f * depth : (f + 1) * depth, :].astype(bf16)

        def down_tile(i):
            lanes = column_block(i, 128)
            down_ref[pl.ds(pl.multiple_of(i * 128, 128), 128), :] = lax.dot_general(
                hidden_ref[:, lanes], grads_ref[...], contract, preferred_element_type=f32
            ).astype(bf16)

        def sums():
            halve.mine()
            for k in range(size):
                halve.block(k)
            halve.finish()

        return extra + [
            (2 * per, tile_of(p.other, p.near)),
            halve.start,
            (per, tile_of(p.far, p.far)),
            halve.send,
            (per, tile_of(p.c, p.c)),
            (units // 128, down_tile),
            sums,
        ]

    return hosted(
        loops,
        jobs,
        size,
        cid,
        "ffn_sums",
        [(low, VM), (back, VM), (hidden, VM), (grads, VM)] + (product.ins[1:] if product else []),
        [(like((size, depth, quarter), bf16), VM), (like((units, width), bf16), VM)],
        [pltpu.VMEM((size, depth, total), bf16)]
        + halve_scratch(size, depth, quarter, False)
        + (product.scratch if product else []),
        PLAN_FFN,
    )


def finish(wgrad, product, normed, gain, gain_rows, small, size, cid):
    width = normed.shape[1]
    held_gains = []

    def loops(p, ins, outs, scratch):
        left_ref, right_ref, normed_ref, gain_ref, gain_rows_ref = ins
        part_ref, total_ref, gains_ref = scratch
        held_gains.append(gains_ref)

        def begin():
            total_ref[...] = jnp.zeros_like(total_ref)

        def add_gain(at, got):
            product_ = got.astype(f32) * normed_ref[at, :].astype(f32)
            total_ref[...] += jnp.sum(product_, axis=0, keepdims=True)

        def gains():
            gains_ref[...] = gain_rows_ref[...]
            first = total_ref[...] / gain_ref[...]
            cols = width // size
            for f in range(size):
                gains_ref[f, 0:1, :] = first[:, f * cols : (f + 1) * cols]

        return [begin] + product.stages(p, left_ref, right_ref, part_ref, add_gain) + [gains]

    return hosted(
        loops,
        [
            scatter_job(product.shape, size, product.held),
            home_job(wgrad, size),
            ctx_sum_job(small),
            all_sum_job(gain_rows, size, held_gains),
        ],
        size,
        cid,
        "finish",
        product.ins + [(normed, VM), (gain, VM), (gain_rows, VM)],
        [],
        product.scratch + [pltpu.VMEM((1, width), f32), pltpu.VMEM(gain_rows.shape, f32)],
        PLAN_FINISH,
    )


PLAN_START = {1: (0, 1), 2: (0, 2), "end": (0, 2)}
PLAN_FORWARD = {
    1: (2,),
    (1, 2): (2,),
    (1, 4): (2,),
    (1, 6): (2,),
    3: (1,),
    (4, 0): (2, 0),
    (4, 1): (1,),
    (4, 3): (1, 0),
    (4, 4): (1, 2),
    (4, 5): (0,),
    (4, 6): (1,),
    (4, 7): (0, 2),
}
PLAN_ATTEND = {1: (0,), (2, 2): (0,), (2, 12): (0,), (2, 22): (0,)}
PLAN_FFN = {1: (0,), (2, 2): (0,), 5: (0,), (7, 1): (0,)}
PLAN_ATTEND_BACK = {
    0: (0, 1),
    (1, 5): (1,),
    (1, 9): (0,),
    (1, 16): (0,),
    "end": (0, 1, 1, 1, 0),
}
PLAN_FINISH = {
    0: (1,),
    (1, 1): (1,),
    2: (0, 1),
    (2, 1): (1,),
    3: (1, 1, 2, 0),
    "end": (3, 1, 0, 2, 3, 1, 0, 1, 3, 1, 2, 0),
}
PLAN_BACKWARD = {
    3: (4, 3),
    (3, 2): (3,),
    (3, 4): (4,),
    (3, 7): (0,),
    (6, 0): (4, 3),
    (6, 1): (1,),
    (6, 2): (4, 0),
    (6, 5): (0, 3, 4),
    (6, 6): (1, 2),
    (6, 7): (0, 2),
    (6, 8): (1,),
    (6, 9): (0, 2),
    (6, 10): (1, 3),
    (6, 12): (0, 2),
    (6, 13): (1,),
    (6, 15): (2,),
}


def column_grads(x, dy):
    return jnp.einsum("ld,lk->dk", x, dy, preferred_element_type=f32).astype(bf16)


def on_device(
    layer_in,
    out_grad,
    doc_lengths,
    block_deal,
    norm_gains,
    query_weight,
    keyval_weight,
    attn_proj,
    mamba_in,
    conv_taps,
    conv_bias,
    step_bias,
    skip_gain,
    decay_log,
    select_proj,
    step_proj,
    mamba_proj,
    gate_weight,
    up_weight,
    down_weight,
):
    size = lax.axis_size("fsdp")
    n_ctx = lax.axis_size("ctx")
    rows = layer_in.shape[1]
    half_rows = rows // 2
    width = layer_in.shape[2]
    blocks_all = 2 * n_ctx
    group = H // KV
    chan = INNER // size
    q_cols, kv_cols = H * HD // size, 2 * KV * HD // size
    ff_cols = gate_weight.shape[1] // size
    rows_all = size * rows
    ctx_place = lax.axis_index("ctx")
    deal_flat = block_deal.reshape(-1)
    my_blocks = lax.dynamic_slice_in_dim(block_deal, ctx_place, 1, 0)[0]
    offsets = jnp.arange(half_rows, dtype=jnp.int32)
    my_places = (my_blocks[:, None] * half_rows + offsets[None, :]).reshape(-1)
    key_places = (deal_flat[:, None] * half_rows + offsets[None, :]).reshape(-1)
    lengths = doc_lengths[0]
    starts = jnp.cumsum(lengths) - lengths

    def segment(places):
        return jnp.sum((places[:, None] >= starts[None, :]).astype(jnp.int32), axis=1)

    allowed = (key_places[:, None] <= my_places[None, :]) & (
        segment(key_places)[:, None] == segment(my_places)[None, :]
    )
    bias_t = jnp.where(allowed, 0.0, -1e30).astype(f32)
    inverse = jnp.argsort(deal_flat)

    depth = query_weight.shape[0]
    chan_up, qkv_up = up_to(chan, 128), up_to(q_cols + kv_cols, 128)
    ff_up = up_to(ff_cols, 128)
    first_cuts = ((0, 0, q_cols), (1, 0, kv_cols), (2, 0, chan), (2, INNER, chan))
    first_at = (0, q_cols, qkv_up, qkv_up + chan_up)
    first_total = up_to(qkv_up + 2 * chan_up, 128 * n_ctx)
    ffn_cuts = ((0, 0, ff_cols), (1, 0, ff_cols))
    ffn_at = (0, ff_up)
    ffn_total = up_to(2 * ff_up, 128 * n_ctx)
    (ffn_packed,), ((stream_all,), (gain_all,), (first_mat,)) = start_exchange(
        layer_in[0],
        norm_gains,
        (query_weight, keyval_weight, mamba_in),
        (gate_weight, up_weight),
        (first_cuts, first_at, first_total),
        (ffn_cuts, ffn_at, ffn_total),
        size,
        0,
    )
    stream_all = stream_all.reshape(rows_all, width)
    gain_float = jnp.moveaxis(gain_all, 0, 1).reshape(4, width).astype(f32)
    first_mat = first_mat.reshape(width, first_total)
    qkv_mat = first_mat[:, :qkv_up]
    entry_mat = first_mat[:, qkv_up : qkv_up + 2 * chan_up]
    ffn_quarter = ffn_total // n_ctx
    attn_wide = up_to(width, 128 * n_ctx)
    attn_packed = jnp.pad(attn_proj, ((0, 0), (0, attn_wide - width)))
    down_mat = jnp.pad(down_weight, ((0, ff_up - ff_cols), (0, 0)))
    more = chan_up - chan
    taps_mat = jnp.pad(conv_taps, ((0, 0), (0, more)))
    mamba_mat = jnp.pad(mamba_proj, ((0, more), (0, 0)))
    select_mat = jnp.pad(select_proj, ((0, more), (0, 0)))
    step_mat = jnp.pad(step_proj, ((0, 0), (0, more)))
    rate = -jnp.exp(jnp.pad(decay_log, ((0, 0), (0, more))).astype(f32))
    rate2 = rate * 1.4426950408889634
    shift_float, step_shift, skip_float = (
        jnp.pad(item, (0, more)).astype(f32) for item in (conv_bias, step_bias, skip_gain)
    )

    stream = layer_in[0].astype(f32)
    _, inv_in = norm_forward(stream, gain_float[0])
    normed_all, inv_all = norm_forward(stream_all.astype(f32), gain_float[0])
    normed_all = normed_all.astype(bf16)

    qkv_t = jnp.einsum("dk,ld->kl", qkv_mat, normed_all, preferred_element_type=f32).astype(bf16)
    entry = jnp.dot(normed_all, entry_mat, preferred_element_type=f32)
    chan = chan_up
    mixer_in = entry[:, :chan].astype(bf16)
    gate_side = entry[:, chan:]
    mixer_blocks = mixer_in.reshape(size, 2, half_rows, chan)
    tails = mixer_blocks[:, :, half_rows - (CONV - 1) :]
    (qkv,), (tails_all,) = together(
        [exchange_job(qkv_t, size, up_to(q_cols + kv_cols, 8)), ctx_gather_job(tails.reshape(-1, chan))],
        size,
        1,
        "edges",
    )
    query_t = qkv[:, :q_cols].reshape(H * HD, rows)
    keyval_t = qkv[:, q_cols : q_cols + kv_cols].reshape(2 * KV * HD, rows)
    tails_all = tails_all.reshape(n_ctx, size, 2, CONV - 1, chan)

    def in_deal_order(values):
        return jnp.moveaxis(values, 2, 1).reshape((blocks_all,) + (size,) + values.shape[3:])

    def of_blocks(values, index):
        return jnp.moveaxis(jnp.take(values, index, axis=0), 0, 1)

    before_index = inverse[jnp.maximum(my_blocks - 1, 0)]
    has_before = my_blocks > 0
    prior_tail = jnp.where(
        has_before[None, :, None, None],
        of_blocks(in_deal_order(tails_all), before_index),
        jnp.zeros_like(tails),
    )
    padded = jnp.concatenate([prior_tail, mixer_blocks], axis=2).astype(f32)
    taps_float = taps_mat.astype(f32)
    conv_blocks_out = shift_float + sum(
        taps_float[offset] * padded[:, :, offset : offset + half_rows] for offset in range(CONV)
    )
    conv_out = conv_blocks_out.reshape(rows_all, chan)
    signal = jax.nn.silu(conv_out).astype(bf16)
    signal_float = signal.astype(f32)
    selected_part = jnp.einsum(
        "ik,li->kl", select_mat, signal, preferred_element_type=f32
    ).astype(bf16)
    (selected,), (keyvals_all,) = together(
        [sum_job(selected_part, size), ctx_gather_job(keyval_t)], size, 3, "select"
    )
    keyvals_t = keyvals_all.transpose(1, 0, 2).reshape(2 * KV * HD, n_ctx * rows)
    keyvals = keyvals_t.reshape(2 * KV, HD, n_ctx * rows).transpose(0, 2, 1)
    key_groups, value_groups = keyvals[:KV], keyvals[KV:]
    step_low = selected[:RANK].T
    write_read = jnp.pad(selected[RANK:], ((0, 128 - 2 * NS), (0, 0))).T.astype(f32)
    step_pre = jnp.dot(step_low, step_mat, preferred_element_type=f32) + step_shift
    step_sizes = jax.nn.softplus(step_pre)
    order = jnp.concatenate([inverse, my_blocks]).astype(jnp.int32)
    (scan_rows, start_state, ends_all), ((grads_all,), (ffn_mat,), (attn_mat,)) = scan_forward(
        order,
        step_sizes,
        signal_float,
        write_read,
        rate2,
        size,
        [
            gather_job(out_grad[0], size),
            move_job(ffn_packed, size),
            gather_job(attn_packed, size, True),
        ],
        size,
        4,
        PLAN_FORWARD,
    )
    grads_all = grads_all.reshape(rows_all, width)
    ffn_mat = ffn_mat.reshape(width, ffn_total)
    gate_mat, up_mat = ffn_mat[:, :ff_up], ffn_mat[:, ff_up : 2 * ff_up]
    attn_mat = attn_mat.reshape(width, attn_wide)[:, :width]
    scanned = scan_rows + skip_float * signal_float
    gate_act = jax.nn.silu(gate_side)
    mamba_rows = (scanned * gate_act).astype(bf16)
    mamba_product = Product(mamba_rows, mamba_mat, size)
    (attn_rows_t, log_totals), ((mamba_out,),) = attention_forward(
        query_t,
        key_groups,
        keyvals_t[KV * HD :],
        bias_t,
        mamba_product,
        [scatter_job(mamba_product.shape, size, mamba_product.held)],
        size,
        5,
        PLAN_ATTEND,
    )
    attn_out = jnp.einsum("hl,hd->ld", attn_rows_t, attn_mat, preferred_element_type=f32)
    attn_normed, inv_attn = norm_forward(attn_out, gain_float[1])

    mamba_normed, inv_mamba = norm_forward(mamba_out, gain_float[2])
    middle = stream + 0.5 * (attn_normed + mamba_normed)
    ffn_normed, inv_ffn = norm_forward(middle, gain_float[3])
    ((ffn_low,),) = together(
        [gather_job(ffn_normed.astype(bf16), size)], size, 6, "ffn_rows"
    )
    ffn_low = ffn_low.reshape(rows_all, width)
    gate_pre = jnp.dot(ffn_low, gate_mat, preferred_element_type=f32)
    up_pre = jnp.dot(ffn_low, up_mat, preferred_element_type=f32)
    hidden = (jax.nn.silu(gate_pre) * up_pre).astype(bf16)
    hidden_back = jnp.einsum("ld,fd->lf", grads_all, down_mat, preferred_element_type=f32)
    gate_back = (hidden_back * up_pre * silu_slope(gate_pre)).astype(bf16)
    up_back = (hidden_back * jax.nn.silu(gate_pre)).astype(bf16)
    ffn_back_low = jnp.concatenate([gate_back, up_back], axis=1)
    ffn_back_low = jnp.pad(ffn_back_low, ((0, 0), (0, ffn_total - 2 * ff_up)))
    fits = size <= 8
    if fits:
        ffn_product = Product(ffn_back_low, ffn_mat, size, True)
        ffn_jobs = [scatter_job(ffn_product.shape, size, ffn_product.held)]
    else:
        ffn_product = None
        ffn_part = jnp.einsum("lf,df->ld", ffn_back_low, ffn_mat, preferred_element_type=f32)
        ffn_jobs = [scatter_job(ffn_part.astype(bf16).reshape(size, rows, width), size)]
    (ffn_quarter_sum, down_wgrad), ffn_back = ffn_sums(
        ffn_low, ffn_back_low, hidden, grads_all, ffn_product, ffn_jobs * fits, size, 7
    )
    if not fits:
        ffn_back = together(ffn_jobs, size, 14, "ffn_sum")
    ffn_back = ffn_back[0][0]
    middle_part, ffn_gain_grad = norm_backward(ffn_back, middle, inv_ffn, gain_float[3])
    middle_back = out_grad[0].astype(f32) + middle_part
    branch_back = 0.5 * middle_back
    attn_part, attn_gain_grad = norm_backward(branch_back, attn_out, inv_attn, gain_float[1])
    mamba_part_back, mamba_gain_grad = norm_backward(
        branch_back, mamba_out, inv_mamba, gain_float[2]
    )
    attn_back = attn_part.astype(bf16)
    attn_back_wide = jnp.pad(attn_back, ((0, 0), (0, attn_wide - width)))
    attn_wgrad = jnp.einsum(
        "hl,ld->hd", attn_rows_t, attn_back_wide, preferred_element_type=f32
    ).astype(bf16)
    dout_t = jnp.einsum("hd,ld->hl", attn_mat, attn_back, preferred_element_type=f32).astype(bf16)
    (query_back_t, keyval_terms), ((mamba_back,), (attn_quarter,)) = (
        attention_backward(
            query_t,
            key_groups,
            keyvals_t[: KV * HD],
            value_groups,
            bias_t,
            log_totals,
            dout_t,
            [
                gather_job(mamba_part_back.astype(bf16), size),
                halve_job(attn_wgrad.reshape(size, depth, attn_wide)),
            ],
            size,
            8,
            PLAN_ATTEND_BACK,
        )
    )
    mamba_back = mamba_back.reshape(rows_all, width)
    mamba_wgrad = jnp.einsum("li,ld->id", mamba_rows, mamba_back, preferred_element_type=f32)
    mrows_back = jnp.einsum("ld,id->li", mamba_back, mamba_mat, preferred_element_type=f32)
    scan_back = mrows_back * gate_act
    side_back = mrows_back * scanned * silu_slope(gate_side)
    skip_grad = jnp.sum(scan_back * signal_float, axis=0)
    down_product = Product(hidden, down_mat, size) if fits else None
    if fits:
        down_jobs = [scatter_job(down_product.shape, size, down_product.held)]
    else:
        down_part = jnp.dot(hidden, down_mat, preferred_element_type=f32).astype(bf16)
        down_jobs = [scatter_job(down_part.reshape(size, rows, width), size)]
    (
        (step_back, carry_writes, read_write_back, decay_sums),
        ((ffn_home,), (attn_piece,), (mamba_share,), (down_share,), *down_out),
    ) = scan_backward(
        order,
        step_sizes,
        signal_float,
        scan_back,
        write_read,
        rate2,
        start_state,
        ends_all,
        down_product,
        size,
        [
            deliver_job(ffn_quarter_sum, size),
            scatter_job(attn_quarter, size),
            ctx_sum_job(mamba_wgrad.astype(bf16), up_to(mamba_proj.shape[0], 64)),
            ctx_sum_job(down_wgrad, up_to(ff_cols, 64)),
        ]
        + down_jobs * fits,
        size,
        9,
        PLAN_BACKWARD,
    )
    if not fits:
        down_out = together(down_jobs, size, 15, "down_sum")
    result = middle + down_out[0][0]
    decay_grad = rate * jnp.sum(decay_sums, axis=(0, 1, 3))
    signal_back = scan_back * skip_float + step_sizes * carry_writes
    read_write_back = read_write_back[:, : 2 * NS]
    pre_back = (step_back * jax.nn.sigmoid(step_pre)).astype(bf16)
    step_wgrad = jnp.einsum("lr,li->ri", step_low, pre_back, preferred_element_type=f32)
    bias_grad = jnp.sum(pre_back.astype(f32), axis=0)
    rank_back = jnp.einsum("li,ri->lr", pre_back, step_mat, preferred_element_type=f32)
    select_part = jnp.concatenate([rank_back, read_write_back], axis=1).astype(bf16).T
    (select_back,), (attn_home,), (keyval_back,) = together(
        [
            sum_job(select_part, size),
            ctx_gather_job(attn_piece.astype(bf16)),
            halve_job(keyval_terms.astype(bf16)[None]),
        ],
        size,
        10,
        "select_back",
    )
    select_back = select_back.T
    select_wgrad = jnp.einsum("li,lk->ik", signal, select_back, preferred_element_type=f32)
    signal_back = signal_back + jnp.einsum(
        "lk,ik->li", select_back, select_mat, preferred_element_type=f32
    )
    conv_back = signal_back * silu_slope(conv_out)
    conv_blocks = conv_back.reshape(size, 2, half_rows, chan)
    taps_grad = jnp.stack(
        [
            jnp.sum(conv_blocks * padded[:, :, offset : offset + half_rows], axis=(0, 1, 2))
            for offset in range(CONV)
        ]
    )
    shift_grad = jnp.sum(conv_back, axis=0)
    padded_back = sum(
        (
            jnp.pad(
                taps_float[offset] * conv_blocks,
                ((0, 0), (0, 0), (offset, CONV - 1 - offset), (0, 0)),
            )
            for offset in range(CONV)
        )
    )
    tail_back = jnp.where(has_before[None, :, None, None], padded_back[:, :, : CONV - 1], 0.0)
    keyval_back_t = keyval_back.reshape(size, kv_cols, rows)
    qkv_back_t = jnp.concatenate([query_back_t.reshape(size, q_cols, rows), keyval_back_t], axis=1)
    pad_rows = up_to(q_cols + kv_cols, 8) - q_cols - kv_cols
    qkv_back_t = jnp.pad(qkv_back_t, ((0, 0), (0, pad_rows), (0, 0)))
    (tails_back_all,), (qkv_back,) = together(
        [ctx_gather_job(tail_back.astype(bf16).reshape(-1, chan)), exchange_job(qkv_back_t, size)],
        size,
        11,
        "edges_back",
    )
    qkv_back = qkv_back.transpose(0, 2, 1).reshape(rows_all, -1)
    qkv_back = jnp.pad(qkv_back, ((0, 0), (0, qkv_up - qkv_back.shape[1])))
    tails_back_all = in_deal_order(tails_back_all.reshape(n_ctx, size, 2, CONV - 1, chan))
    after_index = inverse[jnp.minimum(my_blocks + 1, blocks_all - 1)]
    has_after = my_blocks < blocks_all - 1
    incoming = jnp.where(
        has_after[None, :, None, None], of_blocks(tails_back_all, after_index).astype(f32), 0.0
    )
    mixer_back = padded_back[:, :, CONV - 1 :] + jnp.pad(
        incoming, ((0, 0), (0, 0), (half_rows - (CONV - 1), 0), (0, 0))
    )
    entry_back = jnp.concatenate([mixer_back.reshape(rows_all, chan), side_back], axis=1).astype(
        bf16
    )
    first_back = [qkv_back, entry_back]
    if first_total > qkv_up + 2 * chan_up:
        first_back.append(jnp.zeros((rows_all, first_total - qkv_up - 2 * chan_up), bf16))
    first_back = jnp.concatenate(first_back, axis=1)
    first_wgrad = column_grads(normed_all, first_back)
    gain_rows = jnp.stack(
        [jnp.zeros_like(attn_gain_grad), attn_gain_grad, mamba_gain_grad, ffn_gain_grad]
    )
    gain_rows = jnp.moveaxis(gain_rows.reshape(4, size, -1), 1, 0)
    small = jnp.concatenate(
        [
            taps_grad,
            shift_grad[None],
            bias_grad[None],
            skip_grad[None],
            decay_grad,
            step_wgrad,
            select_wgrad.T,
        ]
    )
    n_small = small.shape[0]
    small = jnp.pad(small, ((0, up_to(n_small, 64) - n_small), (0, 0))).astype(bf16)
    gate_share, up_share = unpack_columns(
        ffn_home, ffn_cuts, ffn_at, (gate_weight.shape, up_weight.shape), size
    )
    input_product = Product(first_back, first_mat, size, True)
    _, ((input_back,), (first_home,), (small,), (gain_share,)) = finish(
        first_wgrad.reshape(size, depth, first_total),
        input_product,
        normed_all,
        gain_float[:1],
        gain_rows,
        small,
        size,
        13,
    )
    stream_part, _ = norm_backward(input_back, stream, inv_in, gain_float[0])
    stream_back = middle_back + stream_part
    query_share, keyval_share, entry_share = unpack_columns(
        first_home,
        first_cuts,
        first_at,
        (query_weight.shape, keyval_weight.shape, mamba_in.shape),
        size,
    )
    chan = conv_bias.shape[0]
    vectors = small.reshape(-1, chan_up)[:, :chan].astype(f32)
    attn_share = jnp.moveaxis(attn_home, 0, 1).reshape(depth, attn_wide)[:, :width].astype(f32)
    mamba_share = mamba_share.reshape(-1, width)[:chan].astype(f32)
    down_share = down_share.reshape(-1, width)[:ff_cols].astype(f32)
    return (
        result.astype(bf16)[None],
        stream_back[None],
        gain_share,
        query_share,
        keyval_share,
        attn_share,
        entry_share,
        vectors[:CONV],
        vectors[CONV],
        vectors[CONV + 1],
        vectors[CONV + 2],
        vectors[CONV + 3 : CONV + 3 + NS],
        vectors[CONV + 3 + NS + RANK : n_small].T,
        vectors[CONV + 3 + NS : CONV + 3 + NS + RANK],
        mamba_share,
        gate_share,
        up_share,
        down_share,
    )


def solution(mesh):
    in_specs = (
        P("fsdp", "ctx", None),
        P("fsdp", "ctx", None),
        P("fsdp", None),
        P(),
        P(None, "fsdp"),
        P("fsdp", None),
        P("fsdp", None),
        P("fsdp", None),
        P("fsdp", None),
        P(None, "fsdp"),
        P("fsdp"),
        P("fsdp"),
        P("fsdp"),
        P(None, "fsdp"),
        P("fsdp", None),
        P(None, "fsdp"),
        P("fsdp", None),
        P("fsdp", None),
        P("fsdp", None),
        P("fsdp", None),
    )
    out_specs = (
        P("fsdp", "ctx", None),
        P("fsdp", "ctx", None),
        P(None, "fsdp"),
        P("fsdp", None),
        P("fsdp", None),
        P("fsdp", None),
        P("fsdp", None),
        P(None, "fsdp"),
        P("fsdp"),
        P("fsdp"),
        P("fsdp"),
        P(None, "fsdp"),
        P("fsdp", None),
        P(None, "fsdp"),
        P("fsdp", None),
        P("fsdp", None),
        P("fsdp", None),
        P("fsdp", None),
    )
    return jax.shard_map(
        on_device, mesh=mesh, in_specs=in_specs, out_specs=out_specs, check_vma=False
    )
```

```python
import functools
import math

import jax
import jax.numpy as jnp
from jax import lax
from jax.experimental import pallas as pl
from jax.experimental.pallas import tpu as pltpu
from jax.sharding import PartitionSpec as P

H = 25
KV = 5
HD = 64
INNER = 3200
NS = 16
RANK = 100
CONV = 4

EPS = 1e-06
score_scale = 0.125
MESH = pl.DeviceIdType.MESH
ANY = pl.BlockSpec(memory_space=pl.ANY)
VM = pl.BlockSpec(memory_space=pltpu.VMEM)
DMA = pltpu.SemaphoreType.DMA
f32 = jnp.float32
bf16 = jnp.bfloat16


def params(cid, vmem=None):
    return pltpu.CompilerParams(collective_id=cid, has_side_effects=True, vmem_limit_bytes=vmem)


def rcopy(src, dst, ssem, rsem, dev):
    return pltpu.make_async_remote_copy(
        src_ref=src, dst_ref=dst, send_sem=ssem, recv_sem=rsem, device_id=dev, device_id_type=MESH
    )


def norm_forward(values, gain):
    inverse = lax.rsqrt(jnp.mean(values * values, axis=-1, keepdims=True) + EPS)
    return (values * inverse * gain, inverse)


def norm_backward(grad, values, inverse, gain):
    normed = values * inverse
    gain_grad = jnp.sum(grad * normed, axis=0)
    scaled = grad * gain
    return (
        inverse * (scaled - normed * jnp.mean(scaled * normed, axis=-1, keepdims=True)),
        gain_grad,
    )


def silu_slope(values):
    sigma = jax.nn.sigmoid(values)
    return sigma * (1.0 + values * (1.0 - sigma))


def up_to(value, step):
    return (value + step - 1) // step * step


def pack_columns(refs, out, cuts, offsets, size):
    out[...] = jnp.zeros_like(out)
    for (which, first, cols), at in zip(cuts, offsets):
        for f in range(size):
            out[f, :, at : at + cols] = refs[which][:, first + f * cols : first + (f + 1) * cols]


def unpack_pieces(home, outs, cuts, offsets, size):
    for (which, first, cols), at in zip(cuts, offsets):
        for f in range(size):
            outs[which][:, first + f * cols : first + (f + 1) * cols] = home[
                f, :, at : at + cols
            ].astype(f32)


def unpack_columns(home, cuts, offsets, shapes, size):
    def kernel(h_ref, *outs):
        unpack_pieces(h_ref, outs, cuts, offsets, size)

    return pl.pallas_call(
        kernel,
        out_shape=[jax.ShapeDtypeStruct(shape, f32) for shape in shapes],
        in_specs=[VM],
        out_specs=[VM] * len(shapes),
        compiler_params=pltpu.CompilerParams(vmem_limit_bytes=60 << 20),
        name="unpack_columns",
    )(home)


class Job:
    def __init__(self, steps, ins, outs, scratch):
        self.steps, self.ins, self.outs, self.scratch = steps, ins, outs, scratch


class Place:
    def __init__(self, size):
        self.size, self.lanes = size, size // 2
        self.f, self.c = lax.axis_index("fsdp"), lax.axis_index("ctx")
        self.a, self.b = self.f // 2, lax.rem(self.f, 2)
        self.near = self.c + 1 - 2 * lax.rem(self.c, 2)
        self.far = lax.rem(self.c + 2, 4)
        self.other = lax.rem(self.near + 2, 4)

    def greet(self):
        bar = pltpu.get_barrier_semaphore()
        for d in range(1, self.size):
            peer = {"fsdp": lax.rem(self.f + d, self.size)}
            pl.semaphore_signal(bar, inc=1, device_id=peer, device_id_type=MESH)
        for peer in (self.near, self.far):
            pl.semaphore_signal(bar, inc=1, device_id={"ctx": peer}, device_id_type=MESH)
        pl.semaphore_wait(bar, self.size + 1)


def part(ref_list, jobs, field):
    out = []
    for job in jobs:
        count = len(getattr(job, field))
        out.append(ref_list[:count])
        ref_list = ref_list[count:]
    return out


class Moving:
    def __init__(self, live):
        self.live = live

    def step(self, which):
        if which < len(self.live) and self.live[which] is not None:
            try:
                next(self.live[which])
            except StopIteration:
                self.live[which] = None

    def drain(self):
        while any(item is not None for item in self.live):
            for which in range(len(self.live)):
                self.step(which)


def together(jobs, size, cid, name, order=()):
    n_in = sum(len(job.ins) for job in jobs)
    n_out = sum(len(job.outs) for job in jobs)

    def kernel(*refs):
        place = Place(size)
        place.greet()
        ins = part(refs[:n_in], jobs, "ins")
        outs = part(refs[n_in : n_in + n_out], jobs, "outs")
        scratch = part(refs[n_in + n_out :], jobs, "scratch")
        moving = Moving(
            [job.steps(place, i, o, s) for job, i, o, s in zip(jobs, ins, outs, scratch)]
        )
        for which in order:
            moving.step(which)
        moving.drain()

    got = pl.pallas_call(
        kernel,
        out_shape=[shape for job in jobs for shape, _ in job.outs],
        in_specs=[spec for job in jobs for _, spec in job.ins],
        out_specs=[spec for job in jobs for _, spec in job.outs],
        scratch_shapes=[item for job in jobs for item in job.scratch],
        compiler_params=params(cid, 60 << 20),
        name=name,
    )(*[array for job in jobs for array, _ in job.ins])
    return part(got, jobs, "outs")


def like(shape, dtype):
    return jax.ShapeDtypeStruct(shape, dtype)


def gather_job(x, size, shared=False):
    rows, cols = x.shape
    lanes = size // 2

    def run(p, ins, outs, scratch):
        (x_ref,), (o_ref,) = ins, outs
        lsem, up_s, up_r, dn_s, dn_r, px_s, px_r = scratch[:7]

        def view(i, q):
            return o_ref.at[i, :, column_block(q, cols // 4)]

        def piece(origin, b):
            i = 2 * origin + b
            return view(i, p.c) if shared else o_ref.at[i]

        def own():
            return x_ref.at[:, column_block(p.c, cols // 4)] if shared else x_ref

        share = Share(p, view, size, scratch[7:]) if shared else None

        def local():
            return pltpu.make_async_copy(own(), piece(p.a, p.b), lsem)

        def up(s):
            src = own() if s == 0 else piece(p.a - s, p.b)
            dev = {"fsdp": 2 * (p.a + 1) + p.b}
            return rcopy(src, piece(p.a - s, p.b), up_s.at[s], up_r.at[s], dev)

        def down(s):
            src = own() if s == 0 else piece(p.a + s, p.b)
            dev = {"fsdp": 2 * (p.a - 1) + p.b}
            return rcopy(src, piece(p.a + s, p.b), dn_s.at[s], dn_r.at[s], dev)

        def across(origin, src=None):
            src = piece(origin, p.b) if src is None else src
            dev = {"fsdp": 2 * p.a + 1 - p.b}
            return rcopy(src, piece(origin, p.b), px_s.at[origin], px_r.at[origin], dev)

        def came(ref, sem, dev):
            rcopy(ref, ref, sem, sem, dev).wait_recv()

        def arrived(origin, b, src=None):
            if shared:
                share.send(2 * origin + b, src)

        local().start()

        @pl.when(p.a < lanes - 1)
        def _():
            up(0).start()

        @pl.when(p.a > 0)
        def _():
            down(0).start()

        across(p.a, own()).start()
        if shared:
            arrived(p.a, p.b, own())
        yield
        for s in range(lanes - 1):
            @pl.when(p.a - 1 - s >= 0)
            def _():
                came(piece(p.a - 1 - s, p.b), up_r.at[s], {"fsdp": 2 * (p.a - 1) + p.b})

                @pl.when(p.a < lanes - 1)
                def _():
                    up(s + 1).start()

                across(p.a - 1 - s).start()
                arrived(p.a - 1 - s, p.b)

            @pl.when(p.a + 1 + s <= lanes - 1)
            def _():
                came(piece(p.a + 1 + s, p.b), dn_r.at[s], {"fsdp": 2 * (p.a + 1) + p.b})

                @pl.when(p.a > 0)
                def _():
                    down(s + 1).start()

                across(p.a + 1 + s).start()
                arrived(p.a + 1 + s, p.b)

            yield
        local().wait()
        for origin in range(lanes):
            came(piece(origin, 1 - p.b), px_r.at[origin], {"fsdp": 2 * p.a + 1 - p.b})
            arrived(origin, 1 - p.b)
        if shared:
            yield
            for i in range(size):
                share.forward(i)
            yield
            share.finish()
        for s in range(lanes - 1):
            @pl.when((p.a - s >= 0) & (p.a < lanes - 1))
            def _():
                up(s).wait_send()

            @pl.when((p.a + s <= lanes - 1) & (p.a > 0))
            def _():
                down(s).wait_send()

        for origin in range(lanes):
            across(origin).wait_send()

    return Job(
        run,
        [(x, ANY)],
        [(like((size, rows, cols), x.dtype), ANY)],
        [DMA] + [DMA((lanes,))] * 6 + (share_sems(size) if shared else []),
    )


def add_blocks(out, terms, dtype, rows):
    if rows % 16:
        total = terms[0][...].astype(f32)
        for ref in terms[1:]:
            total += ref[...].astype(f32)
        out[...] = total.astype(dtype)
        return
    step = 32 if rows % 32 == 0 else 16

    def body(i, carry):
        at = pl.ds(pl.multiple_of(i * step, step), step)
        total = terms[0][at, :].astype(f32)
        for ref in terms[1:]:
            total += ref[at, :].astype(f32)
        out[at, :] = total.astype(dtype)
        return carry

    lax.fori_loop(0, rows // step, body, 0)


def scatter_job(partial, size, held=None):
    rows, cols = partial.shape[1:]
    lanes = size // 2

    def run(p, ins, outs, scratch):
        (o_ref,) = outs
        p_ref = held[0] if held is not None else ins[0]
        xbuf, upb, dnb, up_s, up_r, dn_s, dn_r, px_s, px_r = scratch[:9]

        def own(dest):
            return p_ref.at[2 * dest + p.b] if held is not None else scratch[9].at[dest]

        def local(dest):
            return pltpu.make_async_copy(
                p_ref.at[2 * dest + p.b], scratch[9].at[dest], scratch[10].at[dest]
            )

        def across(dest):
            src = p_ref.at[2 * dest + 1 - p.b]
            dev = {"fsdp": 2 * p.a + 1 - p.b}
            return rcopy(src, xbuf.at[dest], px_s.at[dest], px_r.at[dest], dev)

        def up(dest):
            dev = {"fsdp": 2 * (p.a + 1) + p.b}
            return rcopy(xbuf.at[dest], upb.at[dest], up_s.at[dest], up_r.at[dest], dev)

        def down(dest):
            dev = {"fsdp": 2 * (p.a - 1) + p.b}
            return rcopy(xbuf.at[dest], dnb.at[dest], dn_s.at[dest], dn_r.at[dest], dev)

        def add_in(dest, extra):
            terms = [xbuf.at[dest], own(dest)]
            if extra is not None:
                terms.append(extra.at[dest])
            add_blocks(xbuf.at[dest], terms, bf16, rows)

        if held is None:
            for dest in range(lanes):
                local(dest).start()
        for d in range(lanes - 1, -1, -1):
            @pl.when(p.a + d <= lanes - 1)
            def _():
                across(p.a + d).start()

            if d > 0:
                @pl.when(p.a - d >= 0)
                def _():
                    across(p.a - d).start()

        yield
        if held is None:
            for dest in range(lanes):
                local(dest).wait()
        for d in range(lanes - 1, 0, -1):
            @pl.when(p.a + d <= lanes - 1)
            def _():
                across(p.a + d).wait_recv()

                @pl.when(p.a > 0)
                def _():
                    up(p.a + d).wait_recv()
                    add_in(p.a + d, upb)

                @pl.when(p.a == 0)
                def _():
                    add_in(p.a + d, None)

                up(p.a + d).start()

            @pl.when(p.a - d >= 0)
            def _():
                across(p.a - d).wait_recv()

                @pl.when(p.a < lanes - 1)
                def _():
                    down(p.a - d).wait_recv()
                    add_in(p.a - d, dnb)

                @pl.when(p.a == lanes - 1)
                def _():
                    add_in(p.a - d, None)

                down(p.a - d).start()

            yield
        across(p.a).wait_recv()
        terms = [xbuf.at[p.a], own(p.a)]

        @pl.when(p.a == 0)
        def _():
            down(p.a).wait_recv()
            add_blocks(o_ref, terms + [dnb.at[p.a]], f32, rows)

        @pl.when(p.a == lanes - 1)
        def _():
            up(p.a).wait_recv()
            add_blocks(o_ref, terms + [upb.at[p.a]], f32, rows)

        @pl.when((p.a > 0) & (p.a < lanes - 1))
        def _():
            up(p.a).wait_recv()
            down(p.a).wait_recv()
            add_blocks(o_ref, terms + [upb.at[p.a], dnb.at[p.a]], f32, rows)

        for dest in range(lanes):
            across(dest).wait_send()

        for d in range(lanes - 1, 0, -1):
            @pl.when(p.a + d <= lanes - 1)
            def _():
                up(p.a + d).wait_send()

            @pl.when(p.a - d >= 0)
            def _():
                down(p.a - d).wait_send()

    return Job(
        run,
        [(partial, ANY)] if held is None else [],
        [(like((rows, cols), f32), VM)],
        [pltpu.VMEM((lanes, rows, cols), bf16)] * 3
        + [DMA((lanes,))] * 6
        + ([pltpu.VMEM((lanes, rows, cols), bf16), DMA((lanes,))] if held is None else []),
    )


def column_block(of, quarter):
    return pl.ds(pl.multiple_of(of * quarter, 128), quarter)


class Share:
    def __init__(self, p, view, count, sems):
        self.p, self.view, self.count = p, view, count
        self.fs, self.fr, self.ns, self.nr, self.hs, self.hr = sems

    def far(self, d, q, src=None):
        ref = self.view(d, q)
        src = ref if src is None else src
        return rcopy(src, ref, self.fs.at[d], self.fr.at[d], {"ctx": self.p.far})

    def near(self, d, q, src=None):
        ref = self.view(d, q)
        src = ref if src is None else src
        return rcopy(src, ref, self.ns.at[d], self.nr.at[d], {"ctx": self.p.near})

    def onward(self, d, q):
        ref = self.view(d, q)
        return rcopy(ref, ref, self.hs.at[d], self.hr.at[d], {"ctx": self.p.near})

    def send(self, d, src=None):
        self.far(d, self.p.c, src).start()
        self.near(d, self.p.c, src).start()

    def forward(self, d):
        self.far(d, self.p.far).wait_recv()
        self.onward(d, self.p.far).start()

    def finish(self):
        p = self.p
        for d in range(self.count):
            self.far(d, p.c).wait_send()
            self.near(d, p.c).wait_send()
            self.near(d, p.near).wait_recv()
            self.onward(d, p.far).wait_send()
            self.onward(d, p.other).wait_recv()


def share_sems(count):
    return [DMA((count,))] * 6


def move_job(packed, size, held=None):
    depth, total = packed.shape[-2:]
    quarter = total // 4

    def run(p, ins, outs, scratch):
        (w_ref,) = outs
        p_ref = held[0] if held is not None else ins[0]
        lsem, ws, wr = scratch[:3]

        def source(to):
            return p_ref.at[to, :, column_block(p.c, quarter)]

        def view(d, q):
            return w_ref.at[lax.rem(p.f - d + size, size), :, column_block(q, quarter)]

        def local():
            return pltpu.make_async_copy(source(p.f), view(0, p.c), lsem)

        def move(d):
            to = lax.rem(p.f + d, size)
            return rcopy(source(to), view(0, p.c), ws.at[d], wr.at[d], {"fsdp": to})

        def came(d):
            ref = view(d, p.c)
            rcopy(ref, ref, ws.at[d], wr.at[d], {"fsdp": lax.rem(p.f + d, size)}).wait_recv()

        share = Share(p, view, size, scratch[3:])
        local().start()
        for d in range(1, size):
            move(d).start()
        share.send(0, source(p.f))
        yield
        for d in range(1, size):
            came(d)
            share.send(d)
            if d % 2 == 0:
                yield
        for d in range(size):
            share.forward(d)
            if d % 4 == 3:
                yield
        local().wait()
        share.finish()
        for d in range(1, size):
            move(d).wait_send()

    return Job(
        run,
        [(packed, ANY)] if held is None else [],
        [(like((size, depth, total), packed.dtype), ANY)],
        [DMA, DMA((size,)), DMA((size,))] + share_sems(size),
    )


def spread_job(x, size):
    def run(p, ins, outs, scratch):
        (x_ref,), (o_ref,) = ins, outs
        lsem, ss, rs = scratch

        def copy(d):
            to = {"fsdp": lax.rem(p.f + d, size)}
            return rcopy(x_ref, o_ref.at[p.f], ss.at[d], rs.at[d], to)

        def local():
            return pltpu.make_async_copy(x_ref, o_ref.at[p.f], lsem)

        local().start()
        for d in range(1, size):
            copy(d).start()
        yield
        local().wait()
        for d in range(1, size):
            copy(d).wait()

    return Job(
        run,
        [(x, ANY)],
        [(like((size,) + x.shape, x.dtype), ANY)],
        [DMA, DMA((size,)), DMA((size,))],
    )


def exchange_job(x, size, rows=None):
    blocks = x.shape if rows is None else (size, rows, x.shape[1] // size)

    def run(p, ins, outs, scratch):
        (x_ref,), (o_ref,) = ins, outs
        lsem, ss, rs = scratch

        def block(to):
            if rows is None:
                return x_ref.at[to]
            return x_ref.at[:rows, column_block(to, blocks[2])]

        def copy(d):
            to = lax.rem(p.f + d, size)
            return rcopy(block(to), o_ref.at[p.f], ss.at[d], rs.at[d], {"fsdp": to})

        def local():
            return pltpu.make_async_copy(block(p.f), o_ref.at[p.f], lsem)

        local().start()
        for d in range(1, size):
            copy(d).start()
        yield
        local().wait()
        for d in range(1, size):
            copy(d).wait()

    return Job(
        run, [(x, ANY)], [(like(blocks, x.dtype), ANY)], [DMA, DMA((size,)), DMA((size,))]
    )


def ctx_gather_job(x):
    def run(p, ins, outs, scratch):
        (x_ref,), (o_ref,) = ins, outs
        share = Share(p, lambda d, q: o_ref.at[q], 1, scratch[1:])

        def local():
            return pltpu.make_async_copy(x_ref, o_ref.at[p.c], scratch[0])

        def first(to, ss, rs):
            return rcopy(x_ref, o_ref.at[p.c], ss.at[0], rs.at[0], {"ctx": to})

        local().start()
        first(p.far, share.fs, share.fr).start()
        first(p.near, share.ns, share.nr).start()
        yield
        share.forward(0)
        yield
        local().wait()
        share.finish()

    return Job(
        run, [(x, ANY)], [(like((4,) + x.shape, x.dtype), ANY)], [DMA] + share_sems(1)
    )


class Halve:
    def __init__(self, p, source, bufs, sems, here=False):
        self.p, self.source, self.here = p, source, here
        self.own, self.got, self.away, self.total = bufs
        self.ls, self.ns, self.nr, self.fs, self.fr = sems
        self.count, self.rows = self.total.shape[:2]

    def local(self, i):
        q = self.p.c if i == 0 else self.p.far
        return pltpu.make_async_copy(self.source(q), self.own.at[i], self.ls.at[i])

    def mine_of(self, i, j):
        if self.here:
            return self.source(self.p.c if i == 0 else self.p.far).at[j]
        return self.own.at[i, j]

    def to_near(self, i):
        q = self.p.near if i == 0 else self.p.other
        return rcopy(
            self.source(q), self.got.at[i], self.ns.at[i], self.nr.at[i], {"ctx": self.p.near}
        )

    def index(self, k):
        return lax.rem(self.p.f + k, self.count) if self.count == self.p.size else k

    def to_far(self, k):
        j = self.index(k)
        return rcopy(
            self.own.at[1, j], self.away.at[j], self.fs.at[k], self.fr.at[k], {"ctx": self.p.far}
        )

    def start(self):
        if not self.here:
            for i in (1, 0):
                self.local(i).start()
        for i in (1, 0):
            self.to_near(i).start()

    def send(self):
        if not self.here:
            self.local(1).wait()
        self.to_near(1).wait_recv()
        for k in range(self.count):
            j = self.index(k)
            terms = [self.mine_of(1, j), self.got.at[1, j]]
            add_blocks(self.own.at[1, j], terms, bf16, self.rows)
            self.to_far(k).start()

    def mine(self):
        if not self.here:
            self.local(0).wait()
        self.to_near(0).wait_recv()

    def block(self, k):
        self.to_far(k).wait_recv()
        j = self.index(k)
        add_blocks(
            self.total.at[j],
            [self.mine_of(0, j), self.got.at[0, j], self.away.at[j]],
            bf16,
            self.rows,
        )

    def finish(self):
        for i in range(2):
            self.to_near(i).wait_send()
        for j in range(self.count):
            self.to_far(j).wait_send()


def halve_scratch(count, rows, cols, total=True):
    return [
        pltpu.VMEM((2, count, rows, cols), bf16),
        pltpu.VMEM((2, count, rows, cols), bf16),
        pltpu.VMEM((count, rows, cols), bf16),
    ] + [pltpu.VMEM((count, rows, cols), bf16)] * total + [
        DMA((2,)),
        DMA((2,)),
        DMA((2,)),
        DMA((count,)),
        DMA((count,)),
    ]


def halve_job(x, columns=True):
    n, rows, cols = x.shape
    shape = (n, rows, cols // 4) if columns else (n // 4, rows, cols)

    def run(p, ins, outs, scratch):
        (x_ref,), (o_ref,) = ins, outs

        def source(q):
            if columns:
                return x_ref.at[:, :, column_block(q, shape[2])]
            return x_ref.at[pl.ds(q * shape[0], shape[0])]

        halve = Halve(p, source, list(scratch[:3]) + [o_ref], scratch[3:])
        halve.start()
        yield
        halve.send()
        yield
        halve.mine()
        for j in range(shape[0]):
            halve.block(j)
            if j % 2 == 1:
                yield
        halve.finish()

    return Job(run, [(x, ANY)], [(like(shape, bf16), VM)], halve_scratch(*shape, total=False))


def home_job(wgrad, size):
    _, depth, total = wgrad.shape
    quarter = total // 4

    def run(p, ins, outs, scratch):
        (w_ref,), (h_ref,) = ins, outs
        halve = Halve(
            p, lambda q: w_ref.at[:, :, column_block(q, quarter)], scratch[:4], scratch[4:9]
        )
        lsem, ws, wr = scratch[9:12]

        def view(d, q):
            return h_ref.at[lax.rem(p.f - d + size, size), :, column_block(q, quarter)]

        def local():
            return pltpu.make_async_copy(halve.total.at[p.f], view(0, p.c), lsem)

        def move(d):
            to = lax.rem(p.f + d, size)
            return rcopy(halve.total.at[to], view(0, p.c), ws.at[d], wr.at[d], {"fsdp": to})

        def came(d):
            ref = view(d, p.c)
            rcopy(ref, ref, ws.at[d], wr.at[d], {"fsdp": lax.rem(p.f + d, size)}).wait_recv()

        share = Share(p, view, size, scratch[12:])
        halve.start()
        yield
        halve.send()
        yield
        halve.mine()
        for k in range(size):
            halve.block(k)
            if k == 0:
                local().start()
                share.send(0, halve.total.at[p.f])
            else:
                move(k).start()
            if k % 2 == 1:
                yield
        for d in range(1, size):
            came(d)
            share.send(d)
            if d % 2 == 0:
                yield
        for d in range(size):
            share.forward(d)
            if d % 4 == 3:
                yield
        local().wait()
        share.finish()
        halve.finish()
        for d in range(1, size):
            move(d).wait_send()

    return Job(
        run,
        [(wgrad, ANY)],
        [(like((size, depth, total), bf16), ANY)],
        halve_scratch(size, depth, quarter)
        + [DMA, DMA((size,)), DMA((size,))]
        + share_sems(size),
    )


def deliver_job(piece, size):
    _, depth, quarter = piece.shape

    def run(p, ins, outs, scratch):
        (x_ref,), (h_ref,) = ins, outs
        lsem, ws, wr = scratch[:3]

        def view(d, q):
            return h_ref.at[lax.rem(p.f - d + size, size), :, column_block(q, quarter)]

        def local():
            return pltpu.make_async_copy(x_ref.at[p.f], view(0, p.c), lsem)

        def move(d):
            to = lax.rem(p.f + d, size)
            return rcopy(x_ref.at[to], view(0, p.c), ws.at[d], wr.at[d], {"fsdp": to})

        def came(d):
            ref = view(d, p.c)
            rcopy(ref, ref, ws.at[d], wr.at[d], {"fsdp": lax.rem(p.f + d, size)}).wait_recv()

        share = Share(p, view, size, scratch[3:])
        local().start()
        for d in range(1, size):
            move(d).start()
        share.send(0, x_ref.at[p.f])
        yield
        for d in range(1, size):
            came(d)
            share.send(d)
            if d % 4 == 3:
                yield
        for d in range(size):
            share.forward(d)
            if d % 4 == 3:
                yield
        local().wait()
        share.finish()
        for d in range(1, size):
            move(d).wait_send()

    return Job(
        run,
        [(piece, ANY)],
        [(like((size, depth, 4 * quarter), bf16), ANY)],
        [DMA, DMA((size,)), DMA((size,))] + share_sems(size),
    )


def ctx_sum_job(x, used=None):
    rows, cols = (x.shape[0] if used is None else used) // 4, x.shape[1]
    x = x[None]

    def run(p, ins, outs, scratch):
        (x_ref,), (o_ref,) = ins, outs
        def source(q):
            return x_ref.at[:, pl.ds(pl.multiple_of(q * rows, 16), rows)]

        halve = Halve(p, source, scratch[:4], scratch[4:9])
        share = Share(p, lambda d, q: o_ref.at[q], 1, scratch[10:])
        halve.start()
        yield
        halve.send()
        yield
        halve.mine()
        halve.block(0)
        share.send(0, halve.total.at[0])

        def local():
            return pltpu.make_async_copy(halve.total.at[0], o_ref.at[p.c], scratch[9])

        local().start()
        yield
        share.forward(0)
        yield
        local().wait()
        share.finish()
        halve.finish()

    return Job(
        run,
        [(x, ANY)],
        [(like((4, rows, cols), bf16), ANY)],
        halve_scratch(1, rows, cols) + [DMA] + share_sems(1),
    )


def sum_job(partial, size):
    rows, tokens = partial.shape[0], partial.shape[1] // size

    def run(p, ins, outs, scratch):
        (p_ref,), (o_ref,) = ins, outs
        buf, ss, rs, gs, gr = scratch

        def at(i):
            return pl.ds(pl.multiple_of(i * tokens, 128), tokens)

        def first(d):
            to = lax.rem(p.f + d, size)
            return rcopy(p_ref.at[:, at(to)], buf.at[d], ss.at[d], rs.at[d], {"fsdp": to})

        def second(d):
            to = lax.rem(p.f + d, size)
            ref = o_ref.at[:, at(p.f)]
            return rcopy(ref, ref, gs.at[d], gr.at[d], {"fsdp": to})

        def came(d):
            ref = o_ref.at[:, at(lax.rem(p.f - d + size, size))]
            rcopy(ref, ref, gs.at[d], gr.at[d], {"fsdp": lax.rem(p.f + d, size)}).wait_recv()

        for d in range(1, size):
            first(d).start()
        yield
        total = p_ref[:, at(p.f)].astype(f32)
        for d in range(1, size):
            first(d).wait_recv()
            total += buf[d].astype(f32)
        o_ref[:, at(p.f)] = total.astype(bf16)
        for d in range(1, size):
            second(d).start()
        yield
        for d in range(1, size):
            came(d)
        for d in range(1, size):
            first(d).wait_send()
            second(d).wait_send()

    return Job(
        run,
        [(partial, VM)],
        [(like(partial.shape, bf16), VM)],
        [pltpu.VMEM((size, rows, tokens), bf16)] + [DMA((size,))] * 4,
    )


def all_sum_job(x, size, held):
    rows, cols = x.shape[1:]

    def run(p, ins, outs, scratch):
        (o_ref,), x_ref = outs, held[0]
        buf, mid, far, ss, rs, ts, tr = scratch

        def copy(d):
            to = lax.rem(p.f + d, size)
            return rcopy(x_ref.at[to], buf.at[d], ss.at[d], rs.at[d], {"fsdp": to})

        def swap(i, to):
            return rcopy(mid.at[i], far.at[i], ts.at[i], tr.at[i], {"ctx": to})

        for d in range(1, size):
            copy(d).start()
        yield
        total = x_ref[p.f]
        for d in range(1, size):
            copy(d).wait_recv()
            total += buf[d]
        mid[0] = total
        swap(0, p.near).start()
        yield
        swap(0, p.near).wait_recv()
        mid[1] = mid[0] + far[0]
        swap(1, p.far).start()
        yield
        swap(1, p.far).wait_recv()
        o_ref[...] = mid[1] + far[1]
        for d in range(1, size):
            copy(d).wait_send()
        swap(0, p.near).wait_send()
        swap(1, p.far).wait_send()

    return Job(
        run,
        [],
        [(like((rows, cols), f32), VM)],
        [pltpu.VMEM((size, rows, cols), f32)]
        + [pltpu.VMEM((2, rows, cols), f32)] * 2
        + [DMA((size,)), DMA((size,)), DMA((2,)), DMA((2,))],
    )


UNROLL = 8
LN2 = 0.6931471805599453


def steps(length, body, init):
    count = UNROLL if length % UNROLL == 0 else 1

    def some(i, carry):
        for j in range(count):
            carry = body(i * count + j, carry)
        return carry

    return lax.fori_loop(0, length // count, some, init)


class Product:
    def __init__(self, left, right, size, transposed=False):
        rows_all = left.shape[0]
        width = right.shape[0 if transposed else 1]
        self.size, self.rows, self.transposed = size, rows_all // size, transposed
        self.shape = like((size, self.rows, width), bf16)
        self.ins = [(left, VM), (right, VM)]
        self.scratch = [pltpu.VMEM(self.shape.shape, bf16)]
        self.held = []

    def stages(self, p, left, right, out, also=None):
        self.held.append(out)
        contract = (((1,), (1 if self.transposed else 0,)), ((), ()))

        def block(i):
            at = pl.ds(pl.multiple_of(i * self.rows, self.rows), self.rows)
            got = lax.dot_general(
                left[at, :], right[...], contract, preferred_element_type=f32
            ).astype(bf16)
            out[i] = got
            if also is not None:
                also(at, got)

        def partner(k):
            block(2 * k + 1 - p.b)

        def own(k):
            block(2 * k + p.b)

        return [(self.size // 2, partner), (self.size // 2, own)]


class Scan:
    def __init__(self, streams, length, chan):
        self.width = math.gcd(streams, 8)
        self.groups, self.tiles, self.length = streams // self.width, chan // 128, length
        self.pieces = 2 * self.groups * self.tiles

    def piece(self, i):
        tile = lax.rem(i, self.tiles)
        rest = i // self.tiles
        return lax.rem(rest, self.groups), rest // self.groups, tile

    def lanes(self, tile):
        return pl.ds(pl.multiple_of(tile * 128, 128), 128)

    def rows(self, group, block, o):
        first = group * (self.width * 2 * self.length) + block * self.length + o
        return pl.ds(first, self.width, stride=2 * self.length)

    def spread(self, wr, group, block, out, column):
        def body(o, carry):
            values = wr[self.rows(group, block, o), :]
            for n in range(NS):
                out[o, n] = jnp.broadcast_to(
                    values[:, column + n : column + n + 1], (self.width, 128)
                )
            return carry

        steps(self.length, body, 0)

    def tiled(self):
        return pltpu.VMEM((self.tiles, self.groups * self.width * 2 * self.length, 128), f32)

    def tile_copies(self, flat, tiled, sems, out=False):
        copies = []
        for t in range(self.tiles):
            there = flat.at[:, t * 128 : (t + 1) * 128]
            pair = (tiled.at[t], there) if out else (there, tiled.at[t])
            copies.append(pltpu.make_async_copy(*pair, sems.at[t]))
        return copies

    def zero(self):
        return jnp.zeros((self.width, 128), f32)

    def link(self, order, b, ends, group, lanes, rates):
        at = order[b]
        total = ends[at, group, NS, :, lanes].astype(f32)
        return at, [jnp.exp2(total * rate) for rate in rates]

    def link_shape(self, blocks, chan, extra):
        return (blocks, self.groups, NS + extra, self.width, chan)


def hosted(loops, jobs, size, cid, name, ins, outs, scratch, plan):
    n_in, n_out = len(ins), len(outs)
    job_in = sum(len(job.ins) for job in jobs)
    job_out = sum(len(job.outs) for job in jobs)

    def kernel(*refs):
        place = Place(size)
        place.greet()
        own_in, refs = refs[:n_in], refs[n_in:]
        ins_, refs = part(refs[:job_in], jobs, "ins"), refs[job_in:]
        own_out, refs = refs[:n_out], refs[n_out:]
        outs_, refs = part(refs[:job_out], jobs, "outs"), refs[job_out:]
        own_scratch, refs = refs[: len(scratch)], refs[len(scratch) :]
        scratch_ = part(refs, jobs, "scratch")
        moving = Moving(
            [job.steps(place, i, o, s) for job, i, o, s in zip(jobs, ins_, outs_, scratch_)]
        )
        for at, stage in enumerate(loops(place, own_in, own_out, own_scratch)):
            for which in plan.get(at, ()):
                moving.step(which)
            if callable(stage):
                stage()
                continue
            count, body = stage

            def whole(i, carry):
                body(i)
                for k in range(count):
                    if plan.get((at, k)):
                        @pl.when(i == k)
                        def _():
                            for which in plan[at, k]:
                                moving.step(which)

                return carry

            lax.fori_loop(0, count, whole, 0)
        for which in plan.get("end", ()):
            moving.step(which)
        moving.drain()

    got = pl.pallas_call(
        kernel,
        out_shape=[shape for shape, _ in outs] + [shape for job in jobs for shape, _ in job.outs],
        in_specs=[spec for _, spec in ins] + [spec for job in jobs for _, spec in job.ins],
        out_specs=[spec for _, spec in outs] + [spec for job in jobs for _, spec in job.outs],
        scratch_shapes=list(scratch) + [item for job in jobs for item in job.scratch],
        compiler_params=params(cid, 63 << 20),
        name=name,
    )(*[array for array, _ in ins], *[array for job in jobs for array, _ in job.ins])
    return got[:n_out], part(got[n_out:], jobs, "outs")


SM = pl.BlockSpec(memory_space=pltpu.SMEM)


def scan_forward(order, dt, x, wr, rate2, streams, jobs, size, cid, plan):
    chan = dt.shape[1]
    scan = Scan(streams, dt.shape[0] // streams // 2, chan)
    blocks = order.shape[0] - 2
    length = scan.length

    def loops(p, ins, outs, scratch):
        order_ref, dt_flat, x_flat, wr_ref, rate_ref = ins
        y_flat, s_ref, ends_ref = outs
        wb, rb, dt_ref, x_ref, y_ref, dt_sem, x_sem, y_sem = scratch[:8]
        share = Share(p, lambda d, q: ends_ref.at[pl.ds(2 * q, 2)], 1, scratch[8:])

        def load():
            copies = scan.tile_copies(dt_flat, dt_ref, dt_sem)
            copies += scan.tile_copies(x_flat, x_ref, x_sem)
            for copy in copies:
                copy.start()
            for copy in copies:
                copy.wait()

        def store():
            copies = scan.tile_copies(y_flat, y_ref, y_sem, True)
            for copy in copies:
                copy.start()
            for copy in copies:
                copy.wait()

        def ends(i):
            group, block, tile = scan.piece(i)
            lanes = scan.lanes(tile)

            @pl.when(tile == 0)
            def _():
                scan.spread(wr_ref, group, block, wb, 0)

            rates = [rate_ref[n : n + 1, lanes] for n in range(NS)]

            def body(o, carry):
                total, states = carry
                at = scan.rows(group, block, o)
                step = dt_ref[tile, at, :]
                pushed = step * x_ref[tile, at, :]
                states = tuple(
                    jnp.exp2(step * rates[n]) * states[n] + wb[o, n] * pushed for n in range(NS)
                )
                return (total + step, states)

            total, states = steps(length, body, (scan.zero(), (scan.zero(),) * NS))
            mine = 2 * p.c + block
            for n in range(NS):
                ends_ref[mine, group, n, :, lanes] = states[n].astype(bf16)
            ends_ref[mine, group, NS, :, lanes] = total.astype(bf16)

        def send():
            share.send(0)

        def arrive():
            share.forward(0)
            share.finish()

        def forward(i):
            group, block, tile = scan.piece(i)
            lanes = scan.lanes(tile)

            @pl.when(tile == 0)
            def _():
                scan.spread(wr_ref, group, block, wb, 0)
                scan.spread(wr_ref, group, block, rb, NS)

            rates = [rate_ref[n : n + 1, lanes] for n in range(NS)]
            mine = order_ref[blocks + block]

            def link(b, states):
                at, decays = scan.link(order_ref, b, ends_ref, group, lanes, rates)
                return tuple(
                    jnp.where(
                        b < mine,
                        decays[n] * states[n] + ends_ref[at, group, n, :, lanes].astype(f32),
                        states[n],
                    )
                    for n in range(NS)
                )

            states = lax.fori_loop(0, blocks - 1, link, (scan.zero(),) * NS)
            for n in range(NS):
                s_ref[block, group, n, :, lanes] = states[n]

            def body(o, states):
                at = scan.rows(group, block, o)
                step = dt_ref[tile, at, :]
                pushed = step * x_ref[tile, at, :]
                states = tuple(
                    jnp.exp2(step * rates[n]) * states[n] + wb[o, n] * pushed for n in range(NS)
                )
                total = [rb[o, n] * states[n] for n in range(NS)]
                while len(total) > 1:
                    total = [total[j] + total[j + 1] for j in range(0, len(total), 2)]
                y_ref[tile, at, :] = total[0]
                return states

            steps(length, body, states)

        return [load, (scan.pieces, ends), send, arrive, (scan.pieces, forward), store]

    spread = pltpu.VMEM((length, NS, scan.width, 128), f32)
    return hosted(
        loops,
        jobs,
        size,
        cid,
        "scan_forward",
        [(order, SM), (dt, ANY), (x, ANY), (wr, VM), (rate2, VM)],
        [
            (like(dt.shape, f32), ANY),
            (like(scan.link_shape(2, chan, 0), f32), VM),
            (like(scan.link_shape(blocks, chan, 1), bf16), VM),
        ],
        [spread, spread] + [scan.tiled()] * 3 + [DMA((scan.tiles,))] * 3 + share_sems(1),
        plan,
    )


def scan_backward(
    order, dt, x, g, wr, rate2, starts, ends, product, streams, jobs, size, cid, plan
):
    chan = dt.shape[1]
    scan = Scan(streams, dt.shape[0] // streams // 2, chan)
    blocks = order.shape[0] - 2
    length, width = scan.length, scan.width

    def loops(p, ins, outs, scratch):
        order_ref, dt_flat, x_flat, g_flat, wr_ref, rate_ref, start_ref, ends_ref = ins[:8]
        sb_flat, cw_flat, wrb_ref, dec_ref = outs
        backs_ref, wb, rb, kept, decays, wparts, rparts, sums = scratch[:8]
        dt_ref, x_ref, g_ref, sb_ref, cw_ref, dt_sem, x_sem, g_sem, sb_sem, cw_sem = scratch[8:18]
        share = Share(p, lambda d, q: backs_ref.at[pl.ds(2 * q, 2)], 1, scratch[18:24])
        extra = product.stages(p, *ins[8:], scratch[24]) if product else []

        def load():
            copies = scan.tile_copies(dt_flat, dt_ref, dt_sem)
            copies += scan.tile_copies(x_flat, x_ref, x_sem)
            copies += scan.tile_copies(g_flat, g_ref, g_sem)
            for copy in copies:
                copy.start()
            for copy in copies:
                copy.wait()

        def store():
            copies = scan.tile_copies(sb_flat, sb_ref, sb_sem, True)
            copies += scan.tile_copies(cw_flat, cw_ref, cw_sem, True)
            for copy in copies:
                copy.start()
            for copy in copies:
                copy.wait()

        def backs(i):
            group, block, tile = scan.piece(i)
            lanes = scan.lanes(tile)

            @pl.when(tile == 0)
            def _():
                scan.spread(wr_ref, group, block, rb, NS)

            rates = [rate_ref[n : n + 1, lanes] for n in range(NS)]

            def body(j, carries):
                o = length - 1 - j
                at = scan.rows(group, block, o)
                step = dt_ref[tile, at, :]
                grad = g_ref[tile, at, :]
                return tuple(
                    jnp.exp2(step * rates[n]) * (carries[n] + rb[o, n] * grad) for n in range(NS)
                )

            carries = steps(length, body, (scan.zero(),) * NS)
            mine = 2 * p.c + block
            for n in range(NS):
                backs_ref[mine, group, n, :, lanes] = carries[n].astype(bf16)

        def send():
            share.send(0)

        def arrive():
            share.forward(0)
            share.finish()

        def both(i):
            @pl.when(lax.rem(i, 2) == 0)
            def _():
                again(i // 2)

            @pl.when(lax.rem(i, 2) == 1)
            def _():
                backward(i // 2)

        def again(i):
            group, block, tile = scan.piece(i)
            lanes = scan.lanes(tile)

            @pl.when(tile == 0)
            def _():
                scan.spread(wr_ref, group, block, wb, 0)
                scan.spread(wr_ref, group, block, rb, NS)
                sums[...] = jnp.zeros_like(sums)

            rates = [rate_ref[n : n + 1, lanes] for n in range(NS)]

            def forward(o, states):
                at = scan.rows(group, block, o)
                step = dt_ref[tile, at, :]
                pushed = step * x_ref[tile, at, :]
                new = []
                for n in range(NS):
                    decay = jnp.exp2(step * rates[n])
                    decays[o, n] = decay
                    kept[o, n] = states[n]
                    new.append(decay * states[n] + wb[o, n] * pushed)
                return tuple(new)

            first = tuple(start_ref[block, group, n, :, lanes] for n in range(NS))
            last = steps(length, forward, first)
            for n in range(NS):
                kept[length, n] = last[n]

        def backward(i):
            group, block, tile = scan.piece(i)
            lanes = scan.lanes(tile)
            rates = [rate_ref[n : n + 1, lanes] for n in range(NS)]
            mine = order_ref[blocks + block]

            def link(j, carries):
                b = blocks - 1 - j
                at, decay = scan.link(order_ref, b, ends_ref, group, lanes, rates)
                return tuple(
                    jnp.where(
                        b > mine,
                        backs_ref[at, group, n, :, lanes].astype(f32) + decay[n] * carries[n],
                        carries[n],
                    )
                    for n in range(NS)
                )

            carries = lax.fori_loop(0, blocks - 1, link, (scan.zero(),) * NS)
            for n in range(NS):
                dec_ref[block, group, n, :, lanes] = scan.zero()

            def body(j, carries):
                o = length - 1 - j
                at = scan.rows(group, block, o)
                step = dt_ref[tile, at, :]
                value = x_ref[tile, at, :]
                grad = g_ref[tile, at, :]
                pushed = step * value
                slope, pulled, new = [], [], []
                to = pl.ds(pl.multiple_of(o * width, width), width)
                for n in range(NS):
                    full = carries[n] + rb[o, n] * grad
                    moved = decays[o, n] * full
                    new.append(moved)
                    back = moved * kept[o, n]
                    slope.append(back * rates[n])
                    dec_ref[block, group, n, :, lanes] += back * step
                    pulled.append(full * wb[o, n])
                    wparts[to, n * 128 : (n + 1) * 128] = full * pushed
                    rparts[to, n * 128 : (n + 1) * 128] = kept[o + 1, n] * grad
                while len(slope) > 1:
                    slope = [slope[j] + slope[j + 1] for j in range(0, len(slope), 2)]
                    pulled = [pulled[j] + pulled[j + 1] for j in range(0, len(pulled), 2)]
                sb_ref[tile, at, :] = slope[0] * LN2 + pulled[0] * value
                cw_ref[tile, at, :] = pulled[0]
                return tuple(new)

            steps(length, body, carries)
            source = lax.broadcasted_iota(jnp.int32, (NS * 128, 128), 0) // 128
            target = lax.broadcasted_iota(jnp.int32, (NS * 128, 128), 1)
            pick_w = jnp.where(source == target, 1.0, 0.0).astype(bf16)
            pick_r = jnp.where(source + NS == target, 1.0, 0.0).astype(bf16)
            sums[...] += jnp.dot(
                wparts[...].astype(bf16), pick_w, preferred_element_type=f32
            ) + jnp.dot(rparts[...].astype(bf16), pick_r, preferred_element_type=f32)

            @pl.when(tile == scan.tiles - 1)
            def _():
                def out(o, carry):
                    wrb_ref[scan.rows(group, block, o), :] = sums[
                        pl.ds(pl.multiple_of(o * width, width), width), :
                    ]
                    return carry

                steps(length, out, 0)

        return extra + [load, (scan.pieces, backs), send, arrive, (2 * scan.pieces, both), store]

    spread = pltpu.VMEM((length, NS, width, 128), f32)
    parts = pltpu.VMEM((length * width, NS * 128), f32)
    return hosted(
        loops,
        jobs,
        size,
        cid,
        "scan_backward",
        [
            (order, SM), (dt, ANY), (x, ANY), (g, ANY), (wr, VM), (rate2, VM), (starts, VM), (ends, VM),
        ]
        + (product.ins if product else []),
        [
            (like(dt.shape, f32), ANY),
            (like(dt.shape, f32), ANY),
            (like((dt.shape[0], 128), f32), VM),
            (like(scan.link_shape(2, chan, 0), f32), VM),
        ],
        [
            pltpu.VMEM(scan.link_shape(blocks, chan, 0), bf16),
            spread,
            spread,
            pltpu.VMEM((length + 1, NS, width, 128), f32),
            spread,
            parts,
            parts,
            pltpu.VMEM((length * width, 128), f32),
        ]
        + [scan.tiled()] * 5
        + [DMA((scan.tiles,))] * 5
        + share_sems(1)
        + (product.scratch if product else []),
        plan,
    )


def attention_forward(q_t, k, v_t, bias_t, product, jobs, size, cid, plan):
    rows = q_t.shape[1]
    group = H // KV

    def loops(p, ins, outs, scratch):
        q_ref, k_ref, v_ref, bias_ref = ins[:4]
        o_ref, log_ref = outs

        def head(h):
            at = pl.ds(pl.multiple_of(h * HD, HD), HD)
            g = h // group
            scores = (
                jnp.dot(k_ref[g], q_ref[at, :], preferred_element_type=f32) * score_scale
                + bias_ref[...]
            )
            largest = jnp.max(scores, axis=0, keepdims=True)
            expo = jnp.exp(scores - largest)
            total = jnp.sum(expo, axis=0, keepdims=True)
            probs = (expo * (1.0 / total)).astype(bf16)
            values = v_ref[pl.ds(pl.multiple_of(g * HD, HD), HD), :]
            o_ref[at, :] = jnp.dot(values, probs, preferred_element_type=f32).astype(bf16)
            log_ref[pl.ds(h, 1), :] = largest + jnp.log(total)

        return product.stages(p, *ins[4:], scratch[0]) + [(H, head)]

    return hosted(
        loops,
        jobs,
        size,
        cid,
        "attention_forward",
        [(q_t, VM), (k, VM), (v_t, VM), (bias_t, VM)] + product.ins,
        [(like(q_t.shape, bf16), VM), (like((H, rows), f32), VM)],
        product.scratch,
        plan,
    )


def attention_backward(q_t, k, k_t, v, bias_t, log_total, dout_t, jobs, size, cid, plan):
    group = H // KV
    keys = k.shape[1]

    def loops(p, ins, outs, scratch):
        q_ref, k_ref, kt_ref, v_ref, bias_ref, log_ref, do_ref = ins
        dq_ref, dkv_ref = outs
        contract = (((1,), (1,)), ((), ()))

        def zero():
            dkv_ref[...] = jnp.zeros_like(dkv_ref)

        def head(h):
            at = pl.ds(pl.multiple_of(h * HD, HD), HD)
            g = h // group
            to_k = pl.ds(pl.multiple_of(g * HD, HD), HD)
            to_v = pl.ds(pl.multiple_of((KV + g) * HD, HD), HD)
            query, dout = q_ref[at, :], do_ref[at, :]
            scores = (
                jnp.dot(k_ref[g], query, preferred_element_type=f32) * score_scale + bias_ref[...]
            )
            probs = jnp.exp(scores - log_ref[pl.ds(h, 1), :])
            back = jnp.dot(v_ref[g], dout, preferred_element_type=f32)
            centre = jnp.sum(probs * back, axis=0, keepdims=True)
            score_back = (probs * (back - centre)).astype(bf16)
            dq_ref[at, :] = (
                jnp.dot(kt_ref[to_k, :], score_back, preferred_element_type=f32) * score_scale
            ).astype(bf16)
            dkv_ref[to_k, :] += score_scale * lax.dot_general(
                query, score_back, contract, preferred_element_type=f32
            )
            dkv_ref[to_v, :] += lax.dot_general(
                dout, probs.astype(bf16), contract, preferred_element_type=f32
            )

        return [zero, (H, head)]

    return hosted(
        loops,
        jobs,
        size,
        cid,
        "attention_backward",
        [
            (q_t, VM), (k, VM), (k_t, VM), (v, VM), (bias_t, VM), (log_total, VM), (dout_t, VM),
        ],
        [(like(q_t.shape, bf16), VM), (like((2 * KV * HD, keys), f32), VM)],
        [],
        plan,
    )


def start_exchange(rows_in, gains, first, ffn, first_pack, ffn_pack, size, cid):
    depth = first[0].shape[0]
    n_first = len(first)
    weights = list(first) + list(ffn)
    (first_cuts, first_at, first_total), (ffn_cuts, ffn_at, ffn_total) = first_pack, ffn_pack
    held = []

    def loops(p, ins, outs, scratch):
        (packed_ref,) = outs
        mine, sems = scratch[1 : 1 + len(weights)], scratch[-1]
        held.append(scratch[0])

        def load(which):
            return pltpu.make_async_copy(ins[which], mine[which], sems.at[which])

        def begin():
            for which in range(len(weights)):
                load(which).start()

        def pack_first():
            for which in range(n_first):
                load(which).wait()
            pack_columns(mine[:n_first], scratch[0], first_cuts, first_at, size)

        def pack_ffn():
            for which in range(n_first, len(weights)):
                load(which).wait()
            pack_columns(mine[n_first:], packed_ref, ffn_cuts, ffn_at, size)

        return [begin, pack_first, pack_ffn]

    packed = like((size, depth, first_total), bf16)
    return hosted(
        loops,
        [gather_job(rows_in, size), spread_job(gains, size), move_job(packed, size, held)],
        size,
        cid,
        "start",
        [(item, ANY) for item in weights],
        [(like((size, depth, ffn_total), bf16), VM)],
        [pltpu.VMEM(packed.shape, bf16)]
        + [pltpu.VMEM(item.shape, bf16) for item in weights]
        + [DMA((len(weights),))],
        PLAN_START,
    )


def ffn_sums(low, back, hidden, grads, product, jobs, size, cid):
    rows, width = low.shape
    total, units = back.shape[1], hidden.shape[1]
    depth, quarter = width // size, total // 4
    contract = (((0,), (0,)), ((), ()))

    def loops(p, ins, outs, scratch):
        low_ref, back_ref, hidden_ref, grads_ref = ins[:4]
        quarter_ref, down_ref = outs
        whole = scratch[0]
        halve = Halve(
            p,
            lambda q: whole.at[:, :, column_block(q, quarter)],
            list(scratch[1:4]) + [quarter_ref],
            scratch[4:9],
            True,
        )
        per = quarter // 128
        extra = product.stages(p, back_ref, ins[4], scratch[9]) if product else []

        def tile_of(first, second):
            def tile(i):
                tile_at(jnp.where(i < per, first * per + i, second * per + i - per))

            return tile

        def tile_at(i):
            lanes = column_block(i, 128)
            got = lax.dot_general(
                low_ref[...], back_ref[:, lanes], contract, preferred_element_type=f32
            )
            for f in range(size):
                whole[f, :, lanes] = got[f * depth : (f + 1) * depth, :].astype(bf16)

        def down_tile(i):
            lanes = column_block(i, 128)
            down_ref[pl.ds(pl.multiple_of(i * 128, 128), 128), :] = lax.dot_general(
                hidden_ref[:, lanes], grads_ref[...], contract, preferred_element_type=f32
            ).astype(bf16)

        def sums():
            halve.mine()
            for k in range(size):
                halve.block(k)
            halve.finish()

        return extra + [
            (2 * per, tile_of(p.other, p.near)),
            halve.start,
            (per, tile_of(p.far, p.far)),
            halve.send,
            (per, tile_of(p.c, p.c)),
            (units // 128, down_tile),
            sums,
        ]

    return hosted(
        loops,
        jobs,
        size,
        cid,
        "ffn_sums",
        [(low, VM), (back, VM), (hidden, VM), (grads, VM)] + (product.ins[1:] if product else []),
        [(like((size, depth, quarter), bf16), VM), (like((units, width), bf16), VM)],
        [pltpu.VMEM((size, depth, total), bf16)]
        + halve_scratch(size, depth, quarter, False)
        + (product.scratch if product else []),
        PLAN_FFN,
    )


def finish(wgrad, product, normed, gain, gain_rows, small, size, cid):
    width = normed.shape[1]
    held_gains = []

    def loops(p, ins, outs, scratch):
        left_ref, right_ref, normed_ref, gain_ref, gain_rows_ref = ins
        part_ref, total_ref, gains_ref = scratch
        held_gains.append(gains_ref)

        def begin():
            total_ref[...] = jnp.zeros_like(total_ref)

        def add_gain(at, got):
            product_ = got.astype(f32) * normed_ref[at, :].astype(f32)
            total_ref[...] += jnp.sum(product_, axis=0, keepdims=True)

        def gains():
            gains_ref[...] = gain_rows_ref[...]
            first = total_ref[...] / gain_ref[...]
            cols = width // size
            for f in range(size):
                gains_ref[f, 0:1, :] = first[:, f * cols : (f + 1) * cols]

        return [begin] + product.stages(p, left_ref, right_ref, part_ref, add_gain) + [gains]

    return hosted(
        loops,
        [
            scatter_job(product.shape, size, product.held),
            home_job(wgrad, size),
            ctx_sum_job(small),
            all_sum_job(gain_rows, size, held_gains),
        ],
        size,
        cid,
        "finish",
        product.ins + [(normed, VM), (gain, VM), (gain_rows, VM)],
        [],
        product.scratch + [pltpu.VMEM((1, width), f32), pltpu.VMEM(gain_rows.shape, f32)],
        PLAN_FINISH,
    )


PLAN_START = {1: (0, 1), 2: (0, 2), "end": (0, 2)}
PLAN_FORWARD = {
    1: (3, 2),
    (1, 2): (2,),
    (1, 4): (2, 3),
    (1, 6): (2,),
    3: (1,),
    (4, 0): (2, 0),
    (4, 1): (1,),
    (4, 3): (1, 0, 3),
    (4, 4): (1, 2),
    (4, 5): (0,),
    (4, 6): (1,),
    (4, 7): (0, 2),
}
PLAN_ATTEND = {1: (0,), (2, 2): (0,), (2, 12): (0,), (2, 22): (0,)}
PLAN_FFN = {1: (0,), (2, 2): (0,), 5: (0,), (7, 1): (0,)}
PLAN_ATTEND_BACK = {
    0: (0, 1),
    (1, 5): (1,),
    (1, 9): (0,),
    (1, 16): (0,),
    "end": (0, 1, 1, 1, 0),
}
PLAN_FINISH = {
    0: (1, 2),
    (1, 1): (1, 2),
    (1, 3): (1,),
    2: (0, 1),
    (2, 1): (1,),
    3: (1, 0),
    "end": (3, 1, 1, 0, 2, 1, 3, 1, 0, 1, 1, 3, 2, 0),
}
PLAN_BACKWARD = {
    3: (4, 3),
    (3, 2): (3,),
    (3, 4): (4,),
    (3, 7): (0,),
    (6, 0): (4, 3),
    (6, 1): (1,),
    (6, 2): (4, 0),
    (6, 5): (0, 3, 4),
    (6, 6): (1, 2),
    (6, 7): (0, 2),
    (6, 8): (1,),
    (6, 9): (0, 2),
    (6, 10): (1, 3),
    (6, 12): (0, 2),
    (6, 13): (1,),
    (6, 15): (2,),
}


def column_grads(x, dy):
    return jnp.einsum("ld,lk->dk", x, dy, preferred_element_type=f32).astype(bf16)


def on_device(
    layer_in,
    out_grad,
    doc_lengths,
    block_deal,
    norm_gains,
    query_weight,
    keyval_weight,
    attn_proj,
    mamba_in,
    conv_taps,
    conv_bias,
    step_bias,
    skip_gain,
    decay_log,
    select_proj,
    step_proj,
    mamba_proj,
    gate_weight,
    up_weight,
    down_weight,
):
    size = lax.axis_size("fsdp")
    n_ctx = lax.axis_size("ctx")
    rows = layer_in.shape[1]
    half_rows = rows // 2
    width = layer_in.shape[2]
    blocks_all = 2 * n_ctx
    group = H // KV
    chan = INNER // size
    q_cols, kv_cols = H * HD // size, 2 * KV * HD // size
    ff_cols = gate_weight.shape[1] // size
    rows_all = size * rows
    ctx_place = lax.axis_index("ctx")
    deal_flat = block_deal.reshape(-1)
    my_blocks = lax.dynamic_slice_in_dim(block_deal, ctx_place, 1, 0)[0]
    offsets = jnp.arange(half_rows, dtype=jnp.int32)
    my_places = (my_blocks[:, None] * half_rows + offsets[None, :]).reshape(-1)
    key_places = (deal_flat[:, None] * half_rows + offsets[None, :]).reshape(-1)
    lengths = doc_lengths[0]
    starts = jnp.cumsum(lengths) - lengths

    def segment(places):
        return jnp.sum((places[:, None] >= starts[None, :]).astype(jnp.int32), axis=1)

    allowed = (key_places[:, None] <= my_places[None, :]) & (
        segment(key_places)[:, None] == segment(my_places)[None, :]
    )
    bias_t = jnp.where(allowed, 0.0, -1e30).astype(f32)
    inverse = jnp.argsort(deal_flat)

    depth = query_weight.shape[0]
    chan_up, qkv_up = up_to(chan, 128), up_to(q_cols + kv_cols, 128)
    ff_up = up_to(ff_cols, 128)
    first_cuts = ((0, 0, q_cols), (1, 0, kv_cols), (2, 0, chan), (2, INNER, chan))
    first_at = (0, q_cols, qkv_up, qkv_up + chan_up)
    first_total = up_to(qkv_up + 2 * chan_up, 128 * n_ctx)
    ffn_cuts = ((0, 0, ff_cols), (1, 0, ff_cols))
    ffn_at = (0, ff_up)
    ffn_total = up_to(2 * ff_up, 128 * n_ctx)
    (ffn_packed,), ((stream_all,), (gain_all,), (first_mat,)) = start_exchange(
        layer_in[0],
        norm_gains,
        (query_weight, keyval_weight, mamba_in),
        (gate_weight, up_weight),
        (first_cuts, first_at, first_total),
        (ffn_cuts, ffn_at, ffn_total),
        size,
        0,
    )
    stream_all = stream_all.reshape(rows_all, width)
    gain_float = jnp.moveaxis(gain_all, 0, 1).reshape(4, width).astype(f32)
    first_mat = first_mat.reshape(width, first_total)
    qkv_mat = first_mat[:, :qkv_up]
    entry_mat = first_mat[:, qkv_up : qkv_up + 2 * chan_up]
    ffn_quarter = ffn_total // n_ctx
    attn_wide = up_to(width, 128 * n_ctx)
    attn_packed = jnp.pad(attn_proj, ((0, 0), (0, attn_wide - width)))
    down_mat = jnp.pad(down_weight, ((0, ff_up - ff_cols), (0, 0)))
    more = chan_up - chan
    taps_mat = jnp.pad(conv_taps, ((0, 0), (0, more)))
    mamba_mat = jnp.pad(mamba_proj, ((0, more), (0, 0)))
    select_mat = jnp.pad(select_proj, ((0, more), (0, 0)))
    step_mat = jnp.pad(step_proj, ((0, 0), (0, more)))
    rate = -jnp.exp(jnp.pad(decay_log, ((0, 0), (0, more))).astype(f32))
    rate2 = rate * 1.4426950408889634
    shift_float, step_shift, skip_float = (
        jnp.pad(item, (0, more)).astype(f32) for item in (conv_bias, step_bias, skip_gain)
    )

    stream = layer_in[0].astype(f32)
    _, inv_in = norm_forward(stream, gain_float[0])
    normed_all, inv_all = norm_forward(stream_all.astype(f32), gain_float[0])
    normed_all = normed_all.astype(bf16)

    qkv_t = jnp.einsum("dk,ld->kl", qkv_mat, normed_all, preferred_element_type=f32).astype(bf16)
    entry = jnp.dot(normed_all, entry_mat, preferred_element_type=f32)
    chan = chan_up
    mixer_in = entry[:, :chan].astype(bf16)
    gate_side = entry[:, chan:]
    mixer_blocks = mixer_in.reshape(size, 2, half_rows, chan)
    tails = mixer_blocks[:, :, half_rows - (CONV - 1) :]
    (qkv,), (tails_all,) = together(
        [exchange_job(qkv_t, size, up_to(q_cols + kv_cols, 8)), ctx_gather_job(tails.reshape(-1, chan))],
        size,
        1,
        "edges",
    )
    query_t = qkv[:, :q_cols].reshape(H * HD, rows)
    keyval_t = qkv[:, q_cols : q_cols + kv_cols].reshape(2 * KV * HD, rows)
    tails_all = tails_all.reshape(n_ctx, size, 2, CONV - 1, chan)

    def in_deal_order(values):
        return jnp.moveaxis(values, 2, 1).reshape((blocks_all,) + (size,) + values.shape[3:])

    def of_blocks(values, index):
        return jnp.moveaxis(jnp.take(values, index, axis=0), 0, 1)

    before_index = inverse[jnp.maximum(my_blocks - 1, 0)]
    has_before = my_blocks > 0
    prior_tail = jnp.where(
        has_before[None, :, None, None],
        of_blocks(in_deal_order(tails_all), before_index),
        jnp.zeros_like(tails),
    )
    padded = jnp.concatenate([prior_tail, mixer_blocks], axis=2).astype(f32)
    taps_float = taps_mat.astype(f32)
    conv_blocks_out = shift_float + sum(
        taps_float[offset] * padded[:, :, offset : offset + half_rows] for offset in range(CONV)
    )
    conv_out = conv_blocks_out.reshape(rows_all, chan)
    signal = jax.nn.silu(conv_out).astype(bf16)
    signal_float = signal.astype(f32)
    selected_part = jnp.einsum(
        "ik,li->kl", select_mat, signal, preferred_element_type=f32
    ).astype(bf16)
    ((selected,),) = together([sum_job(selected_part, size)], size, 3, "select")
    step_low = selected[:RANK].T
    write_read = jnp.pad(selected[RANK:], ((0, 128 - 2 * NS), (0, 0))).T.astype(f32)
    step_pre = jnp.dot(step_low, step_mat, preferred_element_type=f32) + step_shift
    step_sizes = jax.nn.softplus(step_pre)
    order = jnp.concatenate([inverse, my_blocks]).astype(jnp.int32)
    (scan_rows, start_state, ends_all), ((grads_all,), (ffn_mat,), (attn_mat,), (keyvals_all,)) = scan_forward(
        order,
        step_sizes,
        signal_float,
        write_read,
        rate2,
        size,
        [
            gather_job(out_grad[0], size),
            move_job(ffn_packed, size),
            gather_job(attn_packed, size, True),
            ctx_gather_job(keyval_t),
        ],
        size,
        4,
        PLAN_FORWARD,
    )
    keyvals_t = keyvals_all.transpose(1, 0, 2).reshape(2 * KV * HD, n_ctx * rows)
    keyvals = keyvals_t.reshape(2 * KV, HD, n_ctx * rows).transpose(0, 2, 1)
    key_groups, value_groups = keyvals[:KV], keyvals[KV:]
    grads_all = grads_all.reshape(rows_all, width)
    ffn_mat = ffn_mat.reshape(width, ffn_total)
    gate_mat, up_mat = ffn_mat[:, :ff_up], ffn_mat[:, ff_up : 2 * ff_up]
    attn_mat = attn_mat.reshape(width, attn_wide)[:, :width]
    scanned = scan_rows + skip_float * signal_float
    gate_act = jax.nn.silu(gate_side)
    mamba_rows = (scanned * gate_act).astype(bf16)
    mamba_product = Product(mamba_rows, mamba_mat, size)
    (attn_rows_t, log_totals), ((mamba_out,),) = attention_forward(
        query_t,
        key_groups,
        keyvals_t[KV * HD :],
        bias_t,
        mamba_product,
        [scatter_job(mamba_product.shape, size, mamba_product.held)],
        size,
        5,
        PLAN_ATTEND,
    )
    attn_out = jnp.einsum("hl,hd->ld", attn_rows_t, attn_mat, preferred_element_type=f32)
    attn_normed, inv_attn = norm_forward(attn_out, gain_float[1])

    mamba_normed, inv_mamba = norm_forward(mamba_out, gain_float[2])
    middle = stream + 0.5 * (attn_normed + mamba_normed)
    ffn_normed, inv_ffn = norm_forward(middle, gain_float[3])
    ((ffn_low,),) = together(
        [gather_job(ffn_normed.astype(bf16), size)], size, 6, "ffn_rows"
    )
    ffn_low = ffn_low.reshape(rows_all, width)
    gate_pre = jnp.dot(ffn_low, gate_mat, preferred_element_type=f32)
    up_pre = jnp.dot(ffn_low, up_mat, preferred_element_type=f32)
    hidden = (jax.nn.silu(gate_pre) * up_pre).astype(bf16)
    hidden_back = jnp.einsum("ld,fd->lf", grads_all, down_mat, preferred_element_type=f32)
    gate_back = (hidden_back * up_pre * silu_slope(gate_pre)).astype(bf16)
    up_back = (hidden_back * jax.nn.silu(gate_pre)).astype(bf16)
    ffn_back_low = jnp.concatenate([gate_back, up_back], axis=1)
    ffn_back_low = jnp.pad(ffn_back_low, ((0, 0), (0, ffn_total - 2 * ff_up)))
    fits = size <= 8
    if fits:
        ffn_product = Product(ffn_back_low, ffn_mat, size, True)
        ffn_jobs = [scatter_job(ffn_product.shape, size, ffn_product.held)]
    else:
        ffn_product = None
        ffn_part = jnp.einsum("lf,df->ld", ffn_back_low, ffn_mat, preferred_element_type=f32)
        ffn_jobs = [scatter_job(ffn_part.astype(bf16).reshape(size, rows, width), size)]
    (ffn_quarter_sum, down_wgrad), ffn_back = ffn_sums(
        ffn_low, ffn_back_low, hidden, grads_all, ffn_product, ffn_jobs * fits, size, 7
    )
    if not fits:
        ffn_back = together(ffn_jobs, size, 14, "ffn_sum")
    ffn_back = ffn_back[0][0]
    middle_part, ffn_gain_grad = norm_backward(ffn_back, middle, inv_ffn, gain_float[3])
    middle_back = out_grad[0].astype(f32) + middle_part
    branch_back = 0.5 * middle_back
    attn_part, attn_gain_grad = norm_backward(branch_back, attn_out, inv_attn, gain_float[1])
    mamba_part_back, mamba_gain_grad = norm_backward(
        branch_back, mamba_out, inv_mamba, gain_float[2]
    )
    attn_back = attn_part.astype(bf16)
    attn_back_wide = jnp.pad(attn_back, ((0, 0), (0, attn_wide - width)))
    attn_wgrad = jnp.einsum(
        "hl,ld->hd", attn_rows_t, attn_back_wide, preferred_element_type=f32
    ).astype(bf16)
    dout_t = jnp.einsum("hd,ld->hl", attn_mat, attn_back, preferred_element_type=f32).astype(bf16)
    (query_back_t, keyval_terms), ((mamba_back,), (attn_quarter,)) = (
        attention_backward(
            query_t,
            key_groups,
            keyvals_t[: KV * HD],
            value_groups,
            bias_t,
            log_totals,
            dout_t,
            [
                gather_job(mamba_part_back.astype(bf16), size),
                halve_job(attn_wgrad.reshape(size, depth, attn_wide)),
            ],
            size,
            8,
            PLAN_ATTEND_BACK,
        )
    )
    mamba_back = mamba_back.reshape(rows_all, width)
    mamba_wgrad = jnp.einsum("li,ld->id", mamba_rows, mamba_back, preferred_element_type=f32)
    mrows_back = jnp.einsum("ld,id->li", mamba_back, mamba_mat, preferred_element_type=f32)
    scan_back = mrows_back * gate_act
    side_back = mrows_back * scanned * silu_slope(gate_side)
    skip_grad = jnp.sum(scan_back * signal_float, axis=0)
    down_product = Product(hidden, down_mat, size) if fits else None
    if fits:
        down_jobs = [scatter_job(down_product.shape, size, down_product.held)]
    else:
        down_part = jnp.dot(hidden, down_mat, preferred_element_type=f32).astype(bf16)
        down_jobs = [scatter_job(down_part.reshape(size, rows, width), size)]
    (
        (step_back, carry_writes, read_write_back, decay_sums),
        ((ffn_home,), (attn_piece,), (mamba_share,), (down_share,), *down_out),
    ) = scan_backward(
        order,
        step_sizes,
        signal_float,
        scan_back,
        write_read,
        rate2,
        start_state,
        ends_all,
        down_product,
        size,
        [
            deliver_job(ffn_quarter_sum, size),
            scatter_job(attn_quarter, size),
            ctx_sum_job(mamba_wgrad.astype(bf16), up_to(mamba_proj.shape[0], 64)),
            ctx_sum_job(down_wgrad, up_to(ff_cols, 64)),
        ]
        + down_jobs * fits,
        size,
        9,
        PLAN_BACKWARD,
    )
    if not fits:
        down_out = together(down_jobs, size, 15, "down_sum")
    result = middle + down_out[0][0]
    decay_grad = rate * jnp.sum(decay_sums, axis=(0, 1, 3))
    signal_back = scan_back * skip_float + step_sizes * carry_writes
    read_write_back = read_write_back[:, : 2 * NS]
    pre_back = (step_back * jax.nn.sigmoid(step_pre)).astype(bf16)
    step_wgrad = jnp.einsum("lr,li->ri", step_low, pre_back, preferred_element_type=f32)
    bias_grad = jnp.sum(pre_back.astype(f32), axis=0)
    rank_back = jnp.einsum("li,ri->lr", pre_back, step_mat, preferred_element_type=f32)
    select_part = jnp.concatenate([rank_back, read_write_back], axis=1).astype(bf16).T
    (select_back,), (attn_home,), (keyval_back,) = together(
        [
            sum_job(select_part, size),
            ctx_gather_job(attn_piece.astype(bf16)),
            halve_job(keyval_terms.astype(bf16)[None]),
        ],
        size,
        10,
        "select_back",
    )
    select_back = select_back.T
    select_wgrad = jnp.einsum("li,lk->ik", signal, select_back, preferred_element_type=f32)
    signal_back = signal_back + jnp.einsum(
        "lk,ik->li", select_back, select_mat, preferred_element_type=f32
    )
    conv_back = signal_back * silu_slope(conv_out)
    conv_blocks = conv_back.reshape(size, 2, half_rows, chan)
    taps_grad = jnp.stack(
        [
            jnp.sum(conv_blocks * padded[:, :, offset : offset + half_rows], axis=(0, 1, 2))
            for offset in range(CONV)
        ]
    )
    shift_grad = jnp.sum(conv_back, axis=0)
    padded_back = sum(
        (
            jnp.pad(
                taps_float[offset] * conv_blocks,
                ((0, 0), (0, 0), (offset, CONV - 1 - offset), (0, 0)),
            )
            for offset in range(CONV)
        )
    )
    tail_back = jnp.where(has_before[None, :, None, None], padded_back[:, :, : CONV - 1], 0.0)
    keyval_back_t = keyval_back.reshape(size, kv_cols, rows)
    qkv_back_t = jnp.concatenate([query_back_t.reshape(size, q_cols, rows), keyval_back_t], axis=1)
    pad_rows = up_to(q_cols + kv_cols, 8) - q_cols - kv_cols
    qkv_back_t = jnp.pad(qkv_back_t, ((0, 0), (0, pad_rows), (0, 0)))
    (tails_back_all,), (qkv_back,) = together(
        [ctx_gather_job(tail_back.astype(bf16).reshape(-1, chan)), exchange_job(qkv_back_t, size)],
        size,
        11,
        "edges_back",
    )
    qkv_back = qkv_back.transpose(0, 2, 1).reshape(rows_all, -1)
    qkv_back = jnp.pad(qkv_back, ((0, 0), (0, qkv_up - qkv_back.shape[1])))
    tails_back_all = in_deal_order(tails_back_all.reshape(n_ctx, size, 2, CONV - 1, chan))
    after_index = inverse[jnp.minimum(my_blocks + 1, blocks_all - 1)]
    has_after = my_blocks < blocks_all - 1
    incoming = jnp.where(
        has_after[None, :, None, None], of_blocks(tails_back_all, after_index).astype(f32), 0.0
    )
    mixer_back = padded_back[:, :, CONV - 1 :] + jnp.pad(
        incoming, ((0, 0), (0, 0), (half_rows - (CONV - 1), 0), (0, 0))
    )
    entry_back = jnp.concatenate([mixer_back.reshape(rows_all, chan), side_back], axis=1).astype(
        bf16
    )
    first_back = [qkv_back, entry_back]
    if first_total > qkv_up + 2 * chan_up:
        first_back.append(jnp.zeros((rows_all, first_total - qkv_up - 2 * chan_up), bf16))
    first_back = jnp.concatenate(first_back, axis=1)
    first_wgrad = column_grads(normed_all, first_back)
    gain_rows = jnp.stack(
        [jnp.zeros_like(attn_gain_grad), attn_gain_grad, mamba_gain_grad, ffn_gain_grad]
    )
    gain_rows = jnp.moveaxis(gain_rows.reshape(4, size, -1), 1, 0)
    small = jnp.concatenate(
        [
            taps_grad,
            shift_grad[None],
            bias_grad[None],
            skip_grad[None],
            decay_grad,
            step_wgrad,
            select_wgrad.T,
        ]
    )
    n_small = small.shape[0]
    small = jnp.pad(small, ((0, up_to(n_small, 64) - n_small), (0, 0))).astype(bf16)
    gate_share, up_share = unpack_columns(
        ffn_home, ffn_cuts, ffn_at, (gate_weight.shape, up_weight.shape), size
    )
    input_product = Product(first_back, first_mat, size, True)
    _, ((input_back,), (first_home,), (small,), (gain_share,)) = finish(
        first_wgrad.reshape(size, depth, first_total),
        input_product,
        normed_all,
        gain_float[:1],
        gain_rows,
        small,
        size,
        13,
    )
    stream_part, _ = norm_backward(input_back, stream, inv_in, gain_float[0])
    stream_back = middle_back + stream_part
    query_share, keyval_share, entry_share = unpack_columns(
        first_home,
        first_cuts,
        first_at,
        (query_weight.shape, keyval_weight.shape, mamba_in.shape),
        size,
    )
    chan = conv_bias.shape[0]
    vectors = small.reshape(-1, chan_up)[:, :chan].astype(f32)
    attn_share = jnp.moveaxis(attn_home, 0, 1).reshape(depth, attn_wide)[:, :width].astype(f32)
    mamba_share = mamba_share.reshape(-1, width)[:chan].astype(f32)
    down_share = down_share.reshape(-1, width)[:ff_cols].astype(f32)
    return (
        result.astype(bf16)[None],
        stream_back[None],
        gain_share,
        query_share,
        keyval_share,
        attn_share,
        entry_share,
        vectors[:CONV],
        vectors[CONV],
        vectors[CONV + 1],
        vectors[CONV + 2],
        vectors[CONV + 3 : CONV + 3 + NS],
        vectors[CONV + 3 + NS + RANK : n_small].T,
        vectors[CONV + 3 + NS : CONV + 3 + NS + RANK],
        mamba_share,
        gate_share,
        up_share,
        down_share,
    )


def solution(mesh):
    in_specs = (
        P("fsdp", "ctx", None),
        P("fsdp", "ctx", None),
        P("fsdp", None),
        P(),
        P(None, "fsdp"),
        P("fsdp", None),
        P("fsdp", None),
        P("fsdp", None),
        P("fsdp", None),
        P(None, "fsdp"),
        P("fsdp"),
        P("fsdp"),
        P("fsdp"),
        P(None, "fsdp"),
        P("fsdp", None),
        P(None, "fsdp"),
        P("fsdp", None),
        P("fsdp", None),
        P("fsdp", None),
        P("fsdp", None),
    )
    out_specs = (
        P("fsdp", "ctx", None),
        P("fsdp", "ctx", None),
        P(None, "fsdp"),
        P("fsdp", None),
        P("fsdp", None),
        P("fsdp", None),
        P("fsdp", None),
        P(None, "fsdp"),
        P("fsdp"),
        P("fsdp"),
        P("fsdp"),
        P(None, "fsdp"),
        P("fsdp", None),
        P(None, "fsdp"),
        P("fsdp", None),
        P("fsdp", None),
        P("fsdp", None),
        P("fsdp", None),
    )
    return jax.shard_map(
        on_device, mesh=mesh, in_specs=in_specs, out_specs=out_specs, check_vma=False
    )
```
